512 devices in a mesh: lat: 32 (over x, z), lon: 16 (over y, core).
Axes of the slice: x: 4, y: 8, z: 8, core: 2. Of those that a mesh axis runs over, the one named last changes fastest.
Arguments:
- state: float32 [256, 1440, 256], P('lat', 'lon'), may hold values from -6 to 6
- filter_flag: int32 [256], P('lat'), may hold values from 0 to 1, as said below
- cutoff: int32 [256], P('lat'), may hold values from 2 to 179
Outputs:
- state_new: float32 [256, 1440, 256], P('lat', 'lon')
The draws below stay inside these ranges and needn't reach their ends.
Inputs may be any that keep to these rules, and one draw needn't show every extreme that they name: `filter_flag`: row j is flagged exactly when j < S or j >= 128 + S, for one S between 32 and 96.
All inputs are finite; a program needn't handle non-finite values.
Results may differ from the reference program's by a relative error of at most 0.000057.
Values sent between devices are 32-bit elements; how exact they have to be, the bound alone decides.
A program may use at most 64 MiB of HBM per device.

```python
import math
import jax
import jax.numpy as jnp

NLON = 1440
LEV = 64
NLAT = 256


def draw_filter_flag(key, part):
    split = jax.random.randint(key, (), NLAT // 8, 3 * NLAT // 8 + 1)
    index = jnp.arange(NLAT)
    return ((index < split) | (index >= NLAT // 2 + split)).astype(jnp.int32)


def with_ends(values, stream_key, least, top_value):
    shape = values.shape
    spot = [jax.random.randint(jax.random.fold_in(stream_key, axis), (), 0, shape[axis]) for axis in range(len(shape))]
    values = values.at[tuple(spot)].set(least)
    longest = shape.index(max(shape))
    spot[longest] = (spot[longest] + 1) % shape[longest]
    return values.at[tuple(spot)].set(top_value)


def level_of(own_key, shape, pieces, least, top_value):
    factor_of = 1.0
    for axis_at, shards_of in pieces:
        heights = jax.random.uniform(jax.random.fold_in(jax.random.fold_in(own_key, 6), axis_at), (shards_of,), jnp.float32, least / len(pieces), top_value / len(pieces))
        factor_of = factor_of * jnp.repeat(jnp.exp(heights), shape[axis_at] // shards_of).reshape((-1,) + (1,) * (len(shape) - 1 - axis_at))
    return factor_of


def normal_values(own_key, dims, scale, limit, cuts=(), kind=jnp.bfloat16):
    gain = level_of(own_key, dims, cuts, -0.22, 0.18) if cuts else 1.0
    result = jax.random.normal(own_key, dims, jnp.float32) * scale * gain
    return jnp.minimum(jnp.maximum(result, -limit), limit).astype(kind)


def setup_inputs(seed: int = 0) -> dict:
    key_list = jax.random.split(jax.random.key(seed), 4)
    return {
        "state": normal_values(key_list[0], (NLAT, NLON, 4 * LEV), 1.0, 6.0, ((0, 32), (1, 16)), jnp.float32),
        "filter_flag": draw_filter_flag(jax.random.fold_in(key_list[3], 71), 0),
        "cutoff": with_ends(jax.random.randint(key_list[2], (NLAT,), 2, NLON // 8), jax.random.fold_in(key_list[2], 1), 2, (NLON // 8) - 1).astype(jnp.int32),
    }


WIND_COEF = 0.03
VERT_COEF = 0.2
PRESS_COEF = 0.03


def row_cosines(count):
    index = jnp.arange(count).astype(jnp.float32)
    return jnp.cos(-0.5 * math.pi + (index + 0.5) * math.pi / count)


def polar_filter(field, filter_flag, cutoff):
    width = field.shape[1]
    spectra = jnp.fft.rfft(field, axis=1)
    waves = jnp.arange(width // 2 + 1).astype(jnp.float32)
    ratio = cutoff.astype(jnp.float32)[:, None] / jnp.maximum(waves, 1.0)[None, :]
    damping = jnp.minimum(1.0, ratio * ratio)
    smooth = jnp.fft.irfft(spectra * damping[:, :, None], n=width, axis=1).astype(field.dtype)
    return jnp.where(filter_flag[:, None, None] == 1, smooth, field)


def level_diff(field):
    padded = jnp.pad(field, ((0, 0), (0, 0), (1, 1)))
    return 0.5 * (padded[:, :, 2:] - padded[:, :, :-2])


def reference(state, filter_flag, cutoff):
    levels = state.shape[2] // 4
    zonal_wind = state[:, :, :levels]
    merid_wind = state[:, :, levels:2 * levels]
    vert_wind = state[:, :, 2 * levels:3 * levels]
    pressure = state[:, :, 3 * levels:]
    nlat = state.shape[0]
    cos_rows = row_cosines(nlat)[:, None, None]
    grad_x = (jnp.roll(pressure, -1, 1) - jnp.roll(pressure, 1, 1)) / (2.0 * cos_rows)
    padded = jnp.pad(pressure, ((1, 1), (0, 0), (0, 0)))
    grad_y = 0.5 * (padded[2:] - padded[:-2])
    grad_z = level_diff(pressure)
    zonal_new = polar_filter(zonal_wind - WIND_COEF * grad_x, filter_flag, cutoff)
    merid_new = polar_filter(merid_wind - WIND_COEF * grad_y, filter_flag, cutoff)
    vert_new = vert_wind - VERT_COEF * grad_z
    div_x = (jnp.roll(zonal_new, -1, 1) - jnp.roll(zonal_new, 1, 1)) / (2.0 * cos_rows)
    flux = jnp.pad(merid_new * cos_rows, ((1, 1), (0, 0), (0, 0)))
    div_y = (flux[2:] - flux[:-2]) / (2.0 * cos_rows)
    div_z = level_diff(vert_new)
    press_mid = pressure - PRESS_COEF * (div_x + div_y + div_z)
    press_new = polar_filter(press_mid, filter_flag, cutoff)
    return jnp.concatenate([zonal_new, merid_new, vert_new, press_new], 2)
```

```python
import functools
import math

import jax
import jax.numpy as jnp
import numpy as np
from jax import lax
from jax.experimental import pallas as pl
from jax.experimental.pallas import tpu as pltpu
from jax.sharding import PartitionSpec as P

MESH = pl.DeviceIdType.MESH
PARTS = 16
LANES = 128
OPEN_CUT = 4096.0
PACKED = 72


def split_table(table):
    high = np.asarray(table, dtype=jnp.bfloat16)
    low = np.asarray(table - high.astype(np.float64), dtype=jnp.bfloat16)
    return high, low


def dft_tables(nlon, width, wide):
    points = np.full(wide, -10**6)
    points[:width] = np.arange(width)
    points[width] = width
    points[wide - 1] = -1
    used = points > -10**6
    forward = np.zeros((8, 2 * wide, 2 * wide))
    inverse = np.zeros((8, 2 * wide, 2 * wide))
    sines = np.zeros((8, wide))
    for group in range(8):
        for row in range(wide):
            if group:
                if row >= width:
                    continue
                wave = group + PARTS * row
                weight = 2.0 / nlon
            else:
                half = width // 2 + 1
                if row < half:
                    wave = PARTS * row
                elif row < width + 1:
                    wave = 8 + PARTS * (row - half)
                else:
                    continue
                weight = (1.0 if wave in (0, nlon // 2) else 2.0) / nlon
            phase = np.where(used, (points * wave) % nlon, 0) * (2.0 * math.pi / nlon)
            cos_vals = np.where(used, np.cos(phase), 0.0)
            sin_vals = np.where(used, np.sin(phase), 0.0)
            inner = np.arange(wide) < width
            if group:
                forward[group, row, :wide] = cos_vals
                forward[group, row, wide:] = -sin_vals
                forward[group, wide + row, :wide] = -sin_vals
                forward[group, wide + row, wide:] = -cos_vals
                inverse[group, :wide, row] = weight * cos_vals * inner
                inverse[group, :wide, wide + row] = -weight * sin_vals * inner
                inverse[group, wide:, row] = weight * sin_vals * inner
                inverse[group, wide:, wide + row] = weight * cos_vals * inner
            else:
                base = 0 if row < half else wide
                part = slice(base, base + wide)
                forward[0, row, part] = cos_vals
                forward[0, wide + row, part] = -sin_vals
                inverse[0, part, row] = weight * cos_vals * inner
                inverse[0, part, wide + row] = -weight * sin_vals * inner
            sines[group, row] = math.sin(2.0 * math.pi * wave / nlon)
    waves = np.ascontiguousarray(np.broadcast_to(sines.astype(np.float32)[..., None], sines.shape + (LANES,)))
    return split_table(forward) + split_table(inverse) + (waves,)


def coef_table(nlat, bands):
    rows = nlat // bands
    index = np.arange(-1, nlat + 1).astype(np.float32)
    angle = np.float32(-0.5 * math.pi) + (index + np.float32(0.5)) * np.float32(math.pi) / np.float32(nlat)
    cosine = np.cos(angle.astype(np.float64)).astype(np.float32).astype(np.float64)
    flux = cosine.copy()
    flux[0] = 0.0
    flux[-1] = 0.0
    table = np.zeros((bands, 16, LANES))
    for band in range(bands):
        at = band * rows + 1
        for row in range(rows):
            table[band, row] = 0.015 / cosine[at + row]
        for pair in range(rows // 2):
            even = at + 2 * pair
            odd = even + 1
            lane = np.zeros(8)
            lane[0] = 0.03 / cosine[even]
            lane[1] = 0.03 / cosine[odd]
            lane[4] = -0.015 * flux[odd] / cosine[even]
            lane[5] = 0.015 * flux[even] / cosine[odd]
            lane[6] = 0.015 * flux[even - 1] / cosine[even]
            lane[7] = -0.015 * flux[odd + 1] / cosine[odd]
            table[band, 8 + pair] = np.repeat(lane, 16)
    return table.astype(np.float32)


def wave_sum(terms):
    total = None
    for factor, value in terms:
        if abs(factor) < 1e-9:
            continue
        if abs(abs(factor) - 1.0) < 1e-9:
            if total is None:
                total = value if factor > 0 else -value
            else:
                total = total + value if factor > 0 else total - value
        else:
            part = value * np.float32(factor)
            total = part if total is None else total + part
    return total


def half_dft(even_in, odd_in):
    unit = 2.0 * math.pi / PARTS
    sums = [even_in[0] + even_in[8]] + [even_in[a] + even_in[8 - a] for a in (1, 2, 3)] + [even_in[4]]
    diffs = [even_in[0] - even_in[8]] + [even_in[a] - even_in[8 - a] for a in (1, 2, 3)]
    odd_sums = [None] + [odd_in[a] + odd_in[8 - a] for a in (1, 2, 3)] + [odd_in[4]]
    odd_diffs = [None] + [odd_in[a] - odd_in[8 - a] for a in (1, 2, 3)]
    cos_out = []
    sin_out = []
    for k in range(9):
        parts = diffs if k % 2 else sums
        cos_out.append(wave_sum([(math.cos(unit * a * k), parts[a]) for a in range(len(parts))]))
        parts = odd_sums if k % 2 else odd_diffs
        sin_out.append(wave_sum([(math.sin(unit * a * k), parts[a]) for a in range(1, len(parts))]))
    return cos_out, sin_out


def split_value(value):
    high = value.astype(jnp.bfloat16)
    low = (value - high.astype(jnp.float32)).astype(jnp.bfloat16)
    return jnp.concatenate([high, low], axis=1)


def table_dot(high, low, pair):
    both = jnp.dot(high, pair, preferred_element_type=jnp.float32)
    rest = jnp.dot(low, pair[:, :LANES], preferred_element_type=jnp.float32)
    return both[:, :LANES] + both[:, LANES:] + rest


def kernel(
    bands,
    state_hbm, flag_ref, cut_ref, coef_hbm, fhi_hbm, flo_hbm, ihi_hbm, ilo_hbm, wave_hbm,
    out_hbm,
    state, result, winds, press, cuts, coef, fhi, flo, ihi, ilo, waves,
    halo_out, halo_in, send, recv, spectra, fields, bsend, brecv,
    load_sem, store_sem, halo_send, halo_recv, send_sem, recv_sem, bsend_sem, brecv_sem,
):
    lat = lax.axis_index("lat")
    lon = lax.axis_index("lon")
    rows, width = state_hbm.shape[0], state_hbm.shape[1]
    wide = recv.shape[1]
    spare = jnp.zeros((wide - width, LANES), jnp.float32)

    def field(row, part):
        return jnp.concatenate([state[row, :, pl.ds(part * LANES, LANES)], spare], axis=0)

    above = lax.rem(lat + bands - 1, bands)
    below = lax.rem(lat + 1, bands)
    chip = lon // 2
    core = lon % 2

    loads = [pltpu.make_async_copy(state_hbm, state, load_sem.at[0])]
    loads.append(pltpu.make_async_copy(coef_hbm.at[lat], coef, load_sem.at[1]))
    tables = ((fhi_hbm, fhi), (flo_hbm, flo), (ihi_hbm, ihi), (ilo_hbm, ilo), (wave_hbm, waves))
    for at, (source, target) in enumerate(tables):
        loads.append(pltpu.make_async_copy(source, target, load_sem.at[2 + at]))
    for load in loads:
        load.start()

    barrier = pltpu.get_barrier_semaphore()
    for offset in range(1, PARTS):
        pl.semaphore_signal(barrier, inc=1, device_id=(lat, lax.rem(lon + offset, PARTS)), device_id_type=MESH)
    pl.semaphore_signal(barrier, inc=1, device_id=(above, lon), device_id_type=MESH)
    pl.semaphore_signal(barrier, inc=1, device_id=(below, lon), device_id_type=MESH)

    lane = lax.broadcasted_iota(jnp.int32, (wide, LANES), 1)
    line = lax.broadcasted_iota(jnp.int32, (wide, LANES), 0)
    first = lane < 64
    block = (lane // 16) % 4
    for row in range(rows):
        kept = jnp.full((1, LANES), cut_ref[row], jnp.int32).astype(jnp.float32)
        flag = jnp.full((1, LANES), flag_ref[row], jnp.int32)
        cuts[pl.ds(row + 1, 1), :] = jnp.where(flag == 1, kept, OPEN_CUT)
    loads[0].wait()
    loads[1].wait()

    def prepare(row, carry):
        left = field(row, 0)
        right = field(row, 1)
        turned = pltpu.roll(right, 64, 1)
        step = jnp.where(lane < 63, pltpu.roll(turned, LANES - 1, 1), 0.0) - jnp.where(lane > 0, pltpu.roll(turned, 1, 1), 0.0)
        vert = right - 0.1 * step
        step = jnp.where(lane < 63, pltpu.roll(vert, LANES - 1, 1), 0.0) - jnp.where(lane > 0, pltpu.roll(vert, 1, 1), 0.0)
        press[row] = turned - 0.015 * step
        result[row, :, pl.ds(LANES, LANES)] = vert[:width]
        scale = coef[pl.ds(row, 1), :]
        zonal = left - scale * (pltpu.roll(turned, wide - 1, 0) - pltpu.roll(turned, 1, 0))
        north = field(jnp.minimum(row + 1, rows - 1), 1) * jnp.where(row < rows - 1, 0.015, 0.0)
        south = field(jnp.maximum(row - 1, 0), 1) * jnp.where(row > 0, 0.015, 0.0)
        winds[row + 1] = jnp.where(first, zonal, left - (north - south))
        return carry

    lax.fori_loop(0, rows, prepare, 0)
    for side, row in ((0, 0), (1, rows - 1)):
        turned = pltpu.roll(field(row, 1), 64, 1)
        message = jnp.where(first, turned, winds[row + 1])
        halo_out[side] = jnp.where(line == width, cuts[pl.ds(row + 1, 1), :], message)

    def pack(pair, slot):
        even = 2 * pair + 1
        sources = (
            jnp.where(first, winds[even], winds[even + 1]),
            jnp.where(first, winds[even + 1], winds[even]),
            jnp.where(first, press[even - 1], winds[even - 1]),
            jnp.where(first, press[even], winds[even + 2]),
        )
        for quarter in range(4):
            chunk = sources[quarter]
            for at in range(4):
                if at != quarter:
                    chunk = jnp.where(block == at, pltpu.roll(sources[at], (16 * (at - quarter)) % LANES, 1), chunk)
            send[slot + 2 * quarter] = chunk

    def pack_inner(at, carry):
        pack(1 + at, 8 * at)
        return carry

    def pack_outer(at, carry):
        pack(3 * at, 8 * at + 1)
        return carry

    lax.fori_loop(0, 2, pack_inner, 0)
    pl.semaphore_wait(barrier, PARTS + 1)

    halos = []
    for side, device in ((0, above), (1, below)):
        halos.append(
            pltpu.make_async_remote_copy(
                src_ref=halo_out.at[side],
                dst_ref=halo_in.at[1 - side],
                send_sem=halo_send.at[side],
                recv_sem=halo_recv.at[1 - side],
                device_id=(device, lon),
                device_id_type=MESH,
            )
        )
    for halo in halos:
        halo.start()

    def forward_copy(source, slot, device):
        return pltpu.make_async_remote_copy(
            src_ref=send.at[source],
            dst_ref=recv.at[slot],
            send_sem=send_sem.at[source],
            recv_sem=recv_sem.at[slot],
            device_id=(lat, device),
            device_id_type=MESH,
        )

    def backward_copy(source, slot, device):
        return pltpu.make_async_remote_copy(
            src_ref=bsend.at[source],
            dst_ref=brecv.at[slot],
            send_sem=bsend_sem.at[source],
            recv_sem=brecv_sem.at[slot],
            device_id=(lat, device),
            device_id_type=MESH,
        )

    order = (4, 3, 5, 2, 6, 1, 7, 0)

    def send_to(copy, kind):
        for offset in order:
            target = 2 * lax.rem(chip + offset, 8) + kind
            if offset:
                copy(target, lon, target).start()
            else:
                @pl.when(core != kind)
                def _():
                    copy(target, lon, target).start()

    send_to(forward_copy, 0)

    for side in range(2):
        halos[side].wait_recv()
    inside = jnp.where(lat > 0, 0.015, 0.0)
    upper = halo_in[0]
    cuts[pl.ds(0, 1), :] = upper[width : width + 1]
    winds[0] = jnp.where(line < width, upper - 0.015 * field(0, 1), 0.0)
    winds[1] = winds[1] + jnp.where(first | (line >= width), 0.0, inside * pltpu.roll(upper, 64, 1))
    inside = jnp.where(lat < bands - 1, 0.015, 0.0)
    lower = halo_in[1]
    cuts[pl.ds(rows + 1, 1), :] = lower[width : width + 1]
    winds[rows + 1] = jnp.where(line < width, lower + 0.015 * field(rows - 1, 1), 0.0)
    winds[rows] = winds[rows] - jnp.where(first | (line >= width), 0.0, inside * pltpu.roll(lower, 64, 1))

    lax.fori_loop(0, 2, pack_outer, 0)
    send_to(forward_copy, 1)
    recv[lon] = send[lon]

    half = chip // 4
    mine = (1 - core) * (1 + half) + core * 3 * half
    lanes = lax.broadcasted_iota(jnp.int32, (1, LANES), 1) // 16
    cut_even = cuts[pl.ds(2 * mine + 1, 1), :]
    cut_odd = cuts[pl.ds(2 * mine + 2, 1), :]
    limit = jnp.where((lanes == 0) | (lanes == 2) | (lanes == 5), cut_even, cut_odd)
    limit = jnp.where(lanes == 6, cuts[pl.ds(2 * mine, 1), :], limit)
    limit = jnp.where(lanes == 7, cuts[pl.ds(2 * mine + 3, 1), :], limit)
    factor = coef[pl.ds(8 + mine, 1), :]
    for load in loads[2:]:
        load.wait()

    def receive(offset, carry):
        source = lax.rem(lon + offset, PARTS)
        forward_copy(source, source, source).wait_recv()
        return carry

    lax.fori_loop(1, PARTS, receive, 0)

    def gather_waves(at, carry):
        where = pl.multiple_of(16 * at, 16)
        spans = pl.ds(where, 16)
        images = pl.ds(pl.multiple_of(wide + where, 16), 16)
        values = [recv[a, spans, :] for a in range(PARTS)]
        evens = [values[0]] + [values[a] + values[PARTS - a] for a in range(1, 8)] + [values[8]]
        odds = [None] + [values[a] - values[PARTS - a] for a in range(1, 8)]
        cos_out, sin_out = half_dft(evens, odds)
        spectra[0, spans, :] = split_value(cos_out[0])
        spectra[0, images, :] = split_value(cos_out[8])
        for k in range(1, 8):
            spectra[k, spans, :] = split_value(cos_out[k])
            spectra[k, images, :] = split_value(sin_out[k])
        return carry

    lax.fori_loop(0, wide // 16, gather_waves, 0)

    def transform(group, carry):
        values = table_dot(fhi[group], flo[group], spectra[group])
        wave = PARTS * line + group
        folded = jnp.where(line <= width // 2, PARTS * line, PARTS * (line - width // 2 - 1) + 8)
        wave = jnp.where(group > 0, jnp.minimum(wave, PARTS * width - wave), folded)
        ratio = limit / jnp.maximum(wave, 1).astype(jnp.float32)
        damping = jnp.minimum(1.0, ratio * ratio)
        real = values[:wide] * damping
        imag = values[wide:] * damping
        turn = factor * waves[group]
        zonal = lane < 32
        lift_real = jnp.where(zonal, turn * imag, factor * real)
        lift_imag = jnp.where(zonal, -turn * real, factor * imag)
        inner = (lane >= 32) & first
        outs = []
        for value, lift in ((real, lift_real), (imag, lift_imag)):
            total = pltpu.roll(lift, 32, 1) + pltpu.roll(lift, 96, 1) + pltpu.roll(lift, 64, 1)
            outs.append(jnp.where(inner, value + damping * total, value))
        both = split_value(jnp.concatenate(outs, axis=0))
        fields[group] = table_dot(ihi[group], ilo[group], both)
        return carry

    lax.fori_loop(0, 8, transform, 0)

    def scatter_waves(at, carry):
        where = pl.multiple_of(16 * at, 16)
        spans = pl.ds(where, 16)
        images = pl.ds(pl.multiple_of(wide + where, 16), 16)
        evens = [fields[0, spans, :]] + [fields[k, spans, :] for k in range(1, 8)] + [fields[0, images, :]]
        odds = [None] + [fields[k, images, :] for k in range(1, 8)]
        cos_out, sin_out = half_dft(evens, odds)
        circles[0, spans, :] = cos_out[0]
        circles[8, spans, :] = cos_out[8]
        for a in range(1, 8):
            circles[a, spans, :] = cos_out[a] - sin_out[a]
            circles[PARTS - a, spans, :] = cos_out[a] + sin_out[a]
        return carry

    circles = recv
    lax.fori_loop(0, wide // 16, scatter_waves, 0)
    narrow = lax.broadcasted_iota(jnp.int32, (24, LANES), 1)

    def pack_back(a, carry):
        rest = circles[a, pl.ds(72, 24), :]
        for at in range(3):
            spans = pl.ds(24 * at, 24)
            bsend[a, spans, :] = jnp.where(narrow < 96, circles[a, spans, :], pltpu.roll(rest, 96 - 32 * at, 1))
        return carry

    lax.fori_loop(0, PARTS, pack_back, 0)
    send_to(backward_copy, 0)
    send_to(backward_copy, 1)
    brecv[lon] = bsend[lon]

    def unpack(pair, slot):
        chunks = []
        for quarter in range(4):
            source = slot + 2 * quarter

            @pl.when(source != lon)
            def _():
                backward_copy(source, source, source).wait_recv()

            pieces = [brecv[source, pl.ds(24 * at, 24), :] for at in range(3)]
            rest = jnp.where(narrow < 32, pltpu.roll(pieces[0], 32, 1), pltpu.roll(pieces[1], 64, 1))
            rest = jnp.where(narrow < 64, rest, pltpu.roll(pieces[2], 96, 1))
            chunks.append(jnp.concatenate(pieces + [rest], axis=0))
        parts = []
        for at in range(4):
            shift = 64 if at >= 2 else 0
            part = None
            for quarter in range(4):
                amount = (16 * (quarter - at) + shift) % LANES
                moved = pltpu.roll(chunks[quarter], amount, 1) if amount else chunks[quarter]
                part = moved if part is None else jnp.where(block == quarter, moved, part)
            parts.append(part)
        even = 2 * pair
        spans = pl.ds(0, LANES)
        result[even, :, spans] = jnp.where(first, parts[0], parts[1])[:width]
        result[even + 1, :, spans] = jnp.where(first, parts[1], parts[0])[:width]
        spans = pl.ds(LANES, LANES)
        result[even, :, spans] = jnp.where(first[:width], result[even, :, spans], parts[2][:width])
        result[even + 1, :, spans] = jnp.where(first[:width], result[even + 1, :, spans], parts[3][:width])

    def store(pair):
        spans = pl.ds(2 * pair, 2)
        return pltpu.make_async_copy(result.at[spans], out_hbm.at[spans], store_sem.at[pair])

    def unpack_inner(at, carry):
        unpack(1 + at, 8 * at)
        store(1 + at).start()
        return carry

    def unpack_outer(at, carry):
        unpack(3 * at, 8 * at + 1)
        store(3 * at).start()
        return carry

    lax.fori_loop(0, 2, unpack_inner, 0)
    lax.fori_loop(0, 2, unpack_outer, 0)

    def finish(offset, carry):
        target = lax.rem(lon + offset, PARTS)
        forward_copy(target, lon, target).wait_send()
        backward_copy(target, lon, target).wait_send()
        return carry

    lax.fori_loop(1, PARTS, finish, 0)
    for halo in halos:
        halo.wait_send()
    for pair in range(rows // 2):
        store(pair).wait()


def solution(mesh):
    bands = mesh.shape["lat"]

    def body(state, filter_flag, cutoff):
        rows, width, depth = state.shape
        wide = (width + 2 + 15) // 16 * 16
        tables = dft_tables(width * PARTS, width, wide)
        coefs = coef_table(rows * bands, bands)
        f32 = jnp.float32
        table = pltpu.VMEM((8, 2 * wide, 2 * wide), jnp.bfloat16)
        any_spec = pl.BlockSpec(memory_space=pl.ANY)
        smem_spec = pl.BlockSpec(memory_space=pltpu.SMEM)
        dma = pltpu.SemaphoreType.DMA
        return pl.pallas_call(
            functools.partial(kernel, bands),
            out_shape=jax.ShapeDtypeStruct(state.shape, f32),
            in_specs=[any_spec, smem_spec, smem_spec] + [any_spec] * 6,
            out_specs=any_spec,
            scratch_shapes=[
                pltpu.VMEM(state.shape, f32),
                pltpu.VMEM(state.shape, f32),
                pltpu.VMEM((rows + 2, wide, LANES), f32),
                pltpu.VMEM((rows, wide, LANES), f32),
                pltpu.VMEM((16, LANES), f32),
                pltpu.VMEM((16, LANES), f32),
                table, table, table, table,
                pltpu.VMEM((8, wide, LANES), f32),
                pltpu.VMEM((2, wide, LANES), f32),
                pltpu.VMEM((2, wide, LANES), f32),
                pltpu.VMEM((PARTS, wide, LANES), f32),
                pltpu.VMEM((PARTS, wide, LANES), f32),
                pltpu.VMEM((8, 2 * wide, 2 * LANES), jnp.bfloat16),
                pltpu.VMEM((8, 2 * wide, LANES), f32),
                pltpu.VMEM((PARTS, PACKED, LANES), f32),
                pltpu.VMEM((PARTS, PACKED, LANES), f32),
                dma((7,)),
                dma((4,)),
                dma((2,)),
                dma((2,)),
                dma((PARTS,)),
                dma((PARTS,)),
                dma((PARTS,)),
                dma((PARTS,)),
            ],
            compiler_params=pltpu.CompilerParams(collective_id=0, has_side_effects=True),
        )(state, filter_flag, cutoff, coefs, *tables)

    return jax.shard_map(
        body,
        mesh=mesh,
        in_specs=(P("lat", "lon", None), P("lat"), P("lat")),
        out_specs=P("lat", "lon", None),
        check_vma=False,
    )
```

```python
import functools
import math

import jax
import jax.numpy as jnp
import numpy as np
from jax import lax
from jax.experimental import pallas as pl
from jax.experimental.pallas import tpu as pltpu
from jax.sharding import PartitionSpec as P

MESH = pl.DeviceIdType.MESH
PARTS = 16
LANES = 128
OPEN_CUT = 4096.0
PACKED = 72


def split_table(table):
    high = np.asarray(table, dtype=jnp.bfloat16)
    low = np.asarray(table - high.astype(np.float64), dtype=jnp.bfloat16)
    return high, low


def dft_tables(nlon, width, wide):
    points = np.full(wide, -10**6)
    points[:width] = np.arange(width)
    points[width] = width
    points[wide - 1] = -1
    used = points > -10**6
    forward = np.zeros((8, 2 * wide, 2 * wide))
    inverse = np.zeros((8, 2 * wide, 2 * wide))
    sines = np.zeros((8, wide))
    for group in range(8):
        for row in range(wide):
            if group:
                if row >= width:
                    continue
                wave = group + PARTS * row
                weight = 2.0 / nlon
            else:
                half = width // 2 + 1
                if row < half:
                    wave = PARTS * row
                elif row < width + 1:
                    wave = 8 + PARTS * (row - half)
                else:
                    continue
                weight = (1.0 if wave in (0, nlon // 2) else 2.0) / nlon
            phase = np.where(used, (points * wave) % nlon, 0) * (2.0 * math.pi / nlon)
            cos_vals = np.where(used, np.cos(phase), 0.0)
            sin_vals = np.where(used, np.sin(phase), 0.0)
            inner = np.arange(wide) < width
            if group:
                forward[group, row, :wide] = cos_vals
                forward[group, row, wide:] = -sin_vals
                forward[group, wide + row, :wide] = -sin_vals
                forward[group, wide + row, wide:] = -cos_vals
                inverse[group, :wide, row] = weight * cos_vals * inner
                inverse[group, :wide, wide + row] = -weight * sin_vals * inner
                inverse[group, wide:, row] = weight * sin_vals * inner
                inverse[group, wide:, wide + row] = weight * cos_vals * inner
            else:
                base = 0 if row < half else wide
                part = slice(base, base + wide)
                forward[0, row, part] = cos_vals
                forward[0, wide + row, part] = -sin_vals
                inverse[0, part, row] = weight * cos_vals * inner
                inverse[0, part, wide + row] = -weight * sin_vals * inner
            sines[group, row] = math.sin(2.0 * math.pi * wave / nlon)
    waves = np.zeros((wide, LANES), np.float32)
    waves[:, :8] = sines.T
    return np.concatenate(split_table(np.concatenate([forward, inverse])), axis=1), waves


def coef_table(nlat, bands):
    rows = nlat // bands
    index = np.arange(-1, nlat + 1).astype(np.float32)
    angle = np.float32(-0.5 * math.pi) + (index + np.float32(0.5)) * np.float32(math.pi) / np.float32(nlat)
    cosine = np.cos(angle.astype(np.float64)).astype(np.float32).astype(np.float64)
    flux = cosine.copy()
    flux[0] = 0.0
    flux[-1] = 0.0
    table = np.zeros((bands, 16, LANES))
    for band in range(bands):
        at = band * rows + 1
        for row in range(rows):
            table[band, row] = 0.015 / cosine[at + row]
        for pair in range(rows // 2):
            even = at + 2 * pair
            odd = even + 1
            lane = np.zeros(8)
            lane[0] = 0.03 / cosine[even]
            lane[1] = 0.03 / cosine[odd]
            lane[4] = -0.015 * flux[odd] / cosine[even]
            lane[5] = 0.015 * flux[even] / cosine[odd]
            lane[6] = 0.015 * flux[even - 1] / cosine[even]
            lane[7] = -0.015 * flux[odd + 1] / cosine[odd]
            table[band, 8 + pair] = np.repeat(lane, 16)
    return table.astype(np.float32)


def wave_sum(terms):
    total = None
    for factor, value in terms:
        if abs(factor) < 1e-9:
            continue
        if abs(abs(factor) - 1.0) < 1e-9:
            if total is None:
                total = value if factor > 0 else -value
            else:
                total = total + value if factor > 0 else total - value
        else:
            part = value * np.float32(factor)
            total = part if total is None else total + part
    return total


def half_dft(even_in, odd_in):
    unit = 2.0 * math.pi / PARTS
    sums = [even_in[0] + even_in[8]] + [even_in[a] + even_in[8 - a] for a in (1, 2, 3)] + [even_in[4]]
    diffs = [even_in[0] - even_in[8]] + [even_in[a] - even_in[8 - a] for a in (1, 2, 3)]
    odd_sums = [None] + [odd_in[a] + odd_in[8 - a] for a in (1, 2, 3)] + [odd_in[4]]
    odd_diffs = [None] + [odd_in[a] - odd_in[8 - a] for a in (1, 2, 3)]
    cos_out = []
    sin_out = []
    for k in range(9):
        parts = diffs if k % 2 else sums
        cos_out.append(wave_sum([(math.cos(unit * a * k), parts[a]) for a in range(len(parts))]))
        parts = odd_sums if k % 2 else odd_diffs
        sin_out.append(wave_sum([(math.sin(unit * a * k), parts[a]) for a in range(1, len(parts))]))
    return cos_out, sin_out


def split_value(value):
    high = value.astype(jnp.bfloat16)
    low = (value - high.astype(jnp.float32)).astype(jnp.bfloat16)
    return jnp.concatenate([high, low], axis=1)


def table_dot(table, pair):
    both = jnp.dot(table, pair, preferred_element_type=jnp.float32)
    half = table.shape[0] // 2
    return both[:half, :LANES] + both[:half, LANES:] + both[half:, :LANES]


def kernel(
    bands,
    state_hbm, flag_ref, cut_ref, coef_hbm, table_hbm, wave_hbm,
    out_hbm,
    state, result, winds, press, cuts, coef, table, waves, damps, turns,
    halo_out, halo_in, send, recv, spectra, fields, bsend, brecv,
    load_sem, store_sem, halo_send, halo_recv, send_sem, recv_sem, bsend_sem, brecv_sem,
):
    lat = lax.axis_index("lat")
    lon = lax.axis_index("lon")
    width, rows = state_hbm.shape[0], state_hbm.shape[1]
    wide = recv.shape[1]
    spare = jnp.zeros((wide - width, LANES), jnp.float32)

    def field(row, part):
        return jnp.concatenate([state[:, row, pl.ds(part * LANES, LANES)], spare], axis=0)

    above = lax.rem(lat + bands - 1, bands)
    below = lax.rem(lat + 1, bands)
    chip = lon // 2
    core = lon % 2

    loads = [pltpu.make_async_copy(state_hbm, state, load_sem.at[0])]
    loads.append(pltpu.make_async_copy(coef_hbm.at[lat], coef, load_sem.at[1]))
    tables = ((wave_hbm, waves), (table_hbm, table))
    for at, (source, target) in enumerate(tables):
        loads.append(pltpu.make_async_copy(source, target, load_sem.at[2 + at]))
    loads[0].start()
    loads[1].start()

    barrier = pltpu.get_barrier_semaphore()
    for offset in range(1, PARTS):
        pl.semaphore_signal(barrier, inc=1, device_id=(lat, lax.rem(lon + offset, PARTS)), device_id_type=MESH)
    pl.semaphore_signal(barrier, inc=1, device_id=(above, lon), device_id_type=MESH)
    pl.semaphore_signal(barrier, inc=1, device_id=(below, lon), device_id_type=MESH)

    lane = lax.broadcasted_iota(jnp.int32, (wide, LANES), 1)
    line = lax.broadcasted_iota(jnp.int32, (wide, LANES), 0)
    first = lane < 64
    block = (lane // 16) % 4
    for row in range(rows):
        kept = jnp.full((1, LANES), cut_ref[row], jnp.int32).astype(jnp.float32)
        flag = jnp.full((1, LANES), flag_ref[row], jnp.int32)
        cuts[pl.ds(row + 1, 1), :] = jnp.where(flag == 1, kept, OPEN_CUT)
    loads[0].wait()
    loads[1].wait()
    for load in loads[2:]:
        load.start()

    def prepare(row):
        left = field(row, 0)
        right = field(row, 1)
        turned = pltpu.roll(right, 64, 1)
        step = jnp.where(lane < 63, pltpu.roll(turned, LANES - 1, 1), 0.0) - jnp.where(lane > 0, pltpu.roll(turned, 1, 1), 0.0)
        vert = right - 0.1 * step
        step = jnp.where(lane < 63, pltpu.roll(vert, LANES - 1, 1), 0.0) - jnp.where(lane > 0, pltpu.roll(vert, 1, 1), 0.0)
        press[row] = turned - 0.015 * step
        result[:, row, pl.ds(LANES, LANES)] = vert[:width]
        scale = coef[pl.ds(row, 1), :]
        zonal = left - scale * (pltpu.roll(turned, wide - 1, 0) - pltpu.roll(turned, 1, 0))
        merid = left
        if row < rows - 1:
            merid = merid - 0.015 * field(row + 1, 1)
        if row > 0:
            merid = merid + 0.015 * field(row - 1, 1)
        winds[row + 1] = jnp.where(first, zonal, merid)

    for row in range(rows):
        prepare(row)
    for side, row in ((0, 0), (1, rows - 1)):
        turned = pltpu.roll(field(row, 1), 64, 1)
        message = jnp.where(first, turned, winds[row + 1])
        halo_out[side] = jnp.where(line == width, cuts[pl.ds(row + 1, 1), :], message)

    def pack(pair, slot):
        even = 2 * pair + 1
        sources = (
            jnp.where(first, winds[even], winds[even + 1]),
            jnp.where(first, winds[even + 1], winds[even]),
            jnp.where(first, press[even - 1], winds[even - 1]),
            jnp.where(first, press[even], winds[even + 2]),
        )
        for quarter in range(4):
            chunk = sources[quarter]
            for at in range(4):
                if at != quarter:
                    chunk = jnp.where(block == at, pltpu.roll(sources[at], (16 * (at - quarter)) % LANES, 1), chunk)
            send[slot + 2 * quarter] = chunk

    def pack_inner(at, carry):
        pack(1 + at, 8 * at)
        return carry

    def pack_outer(at, carry):
        pack(3 * at, 8 * at + 1)
        return carry

    lax.fori_loop(0, 2, pack_inner, 0, unroll=2)
    pl.semaphore_wait(barrier, PARTS + 1)

    halos = []
    for side, device in ((0, above), (1, below)):
        halos.append(
            pltpu.make_async_remote_copy(
                src_ref=halo_out.at[side],
                dst_ref=halo_in.at[1 - side],
                send_sem=halo_send.at[side],
                recv_sem=halo_recv.at[1 - side],
                device_id=(device, lon),
                device_id_type=MESH,
            )
        )
    for halo in halos:
        halo.start()

    def forward_copy(source, slot, device):
        return pltpu.make_async_remote_copy(
            src_ref=send.at[source],
            dst_ref=recv.at[slot],
            send_sem=send_sem.at[source],
            recv_sem=recv_sem.at[slot],
            device_id=(lat, device),
            device_id_type=MESH,
        )

    def backward_copy(source, slot, device):
        return pltpu.make_async_remote_copy(
            src_ref=bsend.at[source],
            dst_ref=brecv.at[slot],
            send_sem=bsend_sem.at[source],
            recv_sem=brecv_sem.at[slot],
            device_id=(lat, device),
            device_id_type=MESH,
        )

    order = (4, 3, 5, 2, 6, 1, 7, 0)

    def send_to(copy, kind):
        for offset in order:
            target = 2 * lax.rem(chip + offset, 8) + kind
            if offset:
                copy(target, lon, target).start()
            else:
                @pl.when(core != kind)
                def _():
                    copy(target, lon, target).start()

    send_to(forward_copy, 0)

    for side in range(2):
        halos[side].wait_recv()
    inside = jnp.where(lat > 0, 0.015, 0.0)
    upper = halo_in[0]
    cuts[pl.ds(0, 1), :] = upper[width : width + 1]
    winds[0] = jnp.where(line < width, upper - 0.015 * field(0, 1), 0.0)
    winds[1] = winds[1] + jnp.where(first | (line >= width), 0.0, inside * pltpu.roll(upper, 64, 1))
    inside = jnp.where(lat < bands - 1, 0.015, 0.0)
    lower = halo_in[1]
    cuts[pl.ds(rows + 1, 1), :] = lower[width : width + 1]
    winds[rows + 1] = jnp.where(line < width, lower + 0.015 * field(rows - 1, 1), 0.0)
    winds[rows] = winds[rows] - jnp.where(first | (line >= width), 0.0, inside * pltpu.roll(lower, 64, 1))

    lax.fori_loop(0, 2, pack_outer, 0, unroll=2)
    send_to(forward_copy, 1)
    recv[lon] = send[lon]

    half = chip // 4
    mine = (1 - core) * (1 + half) + core * 3 * half
    lanes = lax.broadcasted_iota(jnp.int32, (1, LANES), 1) // 16
    cut_even = cuts[pl.ds(2 * mine + 1, 1), :]
    cut_odd = cuts[pl.ds(2 * mine + 2, 1), :]
    limit = jnp.where((lanes == 0) | (lanes == 2) | (lanes == 5), cut_even, cut_odd)
    limit = jnp.where(lanes == 6, cuts[pl.ds(2 * mine, 1), :], limit)
    limit = jnp.where(lanes == 7, cuts[pl.ds(2 * mine + 3, 1), :], limit)
    factor = coef[pl.ds(8 + mine, 1), :]
    loads[2].wait()

    for group in range(8):
        wave = PARTS * line + group
        if group:
            wave = jnp.minimum(wave, PARTS * width - wave)
        else:
            wave = jnp.where(line <= width // 2, wave, PARTS * (line - width // 2 - 1) + 8)
        ratio = limit / jnp.maximum(wave, 1).astype(jnp.float32)
        damps[group] = jnp.minimum(1.0, ratio * ratio)
        turns[group] = factor * waves[:, group : group + 1]
    for load in loads[3:]:
        load.wait()

    def receive(offset, carry):
        source = lax.rem(lon + offset, PARTS)
        forward_copy(source, source, source).wait_recv()
        return carry

    lax.fori_loop(1, PARTS, receive, 0)

    def gather_waves(at, carry):
        where = pl.multiple_of(16 * at, 16)
        spans = pl.ds(where, 16)
        images = pl.ds(pl.multiple_of(wide + where, 16), 16)
        values = [recv[a, spans, :] for a in range(PARTS)]
        evens = [values[0]] + [values[a] + values[PARTS - a] for a in range(1, 8)] + [values[8]]
        odds = [None] + [values[a] - values[PARTS - a] for a in range(1, 8)]
        cos_out, sin_out = half_dft(evens, odds)
        spectra[0, spans, :] = split_value(cos_out[0])
        spectra[0, images, :] = split_value(cos_out[8])
        for k in range(1, 8):
            spectra[k, spans, :] = split_value(cos_out[k])
            spectra[k, images, :] = split_value(sin_out[k])
        return carry

    lax.fori_loop(0, wide // 16, gather_waves, 0, unroll=6)

    def transform(group, carry):
        values = table_dot(table[group], spectra[group])
        damping = damps[group]
        real = values[:wide] * damping
        imag = values[wide:] * damping
        turn = turns[group]
        zonal = lane < 32
        lift_real = jnp.where(zonal, turn * imag, factor * real)
        lift_imag = jnp.where(zonal, -turn * real, factor * imag)
        inner = (lane >= 32) & first
        outs = []
        for value, lift in ((real, lift_real), (imag, lift_imag)):
            total = pltpu.roll(lift, 32, 1) + pltpu.roll(lift, 96, 1) + pltpu.roll(lift, 64, 1)
            outs.append(jnp.where(inner, value + damping * total, value))
        both = split_value(jnp.concatenate(outs, axis=0))
        fields[group] = table_dot(table[8 + group], both)
        return carry

    lax.fori_loop(0, 8, transform, 0, unroll=8)

    def scatter_waves(at, carry):
        where = pl.multiple_of(16 * at, 16)
        spans = pl.ds(where, 16)
        images = pl.ds(pl.multiple_of(wide + where, 16), 16)
        evens = [fields[0, spans, :]] + [fields[k, spans, :] for k in range(1, 8)] + [fields[0, images, :]]
        odds = [None] + [fields[k, images, :] for k in range(1, 8)]
        cos_out, sin_out = half_dft(evens, odds)
        circles[0, spans, :] = cos_out[0]
        circles[8, spans, :] = cos_out[8]
        for a in range(1, 8):
            circles[a, spans, :] = cos_out[a] - sin_out[a]
            circles[PARTS - a, spans, :] = cos_out[a] + sin_out[a]
        return carry

    circles = recv
    lax.fori_loop(0, wide // 16, scatter_waves, 0, unroll=6)
    narrow = lax.broadcasted_iota(jnp.int32, (24, LANES), 1)

    def pack_back(a, carry):
        rest = circles[a, pl.ds(72, 24), :]
        for at in range(3):
            spans = pl.ds(24 * at, 24)
            bsend[a, spans, :] = jnp.where(narrow < 96, circles[a, spans, :], pltpu.roll(rest, 96 - 32 * at, 1))
        return carry

    lax.fori_loop(0, PARTS, pack_back, 0, unroll=PARTS)
    send_to(backward_copy, 0)
    send_to(backward_copy, 1)
    brecv[lon] = bsend[lon]

    def unpack(pair, slot):
        chunks = []
        for quarter in range(4):
            source = slot + 2 * quarter

            @pl.when(source != lon)
            def _():
                backward_copy(source, source, source).wait_recv()

            pieces = [brecv[source, pl.ds(24 * at, 24), :] for at in range(3)]
            rest = jnp.where(narrow < 32, pltpu.roll(pieces[0], 32, 1), pltpu.roll(pieces[1], 64, 1))
            rest = jnp.where(narrow < 64, rest, pltpu.roll(pieces[2], 96, 1))
            chunks.append(jnp.concatenate(pieces + [rest], axis=0))
        parts = []
        for at in range(4):
            shift = 64 if at >= 2 else 0
            part = None
            for quarter in range(4):
                amount = (16 * (quarter - at) + shift) % LANES
                moved = pltpu.roll(chunks[quarter], amount, 1) if amount else chunks[quarter]
                part = moved if part is None else jnp.where(block == quarter, moved, part)
            parts.append(part)
        even = 2 * pair
        spans = pl.ds(0, LANES)
        result[:, even, spans] = jnp.where(first, parts[0], parts[1])[:width]
        result[:, even + 1, spans] = jnp.where(first, parts[1], parts[0])[:width]
        spans = pl.ds(LANES, LANES)
        result[:, even, spans] = jnp.where(first[:width], result[:, even, spans], parts[2][:width])
        result[:, even + 1, spans] = jnp.where(first[:width], result[:, even + 1, spans], parts[3][:width])

    for at in range(2):
        unpack(1 + at, 8 * at)
    for at in range(2):
        unpack(3 * at, 8 * at + 1)
    store = pltpu.make_async_copy(result, out_hbm, store_sem.at[0])
    store.start()

    def finish(offset, carry):
        target = lax.rem(lon + offset, PARTS)
        forward_copy(target, lon, target).wait_send()
        backward_copy(target, lon, target).wait_send()
        return carry

    lax.fori_loop(1, PARTS, finish, 0)
    for halo in halos:
        halo.wait_send()
    store.wait()


def solution(mesh):
    bands = mesh.shape["lat"]

    def body(state, filter_flag, cutoff):
        rows, width, depth = state.shape
        wide = (width + 2 + 15) // 16 * 16
        tables = dft_tables(width * PARTS, width, wide)
        coefs = coef_table(rows * bands, bands)
        f32 = jnp.float32
        table = pltpu.VMEM((16, 4 * wide, 2 * wide), jnp.bfloat16)
        any_spec = pl.BlockSpec(memory_space=pl.ANY)
        hbm_spec = pl.BlockSpec(memory_space=pltpu.HBM)
        smem_spec = pl.BlockSpec(memory_space=pltpu.SMEM)
        dma = pltpu.SemaphoreType.DMA
        result = pl.pallas_call(
            functools.partial(kernel, bands),
            out_shape=jax.ShapeDtypeStruct((width, rows, depth), f32),
            in_specs=[hbm_spec, smem_spec, smem_spec] + [hbm_spec] * 3,
            out_specs=any_spec,
            scratch_shapes=[
                pltpu.VMEM((width, rows, depth), f32),
                pltpu.VMEM((width, rows, depth), f32),
                pltpu.VMEM((rows + 2, wide, LANES), f32),
                pltpu.VMEM((rows, wide, LANES), f32),
                pltpu.VMEM((16, LANES), f32),
                pltpu.VMEM((16, LANES), f32),
                table,
                pltpu.VMEM((wide, LANES), f32),
                pltpu.VMEM((8, wide, LANES), f32),
                pltpu.VMEM((8, wide, LANES), f32),
                pltpu.VMEM((2, wide, LANES), f32),
                pltpu.VMEM((2, wide, LANES), f32),
                pltpu.VMEM((PARTS, wide, LANES), f32),
                pltpu.VMEM((PARTS, wide, LANES), f32),
                pltpu.VMEM((8, 2 * wide, 2 * LANES), jnp.bfloat16),
                pltpu.VMEM((8, 2 * wide, LANES), f32),
                pltpu.VMEM((PARTS, PACKED, LANES), f32),
                pltpu.VMEM((PARTS, PACKED, LANES), f32),
                dma((4,)),
                dma((1,)),
                dma((2,)),
                dma((2,)),
                dma((PARTS,)),
                dma((PARTS,)),
                dma((PARTS,)),
                dma((PARTS,)),
            ],
            compiler_params=pltpu.CompilerParams(collective_id=0, has_side_effects=True, vmem_limit_bytes=60 << 20),
        )(jnp.transpose(state, (1, 0, 2)), filter_flag, cutoff, coefs, *tables)
        return jnp.transpose(result, (1, 0, 2))

    return jax.shard_map(
        body,
        mesh=mesh,
        in_specs=(P("lat", "lon", None), P("lat"), P("lat")),
        out_specs=P("lat", "lon", None),
        check_vma=False,
    )
```

```python
import functools
import math

import jax
import jax.numpy as jnp
import numpy as np
from jax import lax
from jax.experimental import pallas as pl
from jax.experimental.pallas import tpu as pltpu
from jax.sharding import PartitionSpec as P

MESH = pl.DeviceIdType.MESH
PARTS = 16
LANES = 128
OPEN_CUT = 4096.0
PACKED = 72


def split_table(table):
    high = np.asarray(table, dtype=jnp.bfloat16)
    low = np.asarray(table - high.astype(np.float64), dtype=jnp.bfloat16)
    return high, low


def dft_tables(nlon, width, wide):
    points = np.full(wide, -10**6)
    points[:width] = np.arange(width)
    points[width] = width
    points[wide - 1] = -1
    used = points > -10**6
    forward = np.zeros((8, 2 * wide, 2 * wide))
    inverse = np.zeros((8, 2 * wide, 2 * wide))
    sines = np.zeros((8, wide))
    for group in range(8):
        for row in range(wide):
            if group:
                if row >= width:
                    continue
                wave = group + PARTS * row
                weight = 2.0 / nlon
            else:
                half = width // 2 + 1
                if row < half:
                    wave = PARTS * row
                elif row < width + 1:
                    wave = 8 + PARTS * (row - half)
                else:
                    continue
                weight = (1.0 if wave in (0, nlon // 2) else 2.0) / nlon
            phase = np.where(used, (points * wave) % nlon, 0) * (2.0 * math.pi / nlon)
            cos_vals = np.where(used, np.cos(phase), 0.0)
            sin_vals = np.where(used, np.sin(phase), 0.0)
            inner = np.arange(wide) < width
            if group:
                forward[group, row, :wide] = cos_vals
                forward[group, row, wide:] = -sin_vals
                forward[group, wide + row, :wide] = -sin_vals
                forward[group, wide + row, wide:] = -cos_vals
                inverse[group, :wide, row] = weight * cos_vals * inner
                inverse[group, :wide, wide + row] = -weight * sin_vals * inner
                inverse[group, wide:, row] = weight * sin_vals * inner
                inverse[group, wide:, wide + row] = weight * cos_vals * inner
            else:
                base = 0 if row < half else wide
                part = slice(base, base + wide)
                forward[0, row, part] = cos_vals
                forward[0, wide + row, part] = -sin_vals
                inverse[0, part, row] = weight * cos_vals * inner
                inverse[0, part, wide + row] = -weight * sin_vals * inner
            sines[group, row] = math.sin(2.0 * math.pi * wave / nlon)
    waves = np.zeros((wide, LANES), np.float32)
    waves[:, :8] = sines.T
    return np.concatenate(split_table(np.concatenate([forward, inverse])), axis=1), waves


def coef_table(nlat, bands):
    rows = nlat // bands
    index = np.arange(-1, nlat + 1).astype(np.float32)
    angle = np.float32(-0.5 * math.pi) + (index + np.float32(0.5)) * np.float32(math.pi) / np.float32(nlat)
    cosine = np.cos(angle.astype(np.float64)).astype(np.float32).astype(np.float64)
    flux = cosine.copy()
    flux[0] = 0.0
    flux[-1] = 0.0
    table = np.zeros((bands, 16, LANES))
    for band in range(bands):
        at = band * rows + 1
        for row in range(rows):
            table[band, row] = 0.015 / cosine[at + row]
        for pair in range(rows // 2):
            even = at + 2 * pair
            odd = even + 1
            lane = np.zeros(8)
            lane[0] = 0.03 / cosine[even]
            lane[1] = 0.03 / cosine[odd]
            lane[4] = -0.015 * flux[odd] / cosine[even]
            lane[5] = 0.015 * flux[even] / cosine[odd]
            lane[6] = 0.015 * flux[even - 1] / cosine[even]
            lane[7] = -0.015 * flux[odd + 1] / cosine[odd]
            table[band, 8 + pair] = np.repeat(lane, 16)
    return table.astype(np.float32)


def wave_sum(terms):
    total = None
    for factor, value in terms:
        if abs(factor) < 1e-9:
            continue
        if abs(abs(factor) - 1.0) < 1e-9:
            if total is None:
                total = value if factor > 0 else -value
            else:
                total = total + value if factor > 0 else total - value
        else:
            part = value * np.float32(factor)
            total = part if total is None else total + part
    return total


def half_dft(even_in, odd_in):
    unit = 2.0 * math.pi / PARTS
    sums = [even_in[0] + even_in[8]] + [even_in[a] + even_in[8 - a] for a in (1, 2, 3)] + [even_in[4]]
    diffs = [even_in[0] - even_in[8]] + [even_in[a] - even_in[8 - a] for a in (1, 2, 3)]
    odd_sums = [None] + [odd_in[a] + odd_in[8 - a] for a in (1, 2, 3)] + [odd_in[4]]
    odd_diffs = [None] + [odd_in[a] - odd_in[8 - a] for a in (1, 2, 3)]
    cos_out = []
    sin_out = []
    for k in range(9):
        parts = diffs if k % 2 else sums
        cos_out.append(wave_sum([(math.cos(unit * a * k), parts[a]) for a in range(len(parts))]))
        parts = odd_sums if k % 2 else odd_diffs
        sin_out.append(wave_sum([(math.sin(unit * a * k), parts[a]) for a in range(1, len(parts))]))
    return cos_out, sin_out


def split_value(value):
    high = value.astype(jnp.bfloat16)
    low = (value - high.astype(jnp.float32)).astype(jnp.bfloat16)
    return jnp.concatenate([high, low], axis=1)


def table_dot(table, pair):
    both = jnp.dot(table, pair, preferred_element_type=jnp.float32)
    half = table.shape[0] // 2
    return both[:half, :LANES] + both[:half, LANES:] + both[half:, :LANES]


def kernel(
    bands,
    state_hbm, flag_hbm, cut_hbm, coef_hbm, table_hbm, wave_hbm,
    out_hbm,
    state, flag_ref, cut_ref, result, winds, press, cuts, coef, table, waves, damps, turns,
    halo_out, halo_in, send, recv, spectra, fields, bsend, brecv,
    load_sem, store_sem, halo_send, halo_recv, send_sem, recv_sem, bsend_sem, brecv_sem,
):
    lat = lax.axis_index("lat")
    lon = lax.axis_index("lon")
    width, rows = state_hbm.shape[0], state_hbm.shape[1]
    wide = recv.shape[1]
    spare = jnp.zeros((wide - width, LANES), jnp.float32)

    def field(row, part):
        return jnp.concatenate([state[:, row, pl.ds(part * LANES, LANES)], spare], axis=0)

    above = lax.rem(lat + bands - 1, bands)
    below = lax.rem(lat + 1, bands)
    chip = lon // 2
    core = lon % 2

    loads = [pltpu.make_async_copy(state_hbm, state, load_sem.at[0])]
    loads.append(pltpu.make_async_copy(coef_hbm.at[lat], coef, load_sem.at[1]))
    loads.append(pltpu.make_async_copy(flag_hbm, flag_ref, load_sem.at[2]))
    loads.append(pltpu.make_async_copy(cut_hbm, cut_ref, load_sem.at[3]))
    tables = ((wave_hbm, waves), (table_hbm, table))
    for at, (source, target) in enumerate(tables):
        loads.append(pltpu.make_async_copy(source, target, load_sem.at[4 + at]))
    for load in loads[:4]:
        load.start()

    barrier = pltpu.get_barrier_semaphore()
    for offset in range(1, PARTS):
        pl.semaphore_signal(barrier, inc=1, device_id=(lat, lax.rem(lon + offset, PARTS)), device_id_type=MESH)
    pl.semaphore_signal(barrier, inc=1, device_id=(above, lon), device_id_type=MESH)
    pl.semaphore_signal(barrier, inc=1, device_id=(below, lon), device_id_type=MESH)

    lane = lax.broadcasted_iota(jnp.int32, (wide, LANES), 1)
    line = lax.broadcasted_iota(jnp.int32, (wide, LANES), 0)
    first = lane < 64
    block = (lane // 16) % 4
    for load in loads[:4]:
        load.wait()
    for load in loads[4:]:
        load.start()
    for row in range(rows):
        kept = jnp.full((1, LANES), cut_ref[row], jnp.int32).astype(jnp.float32)
        flag = jnp.full((1, LANES), flag_ref[row], jnp.int32)
        cuts[pl.ds(row + 1, 1), :] = jnp.where(flag == 1, kept, OPEN_CUT)

    def prepare(row):
        left = field(row, 0)
        right = field(row, 1)
        turned = pltpu.roll(right, 64, 1)
        step = jnp.where(lane < 63, pltpu.roll(turned, LANES - 1, 1), 0.0) - jnp.where(lane > 0, pltpu.roll(turned, 1, 1), 0.0)
        vert = right - 0.1 * step
        step = jnp.where(lane < 63, pltpu.roll(vert, LANES - 1, 1), 0.0) - jnp.where(lane > 0, pltpu.roll(vert, 1, 1), 0.0)
        press[row] = turned - 0.015 * step
        result[:, row, pl.ds(LANES, LANES)] = vert[:width]
        scale = coef[pl.ds(row, 1), :]
        zonal = left - scale * (pltpu.roll(turned, wide - 1, 0) - pltpu.roll(turned, 1, 0))
        merid = left
        if row < rows - 1:
            merid = merid - 0.015 * field(row + 1, 1)
        if row > 0:
            merid = merid + 0.015 * field(row - 1, 1)
        winds[row + 1] = jnp.where(first, zonal, merid)

    for row in range(rows):
        prepare(row)
    for side, row in ((0, 0), (1, rows - 1)):
        turned = pltpu.roll(field(row, 1), 64, 1)
        message = jnp.where(first, turned, winds[row + 1])
        halo_out[side] = jnp.where(line == width, cuts[pl.ds(row + 1, 1), :], message)

    def pack(pair, slot):
        even = 2 * pair + 1
        sources = (
            jnp.where(first, winds[even], winds[even + 1]),
            jnp.where(first, winds[even + 1], winds[even]),
            jnp.where(first, press[even - 1], winds[even - 1]),
            jnp.where(first, press[even], winds[even + 2]),
        )
        for quarter in range(4):
            chunk = sources[quarter]
            for at in range(4):
                if at != quarter:
                    chunk = jnp.where(block == at, pltpu.roll(sources[at], (16 * (at - quarter)) % LANES, 1), chunk)
            send[slot + 2 * quarter] = chunk

    def pack_inner(at, carry):
        pack(1 + at, 8 * at)
        return carry

    def pack_outer(at, carry):
        pack(3 * at, 8 * at + 1)
        return carry

    lax.fori_loop(0, 2, pack_inner, 0, unroll=2)
    pl.semaphore_wait(barrier, PARTS + 1)

    halos = []
    for side, device in ((0, above), (1, below)):
        halos.append(
            pltpu.make_async_remote_copy(
                src_ref=halo_out.at[side],
                dst_ref=halo_in.at[1 - side],
                send_sem=halo_send.at[side],
                recv_sem=halo_recv.at[1 - side],
                device_id=(device, lon),
                device_id_type=MESH,
            )
        )
    for halo in halos:
        halo.start()

    def forward_copy(source, slot, device):
        return pltpu.make_async_remote_copy(
            src_ref=send.at[source],
            dst_ref=recv.at[slot],
            send_sem=send_sem.at[source],
            recv_sem=recv_sem.at[slot],
            device_id=(lat, device),
            device_id_type=MESH,
        )

    def backward_copy(source, slot, device):
        return pltpu.make_async_remote_copy(
            src_ref=bsend.at[source],
            dst_ref=brecv.at[slot],
            send_sem=bsend_sem.at[source],
            recv_sem=brecv_sem.at[slot],
            device_id=(lat, device),
            device_id_type=MESH,
        )

    order = (4, 3, 5, 2, 6, 1, 7, 0)

    def send_to(copy, kind):
        for offset in order:
            target = 2 * lax.rem(chip + offset, 8) + kind
            if offset:
                copy(target, lon, target).start()
            else:
                @pl.when(core != kind)
                def _():
                    copy(target, lon, target).start()

    send_to(forward_copy, 0)

    for side in range(2):
        halos[side].wait_recv()
    inside = jnp.where(lat > 0, 0.015, 0.0)
    upper = halo_in[0]
    cuts[pl.ds(0, 1), :] = upper[width : width + 1]
    winds[0] = jnp.where(line < width, upper - 0.015 * field(0, 1), 0.0)
    winds[1] = winds[1] + jnp.where(first | (line >= width), 0.0, inside * pltpu.roll(upper, 64, 1))
    inside = jnp.where(lat < bands - 1, 0.015, 0.0)
    lower = halo_in[1]
    cuts[pl.ds(rows + 1, 1), :] = lower[width : width + 1]
    winds[rows + 1] = jnp.where(line < width, lower + 0.015 * field(rows - 1, 1), 0.0)
    winds[rows] = winds[rows] - jnp.where(first | (line >= width), 0.0, inside * pltpu.roll(lower, 64, 1))

    lax.fori_loop(0, 2, pack_outer, 0, unroll=2)
    send_to(forward_copy, 1)
    recv[lon] = send[lon]

    half = chip // 4
    mine = (1 - core) * (1 + half) + core * 3 * half
    lanes = lax.broadcasted_iota(jnp.int32, (1, LANES), 1) // 16
    cut_even = cuts[pl.ds(2 * mine + 1, 1), :]
    cut_odd = cuts[pl.ds(2 * mine + 2, 1), :]
    limit = jnp.where((lanes == 0) | (lanes == 2) | (lanes == 5), cut_even, cut_odd)
    limit = jnp.where(lanes == 6, cuts[pl.ds(2 * mine, 1), :], limit)
    limit = jnp.where(lanes == 7, cuts[pl.ds(2 * mine + 3, 1), :], limit)
    factor = coef[pl.ds(8 + mine, 1), :]
    loads[4].wait()

    for group in range(8):
        wave = PARTS * line + group
        if group:
            wave = jnp.minimum(wave, PARTS * width - wave)
        else:
            wave = jnp.where(line <= width // 2, wave, PARTS * (line - width // 2 - 1) + 8)
        ratio = limit / jnp.maximum(wave, 1).astype(jnp.float32)
        damps[group] = jnp.minimum(1.0, ratio * ratio)
        turns[group] = factor * waves[:, group : group + 1]
    for load in loads[5:]:
        load.wait()

    def receive(offset, carry):
        source = lax.rem(lon + offset, PARTS)
        forward_copy(source, source, source).wait_recv()
        return carry

    lax.fori_loop(1, PARTS, receive, 0)

    def gather_waves(at, carry):
        where = pl.multiple_of(16 * at, 16)
        spans = pl.ds(where, 16)
        images = pl.ds(pl.multiple_of(wide + where, 16), 16)
        values = [recv[a, spans, :] for a in range(PARTS)]
        evens = [values[0]] + [values[a] + values[PARTS - a] for a in range(1, 8)] + [values[8]]
        odds = [None] + [values[a] - values[PARTS - a] for a in range(1, 8)]
        cos_out, sin_out = half_dft(evens, odds)
        spectra[0, spans, :] = split_value(cos_out[0])
        spectra[0, images, :] = split_value(cos_out[8])
        for k in range(1, 8):
            spectra[k, spans, :] = split_value(cos_out[k])
            spectra[k, images, :] = split_value(sin_out[k])
        return carry

    lax.fori_loop(0, wide // 16, gather_waves, 0, unroll=6)

    def transform(group, carry):
        values = table_dot(table[group], spectra[group])
        damping = damps[group]
        real = values[:wide] * damping
        imag = values[wide:] * damping
        turn = turns[group]
        zonal = lane < 32
        lift_real = jnp.where(zonal, turn * imag, factor * real)
        lift_imag = jnp.where(zonal, -turn * real, factor * imag)
        inner = (lane >= 32) & first
        outs = []
        for value, lift in ((real, lift_real), (imag, lift_imag)):
            total = pltpu.roll(lift, 32, 1) + pltpu.roll(lift, 96, 1) + pltpu.roll(lift, 64, 1)
            outs.append(jnp.where(inner, value + damping * total, value))
        both = split_value(jnp.concatenate(outs, axis=0))
        fields[group] = table_dot(table[8 + group], both)
        return carry

    lax.fori_loop(0, 8, transform, 0, unroll=8)

    def scatter_waves(at, carry):
        where = pl.multiple_of(16 * at, 16)
        spans = pl.ds(where, 16)
        images = pl.ds(pl.multiple_of(wide + where, 16), 16)
        evens = [fields[0, spans, :]] + [fields[k, spans, :] for k in range(1, 8)] + [fields[0, images, :]]
        odds = [None] + [fields[k, images, :] for k in range(1, 8)]
        cos_out, sin_out = half_dft(evens, odds)
        circles[0, spans, :] = cos_out[0]
        circles[8, spans, :] = cos_out[8]
        for a in range(1, 8):
            circles[a, spans, :] = cos_out[a] - sin_out[a]
            circles[PARTS - a, spans, :] = cos_out[a] + sin_out[a]
        return carry

    circles = recv
    lax.fori_loop(0, wide // 16, scatter_waves, 0, unroll=6)
    narrow = lax.broadcasted_iota(jnp.int32, (24, LANES), 1)

    def pack_back(a, carry):
        rest = circles[a, pl.ds(72, 24), :]
        for at in range(3):
            spans = pl.ds(24 * at, 24)
            bsend[a, spans, :] = jnp.where(narrow < 96, circles[a, spans, :], pltpu.roll(rest, 96 - 32 * at, 1))
        return carry

    lax.fori_loop(0, PARTS, pack_back, 0, unroll=PARTS)
    send_to(backward_copy, 0)
    send_to(backward_copy, 1)
    brecv[lon] = bsend[lon]

    def unpack(pair, slot):
        chunks = []
        for quarter in range(4):
            source = slot + 2 * quarter

            @pl.when(source != lon)
            def _():
                backward_copy(source, source, source).wait_recv()

            pieces = [brecv[source, pl.ds(24 * at, 24), :] for at in range(3)]
            rest = jnp.where(narrow < 32, pltpu.roll(pieces[0], 32, 1), pltpu.roll(pieces[1], 64, 1))
            rest = jnp.where(narrow < 64, rest, pltpu.roll(pieces[2], 96, 1))
            chunks.append(jnp.concatenate(pieces + [rest], axis=0))
        parts = []
        for at in range(4):
            shift = 64 if at >= 2 else 0
            part = None
            for quarter in range(4):
                amount = (16 * (quarter - at) + shift) % LANES
                moved = pltpu.roll(chunks[quarter], amount, 1) if amount else chunks[quarter]
                part = moved if part is None else jnp.where(block == quarter, moved, part)
            parts.append(part)
        even = 2 * pair
        spans = pl.ds(0, LANES)
        result[:, even, spans] = jnp.where(first, parts[0], parts[1])[:width]
        result[:, even + 1, spans] = jnp.where(first, parts[1], parts[0])[:width]
        spans = pl.ds(LANES, LANES)
        result[:, even, spans] = jnp.where(first[:width], result[:, even, spans], parts[2][:width])
        result[:, even + 1, spans] = jnp.where(first[:width], result[:, even + 1, spans], parts[3][:width])

    for at in range(2):
        unpack(1 + at, 8 * at)
    for at in range(2):
        unpack(3 * at, 8 * at + 1)
    store = pltpu.make_async_copy(result, out_hbm, store_sem.at[0])
    store.start()

    def finish(offset, carry):
        target = lax.rem(lon + offset, PARTS)
        forward_copy(target, lon, target).wait_send()
        backward_copy(target, lon, target).wait_send()
        return carry

    lax.fori_loop(1, PARTS, finish, 0)
    for halo in halos:
        halo.wait_send()
    store.wait()


def solution(mesh):
    bands = mesh.shape["lat"]

    def body(state, filter_flag, cutoff):
        rows, width, depth = state.shape
        wide = (width + 2 + 15) // 16 * 16
        tables = dft_tables(width * PARTS, width, wide)
        coefs = coef_table(rows * bands, bands)
        f32 = jnp.float32
        table = pltpu.VMEM((16, 4 * wide, 2 * wide), jnp.bfloat16)
        any_spec = pl.BlockSpec(memory_space=pl.ANY)
        hbm_spec = pl.BlockSpec(memory_space=pltpu.HBM)
        dma = pltpu.SemaphoreType.DMA
        operands = (jnp.transpose(state, (1, 0, 2)), filter_flag, cutoff) + tuple(map(jnp.asarray, (coefs,) + tables))
        result = pl.pallas_call(
            functools.partial(kernel, bands),
            out_shape=jax.ShapeDtypeStruct((width, rows, depth), f32),
            in_specs=[hbm_spec] * 6,
            out_specs=any_spec,
            scratch_shapes=[
                pltpu.VMEM((width, rows, depth), f32),
                pltpu.SMEM((rows,), jnp.int32),
                pltpu.SMEM((rows,), jnp.int32),
                pltpu.VMEM((width, rows, depth), f32),
                pltpu.VMEM((rows + 2, wide, LANES), f32),
                pltpu.VMEM((rows, wide, LANES), f32),
                pltpu.VMEM((16, LANES), f32),
                pltpu.VMEM((16, LANES), f32),
                table,
                pltpu.VMEM((wide, LANES), f32),
                pltpu.VMEM((8, wide, LANES), f32),
                pltpu.VMEM((8, wide, LANES), f32),
                pltpu.VMEM((2, wide, LANES), f32),
                pltpu.VMEM((2, wide, LANES), f32),
                pltpu.VMEM((PARTS, wide, LANES), f32),
                pltpu.VMEM((PARTS, wide, LANES), f32),
                pltpu.VMEM((8, 2 * wide, 2 * LANES), jnp.bfloat16),
                pltpu.VMEM((8, 2 * wide, LANES), f32),
                pltpu.VMEM((PARTS, PACKED, LANES), f32),
                pltpu.VMEM((PARTS, PACKED, LANES), f32),
                dma((6,)),
                dma((1,)),
                dma((2,)),
                dma((2,)),
                dma((PARTS,)),
                dma((PARTS,)),
                dma((PARTS,)),
                dma((PARTS,)),
            ],
            compiler_params=pltpu.CompilerParams(collective_id=0, has_side_effects=True, vmem_limit_bytes=32 << 20),
        )(*(pltpu.with_memory_space_constraint(value, pltpu.HBM) for value in operands))
        return jnp.transpose(result, (1, 0, 2))

    return jax.shard_map(
        body,
        mesh=mesh,
        in_specs=(P("lat", "lon", None), P("lat"), P("lat")),
        out_specs=P("lat", "lon", None),
        check_vma=False,
    )
```

```python
import functools
import math

import jax
import jax.numpy as jnp
import numpy as np
from jax import lax
from jax.experimental import pallas as pl
from jax.experimental.pallas import tpu as pltpu
from jax.sharding import PartitionSpec as P

MESH = pl.DeviceIdType.MESH
PARTS = 16
LANES = 128
OPEN_CUT = 4096.0
PACKED = 72


def split_table(table):
    high = np.asarray(table, dtype=jnp.bfloat16)
    low = np.asarray(table - high.astype(np.float64), dtype=jnp.bfloat16)
    return high, low


def dft_tables(nlon, width, wide):
    points = np.full(wide, -10**6)
    points[:width] = np.arange(width)
    points[width] = width
    points[wide - 1] = -1
    used = points > -10**6
    forward = np.zeros((8, 2 * wide, 2 * wide))
    inverse = np.zeros((8, 2 * wide, 2 * wide))
    sines = np.zeros((8, wide))
    for group in range(8):
        for row in range(wide):
            if group:
                if row >= width:
                    continue
                wave = group + PARTS * row
                weight = 2.0 / nlon
            else:
                half = width // 2 + 1
                if row < half:
                    wave = PARTS * row
                elif row < width + 1:
                    wave = 8 + PARTS * (row - half)
                else:
                    continue
                weight = (1.0 if wave in (0, nlon // 2) else 2.0) / nlon
            phase = np.where(used, (points * wave) % nlon, 0) * (2.0 * math.pi / nlon)
            cos_vals = np.where(used, np.cos(phase), 0.0)
            sin_vals = np.where(used, np.sin(phase), 0.0)
            inner = np.arange(wide) < width
            if group:
                forward[group, row, :wide] = cos_vals
                forward[group, row, wide:] = -sin_vals
                forward[group, wide + row, :wide] = -sin_vals
                forward[group, wide + row, wide:] = -cos_vals
                inverse[group, :wide, row] = weight * cos_vals * inner
                inverse[group, :wide, wide + row] = -weight * sin_vals * inner
                inverse[group, wide:, row] = weight * sin_vals * inner
                inverse[group, wide:, wide + row] = weight * cos_vals * inner
            else:
                base = 0 if row < half else wide
                part = slice(base, base + wide)
                forward[0, row, part] = cos_vals
                forward[0, wide + row, part] = -sin_vals
                inverse[0, part, row] = weight * cos_vals * inner
                inverse[0, part, wide + row] = -weight * sin_vals * inner
            sines[group, row] = math.sin(2.0 * math.pi * wave / nlon)
    waves = np.zeros((wide, LANES), np.float32)
    waves[:, :8] = sines.T
    return np.concatenate(split_table(np.concatenate([forward, inverse])), axis=1), waves


def coef_table(nlat, bands):
    rows = nlat // bands
    index = np.arange(-1, nlat + 1).astype(np.float32)
    angle = np.float32(-0.5 * math.pi) + (index + np.float32(0.5)) * np.float32(math.pi) / np.float32(nlat)
    cosine = np.cos(angle.astype(np.float64)).astype(np.float32).astype(np.float64)
    flux = cosine.copy()
    flux[0] = 0.0
    flux[-1] = 0.0
    table = np.zeros((bands, 16, LANES))
    for band in range(bands):
        at = band * rows + 1
        for row in range(rows):
            table[band, row] = 0.015 / cosine[at + row]
        for pair in range(rows // 2):
            even = at + 2 * pair
            odd = even + 1
            lane = np.zeros(8)
            lane[0] = 0.03 / cosine[even]
            lane[1] = 0.03 / cosine[odd]
            lane[4] = -0.015 * flux[odd] / cosine[even]
            lane[5] = 0.015 * flux[even] / cosine[odd]
            lane[6] = 0.015 * flux[even - 1] / cosine[even]
            lane[7] = -0.015 * flux[odd + 1] / cosine[odd]
            table[band, 8 + pair] = np.repeat(lane, 16)
    return table.astype(np.float32)


def wave_sum(terms):
    total = None
    for factor, value in terms:
        if abs(factor) < 1e-9:
            continue
        if abs(abs(factor) - 1.0) < 1e-9:
            if total is None:
                total = value if factor > 0 else -value
            else:
                total = total + value if factor > 0 else total - value
        else:
            part = value * np.float32(factor)
            total = part if total is None else total + part
    return total


def half_dft(even_in, odd_in):
    unit = 2.0 * math.pi / PARTS
    sums = [even_in[0] + even_in[8]] + [even_in[a] + even_in[8 - a] for a in (1, 2, 3)] + [even_in[4]]
    diffs = [even_in[0] - even_in[8]] + [even_in[a] - even_in[8 - a] for a in (1, 2, 3)]
    odd_sums = [None] + [odd_in[a] + odd_in[8 - a] for a in (1, 2, 3)] + [odd_in[4]]
    odd_diffs = [None] + [odd_in[a] - odd_in[8 - a] for a in (1, 2, 3)]
    cos_out = []
    sin_out = []
    for k in range(9):
        parts = diffs if k % 2 else sums
        cos_out.append(wave_sum([(math.cos(unit * a * k), parts[a]) for a in range(len(parts))]))
        parts = odd_sums if k % 2 else odd_diffs
        sin_out.append(wave_sum([(math.sin(unit * a * k), parts[a]) for a in range(1, len(parts))]))
    return cos_out, sin_out


def split_value(value):
    high = value.astype(jnp.bfloat16)
    low = (value - high.astype(jnp.float32)).astype(jnp.bfloat16)
    return jnp.concatenate([high, low], axis=1)


def table_dot(table, pair):
    both = jnp.dot(table, pair, preferred_element_type=jnp.float32)
    half = table.shape[0] // 2
    return both[:half, :LANES] + both[:half, LANES:] + both[half:, :LANES]


def kernel(
    bands,
    state_hbm, flag_hbm, cut_hbm, coef_hbm, table_hbm, wave_hbm,
    result,
    state, flag_ref, cut_ref, winds, press, slopes, cuts, coef, table, waves, damps, turns,
    halo_out, halo_in, send, recv, spectra, fields, bsend, brecv,
    load_sem, halo_send, halo_recv, send_sem, recv_sem, bsend_sem, brecv_sem,
):
    lat = lax.axis_index("lat")
    lon = lax.axis_index("lon")
    width, rows = state_hbm.shape[0], state_hbm.shape[1]
    wide = recv.shape[1]
    spare = jnp.zeros((wide - width, LANES), jnp.float32)

    def field(row, part):
        return jnp.concatenate([state[:, row, pl.ds(part * LANES, LANES)], spare], axis=0)

    above = lax.rem(lat + bands - 1, bands)
    below = lax.rem(lat + 1, bands)
    chip = lon // 2
    core = lon % 2

    def state_copy(part):
        spans = pl.ds(part * LANES, LANES)
        return pltpu.make_async_copy(state_hbm.at[:, :, spans], state.at[:, :, spans], load_sem.at[part])

    loads = [state_copy(1), state_copy(0)]
    loads.append(pltpu.make_async_copy(coef_hbm.at[lat], coef, load_sem.at[2]))
    loads.append(pltpu.make_async_copy(flag_hbm, flag_ref, load_sem.at[3]))
    loads.append(pltpu.make_async_copy(cut_hbm, cut_ref, load_sem.at[4]))
    tables = ((wave_hbm, waves), (table_hbm, table))
    for at, (source, target) in enumerate(tables):
        loads.append(pltpu.make_async_copy(source, target, load_sem.at[5 + at]))
    for load in loads[:5]:
        load.start()

    barrier = pltpu.get_barrier_semaphore()
    for offset in range(1, PARTS):
        pl.semaphore_signal(barrier, inc=1, device_id=(lat, lax.rem(lon + offset, PARTS)), device_id_type=MESH)
    pl.semaphore_signal(barrier, inc=1, device_id=(above, lon), device_id_type=MESH)
    pl.semaphore_signal(barrier, inc=1, device_id=(below, lon), device_id_type=MESH)

    lane = lax.broadcasted_iota(jnp.int32, (wide, LANES), 1)
    line = lax.broadcasted_iota(jnp.int32, (wide, LANES), 0)
    first = lane < 64
    block = (lane // 16) % 4
    loads[0].wait()
    for row in range(rows):
        right = field(row, 1)
        turned = pltpu.roll(right, 64, 1)
        step = jnp.where(lane < 63, pltpu.roll(turned, LANES - 1, 1), 0.0) - jnp.where(lane > 0, pltpu.roll(turned, 1, 1), 0.0)
        vert = right - 0.1 * step
        step = jnp.where(lane < 63, pltpu.roll(vert, LANES - 1, 1), 0.0) - jnp.where(lane > 0, pltpu.roll(vert, 1, 1), 0.0)
        press[row] = turned - 0.015 * step
        result[:, row, pl.ds(LANES, LANES)] = vert[:width]
        slopes[row] = pltpu.roll(turned, wide - 1, 0) - pltpu.roll(turned, 1, 0)
    for load in loads[1:3]:
        load.wait()

    def prepare(row):
        left = field(row, 0)
        zonal = left - coef[pl.ds(row, 1), :] * slopes[row]
        merid = left
        if row < rows - 1:
            merid = merid - 0.015 * field(row + 1, 1)
        if row > 0:
            merid = merid + 0.015 * field(row - 1, 1)
        winds[row + 1] = jnp.where(first, zonal, merid)

    def pack(pair, slot):
        even = 2 * pair + 1
        sources = (
            jnp.where(first, winds[even], winds[even + 1]),
            jnp.where(first, winds[even + 1], winds[even]),
            jnp.where(first, press[even - 1], winds[even - 1]),
            jnp.where(first, press[even], winds[even + 2]),
        )
        for quarter in range(4):
            chunk = sources[quarter]
            for at in range(4):
                if at != quarter:
                    chunk = jnp.where(block == at, pltpu.roll(sources[at], (16 * (at - quarter)) % LANES, 1), chunk)
            send[slot + 2 * quarter] = chunk

    halos = []
    for side, device in ((0, above), (1, below)):
        halos.append(
            pltpu.make_async_remote_copy(
                src_ref=halo_out.at[side],
                dst_ref=halo_in.at[1 - side],
                send_sem=halo_send.at[side],
                recv_sem=halo_recv.at[1 - side],
                device_id=(device, lon),
                device_id_type=MESH,
            )
        )
    def forward_copy(source, slot, device):
        return pltpu.make_async_remote_copy(
            src_ref=send.at[source],
            dst_ref=recv.at[slot],
            send_sem=send_sem.at[source],
            recv_sem=recv_sem.at[slot],
            device_id=(lat, device),
            device_id_type=MESH,
        )

    def backward_copy(source, slot, device):
        return pltpu.make_async_remote_copy(
            src_ref=bsend.at[source],
            dst_ref=brecv.at[slot],
            send_sem=bsend_sem.at[source],
            recv_sem=brecv_sem.at[slot],
            device_id=(lat, device),
            device_id_type=MESH,
        )

    order = (4, 3, 5, 2, 6, 1, 7, 0)

    def send_to(copy, kind):
        for offset in order:
            target = 2 * lax.rem(chip + offset, 8) + kind
            if offset:
                copy(target, lon, target).start()
            else:
                @pl.when(core != kind)
                def _():
                    copy(target, lon, target).start()

    def pack_and_send(pair, at, kind):
        pack(pair, 8 * at + kind)
        if pair == 1:
            pl.semaphore_wait(barrier, PARTS + 1)
        for offset in range(4):
            target = 8 * at + 2 * lax.rem(chip + offset, 4) + kind

            @pl.when(target != lon)
            def _():
                forward_copy(target, lon, target).start()

    for row in range(1, 5):
        prepare(row)
    pack_and_send(1, 0, 0)
    for row in range(5, 7):
        prepare(row)
    pack_and_send(2, 1, 0)
    prepare(0)
    prepare(rows - 1)
    for load in loads[3:5]:
        load.wait()
    for load in loads[5:]:
        load.start()
    for row in range(rows):
        kept = jnp.full((1, LANES), cut_ref[row], jnp.int32).astype(jnp.float32)
        flag = jnp.full((1, LANES), flag_ref[row], jnp.int32)
        cuts[pl.ds(row + 1, 1), :] = jnp.where(flag == 1, kept, OPEN_CUT)
    for side, row in ((0, 0), (1, rows - 1)):
        turned = pltpu.roll(field(row, 1), 64, 1)
        message = jnp.where(first, turned, winds[row + 1])
        halo_out[side] = jnp.where(line == width, cuts[pl.ds(row + 1, 1), :], message)
    for halo in halos:
        halo.start()

    for side in range(2):
        halos[side].wait_recv()
    inside = jnp.where(lat > 0, 0.015, 0.0)
    upper = halo_in[0]
    cuts[pl.ds(0, 1), :] = upper[width : width + 1]
    winds[0] = jnp.where(line < width, upper - 0.015 * field(0, 1), 0.0)
    winds[1] = winds[1] + jnp.where(first | (line >= width), 0.0, inside * pltpu.roll(upper, 64, 1))
    inside = jnp.where(lat < bands - 1, 0.015, 0.0)
    lower = halo_in[1]
    cuts[pl.ds(rows + 1, 1), :] = lower[width : width + 1]
    winds[rows + 1] = jnp.where(line < width, lower + 0.015 * field(rows - 1, 1), 0.0)
    winds[rows] = winds[rows] - jnp.where(first | (line >= width), 0.0, inside * pltpu.roll(lower, 64, 1))

    pack_and_send(0, 0, 1)
    pack_and_send(3, 1, 1)
    recv[lon] = send[lon]

    half = chip // 4
    mine = (1 - core) * (1 + half) + core * 3 * half
    lanes = lax.broadcasted_iota(jnp.int32, (1, LANES), 1) // 16
    cut_even = cuts[pl.ds(2 * mine + 1, 1), :]
    cut_odd = cuts[pl.ds(2 * mine + 2, 1), :]
    limit = jnp.where((lanes == 0) | (lanes == 2) | (lanes == 5), cut_even, cut_odd)
    limit = jnp.where(lanes == 6, cuts[pl.ds(2 * mine, 1), :], limit)
    limit = jnp.where(lanes == 7, cuts[pl.ds(2 * mine + 3, 1), :], limit)
    factor = coef[pl.ds(8 + mine, 1), :]
    loads[5].wait()

    for group in range(8):
        wave = PARTS * line + group
        if group:
            wave = jnp.minimum(wave, PARTS * width - wave)
        else:
            wave = jnp.where(line <= width // 2, wave, PARTS * (line - width // 2 - 1) + 8)
        ratio = limit / jnp.maximum(wave, 1).astype(jnp.float32)
        damps[group] = jnp.minimum(1.0, ratio * ratio)
        turns[group] = factor * waves[:, group : group + 1]
    for load in loads[6:]:
        load.wait()

    def receive(offset, carry):
        source = lax.rem(lon + offset, PARTS)
        forward_copy(source, source, source).wait_recv()
        return carry

    lax.fori_loop(1, PARTS, receive, 0)

    def gather_waves(at, carry):
        where = pl.multiple_of(16 * at, 16)
        spans = pl.ds(where, 16)
        images = pl.ds(pl.multiple_of(wide + where, 16), 16)
        values = [recv[a, spans, :] for a in range(PARTS)]
        evens = [values[0]] + [values[a] + values[PARTS - a] for a in range(1, 8)] + [values[8]]
        odds = [None] + [values[a] - values[PARTS - a] for a in range(1, 8)]
        cos_out, sin_out = half_dft(evens, odds)
        spectra[0, spans, :] = split_value(cos_out[0])
        spectra[0, images, :] = split_value(cos_out[8])
        for k in range(1, 8):
            spectra[k, spans, :] = split_value(cos_out[k])
            spectra[k, images, :] = split_value(sin_out[k])
        return carry

    lax.fori_loop(0, wide // 16, gather_waves, 0, unroll=6)

    def transform(group, carry):
        values = table_dot(table[group], spectra[group])
        damping = damps[group]
        real = values[:wide] * damping
        imag = values[wide:] * damping
        turn = turns[group]
        zonal = lane < 32
        lift_real = jnp.where(zonal, turn * imag, factor * real)
        lift_imag = jnp.where(zonal, -turn * real, factor * imag)
        inner = (lane >= 32) & first
        outs = []
        for value, lift in ((real, lift_real), (imag, lift_imag)):
            total = pltpu.roll(lift, 32, 1) + pltpu.roll(lift, 96, 1) + pltpu.roll(lift, 64, 1)
            outs.append(jnp.where(inner, value + damping * total, value))
        both = split_value(jnp.concatenate(outs, axis=0))
        fields[group] = table_dot(table[8 + group], both)
        return carry

    lax.fori_loop(0, 8, transform, 0, unroll=8)

    def scatter_waves(at, carry):
        where = pl.multiple_of(16 * at, 16)
        spans = pl.ds(where, 16)
        images = pl.ds(pl.multiple_of(wide + where, 16), 16)
        evens = [fields[0, spans, :]] + [fields[k, spans, :] for k in range(1, 8)] + [fields[0, images, :]]
        odds = [None] + [fields[k, images, :] for k in range(1, 8)]
        cos_out, sin_out = half_dft(evens, odds)
        circles[0, spans, :] = cos_out[0]
        circles[8, spans, :] = cos_out[8]
        for a in range(1, 8):
            circles[a, spans, :] = cos_out[a] - sin_out[a]
            circles[PARTS - a, spans, :] = cos_out[a] + sin_out[a]
        return carry

    circles = recv
    lax.fori_loop(0, wide // 16, scatter_waves, 0, unroll=6)
    narrow = lax.broadcasted_iota(jnp.int32, (24, LANES), 1)

    def pack_back(a, carry):
        rest = circles[a, pl.ds(72, 24), :]
        for at in range(3):
            spans = pl.ds(24 * at, 24)
            bsend[a, spans, :] = jnp.where(narrow < 96, circles[a, spans, :], pltpu.roll(rest, 96 - 32 * at, 1))
        return carry

    lax.fori_loop(0, PARTS, pack_back, 0, unroll=PARTS)
    send_to(backward_copy, 0)
    send_to(backward_copy, 1)
    brecv[lon] = bsend[lon]

    def unpack(pair, slot):
        chunks = []
        for quarter in range(4):
            source = slot + 2 * quarter

            @pl.when(source != lon)
            def _():
                backward_copy(source, source, source).wait_recv()

            pieces = [brecv[source, pl.ds(24 * at, 24), :] for at in range(3)]
            rest = jnp.where(narrow < 32, pltpu.roll(pieces[0], 32, 1), pltpu.roll(pieces[1], 64, 1))
            rest = jnp.where(narrow < 64, rest, pltpu.roll(pieces[2], 96, 1))
            chunks.append(jnp.concatenate(pieces + [rest], axis=0))
        parts = []
        for at in range(4):
            shift = 64 if at >= 2 else 0
            part = None
            for quarter in range(4):
                amount = (16 * (quarter - at) + shift) % LANES
                moved = pltpu.roll(chunks[quarter], amount, 1) if amount else chunks[quarter]
                part = moved if part is None else jnp.where(block == quarter, moved, part)
            parts.append(part)
        even = 2 * pair
        spans = pl.ds(0, LANES)
        result[:, even, spans] = jnp.where(first, parts[0], parts[1])[:width]
        result[:, even + 1, spans] = jnp.where(first, parts[1], parts[0])[:width]
        spans = pl.ds(LANES, LANES)
        result[:, even, spans] = jnp.where(first[:width], result[:, even, spans], parts[2][:width])
        result[:, even + 1, spans] = jnp.where(first[:width], result[:, even + 1, spans], parts[3][:width])

    for at in range(2):
        unpack(1 + at, 8 * at)
    for at in range(2):
        unpack(3 * at, 8 * at + 1)

    def finish(offset, carry):
        target = lax.rem(lon + offset, PARTS)
        forward_copy(target, lon, target).wait_send()
        backward_copy(target, lon, target).wait_send()
        return carry

    lax.fori_loop(1, PARTS, finish, 0)
    for halo in halos:
        halo.wait_send()


def solution(mesh):
    bands = mesh.shape["lat"]

    def body(state, filter_flag, cutoff):
        rows, width, depth = state.shape
        wide = (width + 2 + 15) // 16 * 16
        tables = dft_tables(width * PARTS, width, wide)
        coefs = coef_table(rows * bands, bands)
        f32 = jnp.float32
        table = pltpu.VMEM((16, 4 * wide, 2 * wide), jnp.bfloat16)
        hbm_spec = pl.BlockSpec(memory_space=pltpu.HBM)
        dma = pltpu.SemaphoreType.DMA
        operands = (jnp.transpose(state, (1, 0, 2)), filter_flag, cutoff) + tuple(map(jnp.asarray, (coefs,) + tables))
        result = pl.pallas_call(
            functools.partial(kernel, bands),
            out_shape=jax.ShapeDtypeStruct((width, rows, depth), f32),
            in_specs=[hbm_spec] * 6,
            out_specs=pl.BlockSpec(memory_space=pltpu.VMEM),
            scratch_shapes=[
                pltpu.VMEM((width, rows, depth), f32),
                pltpu.SMEM((rows,), jnp.int32),
                pltpu.SMEM((rows,), jnp.int32),
                pltpu.VMEM((rows + 2, wide, LANES), f32),
                pltpu.VMEM((rows, wide, LANES), f32),
                pltpu.VMEM((rows, wide, LANES), f32),
                pltpu.VMEM((16, LANES), f32),
                pltpu.VMEM((16, LANES), f32),
                table,
                pltpu.VMEM((wide, LANES), f32),
                pltpu.VMEM((8, wide, LANES), f32),
                pltpu.VMEM((8, wide, LANES), f32),
                pltpu.VMEM((2, wide, LANES), f32),
                pltpu.VMEM((2, wide, LANES), f32),
                pltpu.VMEM((PARTS, wide, LANES), f32),
                pltpu.VMEM((PARTS, wide, LANES), f32),
                pltpu.VMEM((8, 2 * wide, 2 * LANES), jnp.bfloat16),
                pltpu.VMEM((8, 2 * wide, LANES), f32),
                pltpu.VMEM((PARTS, PACKED, LANES), f32),
                pltpu.VMEM((PARTS, PACKED, LANES), f32),
                dma((7,)),
                dma((2,)),
                dma((2,)),
                dma((PARTS,)),
                dma((PARTS,)),
                dma((PARTS,)),
                dma((PARTS,)),
            ],
            compiler_params=pltpu.CompilerParams(collective_id=0, has_side_effects=True, vmem_limit_bytes=32 << 20),
        )(*(pltpu.with_memory_space_constraint(value, pltpu.HBM) for value in operands))
        return jnp.transpose(result, (1, 0, 2))

    return jax.shard_map(
        body,
        mesh=mesh,
        in_specs=(P("lat", "lon", None), P("lat"), P("lat")),
        out_specs=P("lat", "lon", None),
        check_vma=False,
    )
```

```python
import functools
import math

import jax
import jax.numpy as jnp
import numpy as np
from jax import lax
from jax.experimental import pallas as pl
from jax.experimental.pallas import tpu as pltpu
from jax.sharding import PartitionSpec as P

MESH = pl.DeviceIdType.MESH
PARTS = 16
LANES = 128
OPEN_CUT = 4096.0
PACKED = 72


def split_table(table):
    high = np.asarray(table, dtype=jnp.bfloat16)
    low = np.asarray(table - high.astype(np.float64), dtype=jnp.bfloat16)
    return high, low


def dft_tables(nlon, width, wide):
    points = np.full(wide, -10**6)
    points[:width] = np.arange(width)
    points[width] = width
    points[wide - 1] = -1
    used = points > -10**6
    forward = np.zeros((8, 2 * wide, 2 * wide))
    inverse = np.zeros((8, 2 * wide, 2 * wide))
    sines = np.zeros((8, wide))
    for group in range(8):
        for row in range(wide):
            if group:
                if row >= width:
                    continue
                wave = group + PARTS * row
                weight = 2.0 / nlon
            else:
                half = width // 2 + 1
                if row < half:
                    wave = PARTS * row
                elif row < width + 1:
                    wave = 8 + PARTS * (row - half)
                else:
                    continue
                weight = (1.0 if wave in (0, nlon // 2) else 2.0) / nlon
            phase = np.where(used, (points * wave) % nlon, 0) * (2.0 * math.pi / nlon)
            cos_vals = np.where(used, np.cos(phase), 0.0)
            sin_vals = np.where(used, np.sin(phase), 0.0)
            inner = np.arange(wide) < width
            if group:
                forward[group, row, :wide] = cos_vals
                forward[group, row, wide:] = -sin_vals
                forward[group, wide + row, :wide] = -sin_vals
                forward[group, wide + row, wide:] = -cos_vals
                inverse[group, :wide, row] = weight * cos_vals * inner
                inverse[group, :wide, wide + row] = -weight * sin_vals * inner
                inverse[group, wide:, row] = weight * sin_vals * inner
                inverse[group, wide:, wide + row] = weight * cos_vals * inner
            else:
                base = 0 if row < half else wide
                part = slice(base, base + wide)
                forward[0, row, part] = cos_vals
                forward[0, wide + row, part] = -sin_vals
                inverse[0, part, row] = weight * cos_vals * inner
                inverse[0, part, wide + row] = -weight * sin_vals * inner
            sines[group, row] = math.sin(2.0 * math.pi * wave / nlon)
    waves = np.zeros((wide, LANES), np.float32)
    waves[:, :8] = sines.T
    return np.concatenate(split_table(np.concatenate([forward, inverse])), axis=1), waves


def coef_table(nlat, bands):
    rows = nlat // bands
    index = np.arange(-1, nlat + 1).astype(np.float32)
    angle = np.float32(-0.5 * math.pi) + (index + np.float32(0.5)) * np.float32(math.pi) / np.float32(nlat)
    cosine = np.cos(angle.astype(np.float64)).astype(np.float32).astype(np.float64)
    flux = cosine.copy()
    flux[0] = 0.0
    flux[-1] = 0.0
    table = np.zeros((bands, 16, LANES))
    for band in range(bands):
        at = band * rows + 1
        for row in range(rows):
            table[band, row] = 0.015 / cosine[at + row]
        for pair in range(rows // 2):
            even = at + 2 * pair
            odd = even + 1
            lane = np.zeros(8)
            lane[0] = 0.03 / cosine[even]
            lane[1] = 0.03 / cosine[odd]
            lane[4] = -0.015 * flux[odd] / cosine[even]
            lane[5] = 0.015 * flux[even] / cosine[odd]
            lane[6] = 0.015 * flux[even - 1] / cosine[even]
            lane[7] = -0.015 * flux[odd + 1] / cosine[odd]
            table[band, 8 + pair] = np.repeat(lane, 16)
    return table.astype(np.float32)


def wave_sum(terms):
    total = None
    for factor, value in terms:
        if abs(factor) < 1e-9:
            continue
        if abs(abs(factor) - 1.0) < 1e-9:
            if total is None:
                total = value if factor > 0 else -value
            else:
                total = total + value if factor > 0 else total - value
        else:
            part = value * np.float32(factor)
            total = part if total is None else total + part
    return total


def half_dft(even_in, odd_in):
    unit = 2.0 * math.pi / PARTS
    sums = [even_in[0] + even_in[8]] + [even_in[a] + even_in[8 - a] for a in (1, 2, 3)] + [even_in[4]]
    diffs = [even_in[0] - even_in[8]] + [even_in[a] - even_in[8 - a] for a in (1, 2, 3)]
    odd_sums = [None] + [odd_in[a] + odd_in[8 - a] for a in (1, 2, 3)] + [odd_in[4]]
    odd_diffs = [None] + [odd_in[a] - odd_in[8 - a] for a in (1, 2, 3)]
    cos_out = []
    sin_out = []
    for k in range(9):
        parts = diffs if k % 2 else sums
        cos_out.append(wave_sum([(math.cos(unit * a * k), parts[a]) for a in range(len(parts))]))
        parts = odd_sums if k % 2 else odd_diffs
        sin_out.append(wave_sum([(math.sin(unit * a * k), parts[a]) for a in range(1, len(parts))]))
    return cos_out, sin_out


def split_value(value):
    high = value.astype(jnp.bfloat16)
    low = (value - high.astype(jnp.float32)).astype(jnp.bfloat16)
    return jnp.concatenate([high, low], axis=1)


def table_dot(table, pair):
    both = jnp.dot(table, pair, preferred_element_type=jnp.float32)
    half = table.shape[0] // 2
    return both[:half, :LANES] + both[:half, LANES:] + both[half:, :LANES]


def kernel(
    bands,
    state_hbm, flag_hbm, cut_hbm, coef_hbm, table_hbm, wave_hbm,
    result,
    state, flag_ref, cut_ref, winds, press, slopes, cuts, coef, table, waves, damps, turns,
    halo_out, halo_in, send, recv, spectra, fields, bsend, brecv,
    load_sem, halo_send, halo_recv, send_sem, recv_sem, bsend_sem, brecv_sem,
):
    lat = lax.axis_index("lat")
    lon = lax.axis_index("lon")
    width, rows = state_hbm.shape[0], state_hbm.shape[1]
    wide = recv.shape[1]
    spare = jnp.zeros((wide - width, LANES), jnp.float32)

    def field(row, part):
        return jnp.concatenate([state[:, row, pl.ds(part * LANES, LANES)], spare], axis=0)

    above = jnp.maximum(lat - 1, 0)
    below = jnp.minimum(lat + 1, bands - 1)
    sides = (lat > 0, lat < bands - 1)
    greeted = jnp.where(lat > 0, 1, 0) + jnp.where(lat < bands - 1, 1, 0)
    odd = lax.rem(lat, 2)
    chip = lon // 2
    core = lon % 2

    def state_copy(part):
        spans = pl.ds(part * LANES, LANES)
        return pltpu.make_async_copy(state_hbm.at[:, :, spans], state.at[:, :, spans], load_sem.at[part])

    loads = [state_copy(1), state_copy(0)]
    loads.append(pltpu.make_async_copy(coef_hbm.at[lat], coef, load_sem.at[2]))
    loads.append(pltpu.make_async_copy(flag_hbm, flag_ref, load_sem.at[3]))
    loads.append(pltpu.make_async_copy(cut_hbm, cut_ref, load_sem.at[4]))
    tables = ((wave_hbm, waves), (table_hbm, table))
    for at, (source, target) in enumerate(tables):
        loads.append(pltpu.make_async_copy(source, target, load_sem.at[5 + at]))
    for load in loads[:5]:
        load.start()

    barrier = pltpu.get_barrier_semaphore()
    for offset in range(1, PARTS):
        pl.semaphore_signal(barrier, inc=1, device_id=(lat, lax.rem(lon + offset, PARTS)), device_id_type=MESH)

    lane = lax.broadcasted_iota(jnp.int32, (wide, LANES), 1)
    line = lax.broadcasted_iota(jnp.int32, (wide, LANES), 0)
    first = lane < 64
    block = (lane // 16) % 4
    loads[0].wait()
    for row in range(rows):
        right = field(row, 1)
        turned = pltpu.roll(right, 64, 1)
        step = jnp.where(lane < 63, pltpu.roll(turned, LANES - 1, 1), 0.0) - jnp.where(lane > 0, pltpu.roll(turned, 1, 1), 0.0)
        vert = right - 0.1 * step
        step = jnp.where(lane < 63, pltpu.roll(vert, LANES - 1, 1), 0.0) - jnp.where(lane > 0, pltpu.roll(vert, 1, 1), 0.0)
        press[row] = turned - 0.015 * step
        result[:, row, pl.ds(LANES, LANES)] = vert[:width]
        slopes[row] = pltpu.roll(turned, wide - 1, 0) - pltpu.roll(turned, 1, 0)
    for load in loads[1:3]:
        load.wait()

    def prepare(row):
        left = field(row, 0)
        zonal = left - coef[pl.ds(row, 1), :] * slopes[row]
        merid = left
        if row < rows - 1:
            merid = merid - 0.015 * field(row + 1, 1)
        if row > 0:
            merid = merid + 0.015 * field(row - 1, 1)
        winds[row + 1] = jnp.where(first, zonal, merid)

    def pack(pair, slot):
        even = 2 * pair + 1
        sources = (
            jnp.where(first, winds[even], winds[even + 1]),
            jnp.where(first, winds[even + 1], winds[even]),
            jnp.where(first, press[even - 1], winds[even - 1]),
            jnp.where(first, press[even], winds[even + 2]),
        )
        for quarter in range(4):
            chunk = sources[quarter]
            for at in range(4):
                if at != quarter:
                    chunk = jnp.where(block == at, pltpu.roll(sources[at], (16 * (at - quarter)) % LANES, 1), chunk)
            send[slot + 2 * quarter] = chunk

    halos = []
    for side, device in ((0, above), (1, below)):
        halos.append(
            pltpu.make_async_remote_copy(
                src_ref=halo_out.at[side],
                dst_ref=halo_in.at[1 - side],
                send_sem=halo_send.at[side],
                recv_sem=halo_recv.at[1 - side],
                device_id=(device, lon),
                device_id_type=MESH,
            )
        )
    def forward_copy(source, slot, device):
        return pltpu.make_async_remote_copy(
            src_ref=send.at[source],
            dst_ref=recv.at[slot],
            send_sem=send_sem.at[source],
            recv_sem=recv_sem.at[slot],
            device_id=(lat, device),
            device_id_type=MESH,
        )

    def backward_copy(source, slot, device):
        return pltpu.make_async_remote_copy(
            src_ref=bsend.at[source],
            dst_ref=brecv.at[slot],
            send_sem=bsend_sem.at[source],
            recv_sem=brecv_sem.at[slot],
            device_id=(lat, device),
            device_id_type=MESH,
        )

    order = (4, 3, 5, 2, 6, 1, 7, 0)

    def send_to(copy, kind):
        for offset in order:
            target = 2 * lax.rem(chip + offset, 8) + kind
            if offset:
                copy(target, lon, target).start()
            else:
                @pl.when(core != kind)
                def _():
                    copy(target, lon, target).start()

    def pack_and_send(pair, at, kind):
        pack(pair, 8 * at + kind)
        if pair == 1:
            pl.semaphore_wait(barrier, PARTS - 1 + odd * greeted)
            for present, device in zip(sides, (above, below)):
                @pl.when(present)
                def _():
                    pl.semaphore_signal(barrier, inc=1, device_id=(device, lon), device_id_type=MESH)
        for offset in range(4):
            target = 8 * at + 2 * lax.rem(chip + offset, 4) + kind

            @pl.when(target != lon)
            def _():
                forward_copy(target, lon, target).start()

    for row in range(1, 5):
        prepare(row)
    pack_and_send(1, 0, 0)
    for row in range(5, 7):
        prepare(row)
    pack_and_send(2, 1, 0)
    prepare(0)
    prepare(rows - 1)
    for load in loads[3:5]:
        load.wait()
    for load in loads[5:]:
        load.start()
    for row in range(rows):
        kept = jnp.full((1, LANES), cut_ref[row], jnp.int32).astype(jnp.float32)
        flag = jnp.full((1, LANES), flag_ref[row], jnp.int32)
        cuts[pl.ds(row + 1, 1), :] = jnp.where(flag == 1, kept, OPEN_CUT)
    for side, row in ((0, 0), (1, rows - 1)):
        turned = pltpu.roll(field(row, 1), 64, 1)
        message = jnp.where(first, turned, winds[row + 1])
        halo_out[side] = jnp.where(line == width, cuts[pl.ds(row + 1, 1), :], message)

    @pl.when(odd == 0)
    def _():
        pl.semaphore_wait(barrier, greeted)

    for side in range(2):
        pl.when(sides[side])(halos[side].start)

    for side in range(2):
        pl.when(sides[1 - side])(halos[side].wait_recv)

        @pl.when(jnp.logical_not(sides[side]))
        def _():
            halo_in[side] = jnp.zeros((wide, LANES), jnp.float32)

    inside = jnp.where(lat > 0, 0.015, 0.0)
    upper = halo_in[0]
    cuts[pl.ds(0, 1), :] = upper[width : width + 1]
    winds[0] = jnp.where(line < width, upper - 0.015 * field(0, 1), 0.0)
    winds[1] = winds[1] + jnp.where(first | (line >= width), 0.0, inside * pltpu.roll(upper, 64, 1))
    inside = jnp.where(lat < bands - 1, 0.015, 0.0)
    lower = halo_in[1]
    cuts[pl.ds(rows + 1, 1), :] = lower[width : width + 1]
    winds[rows + 1] = jnp.where(line < width, lower + 0.015 * field(rows - 1, 1), 0.0)
    winds[rows] = winds[rows] - jnp.where(first | (line >= width), 0.0, inside * pltpu.roll(lower, 64, 1))

    pack_and_send(0, 0, 1)
    pack_and_send(3, 1, 1)
    recv[lon] = send[lon]

    half = chip // 4
    mine = (1 - core) * (1 + half) + core * 3 * half
    lanes = lax.broadcasted_iota(jnp.int32, (1, LANES), 1) // 16
    cut_even = cuts[pl.ds(2 * mine + 1, 1), :]
    cut_odd = cuts[pl.ds(2 * mine + 2, 1), :]
    limit = jnp.where((lanes == 0) | (lanes == 2) | (lanes == 5), cut_even, cut_odd)
    limit = jnp.where(lanes == 6, cuts[pl.ds(2 * mine, 1), :], limit)
    limit = jnp.where(lanes == 7, cuts[pl.ds(2 * mine + 3, 1), :], limit)
    factor = coef[pl.ds(8 + mine, 1), :]
    loads[5].wait()

    for group in range(8):
        wave = PARTS * line + group
        if group:
            wave = jnp.minimum(wave, PARTS * width - wave)
        else:
            wave = jnp.where(line <= width // 2, wave, PARTS * (line - width // 2 - 1) + 8)
        ratio = limit / jnp.maximum(wave, 1).astype(jnp.float32)
        damps[group] = jnp.minimum(1.0, ratio * ratio)
        turns[group] = factor * waves[:, group : group + 1]
    for load in loads[6:]:
        load.wait()

    def receive(offset, carry):
        source = lax.rem(lon + offset, PARTS)
        forward_copy(source, source, source).wait_recv()
        return carry

    lax.fori_loop(1, PARTS, receive, 0)

    def gather_waves(at, carry):
        where = pl.multiple_of(16 * at, 16)
        spans = pl.ds(where, 16)
        images = pl.ds(pl.multiple_of(wide + where, 16), 16)
        values = [recv[a, spans, :] for a in range(PARTS)]
        evens = [values[0]] + [values[a] + values[PARTS - a] for a in range(1, 8)] + [values[8]]
        odds = [None] + [values[a] - values[PARTS - a] for a in range(1, 8)]
        cos_out, sin_out = half_dft(evens, odds)
        spectra[0, spans, :] = split_value(cos_out[0])
        spectra[0, images, :] = split_value(cos_out[8])
        for k in range(1, 8):
            spectra[k, spans, :] = split_value(cos_out[k])
            spectra[k, images, :] = split_value(sin_out[k])
        return carry

    lax.fori_loop(0, wide // 16, gather_waves, 0, unroll=6)

    def transform(group, carry):
        values = table_dot(table[group], spectra[group])
        damping = damps[group]
        real = values[:wide] * damping
        imag = values[wide:] * damping
        turn = turns[group]
        zonal = lane < 32
        lift_real = jnp.where(zonal, turn * imag, factor * real)
        lift_imag = jnp.where(zonal, -turn * real, factor * imag)
        inner = (lane >= 32) & first
        outs = []
        for value, lift in ((real, lift_real), (imag, lift_imag)):
            total = pltpu.roll(lift, 32, 1) + pltpu.roll(lift, 96, 1) + pltpu.roll(lift, 64, 1)
            outs.append(jnp.where(inner, value + damping * total, value))
        both = split_value(jnp.concatenate(outs, axis=0))
        fields[group] = table_dot(table[8 + group], both)
        return carry

    lax.fori_loop(0, 8, transform, 0, unroll=8)

    def scatter_waves(at, carry):
        where = pl.multiple_of(16 * at, 16)
        spans = pl.ds(where, 16)
        images = pl.ds(pl.multiple_of(wide + where, 16), 16)
        evens = [fields[0, spans, :]] + [fields[k, spans, :] for k in range(1, 8)] + [fields[0, images, :]]
        odds = [None] + [fields[k, images, :] for k in range(1, 8)]
        cos_out, sin_out = half_dft(evens, odds)
        circles[0, spans, :] = cos_out[0]
        circles[8, spans, :] = cos_out[8]
        for a in range(1, 8):
            circles[a, spans, :] = cos_out[a] - sin_out[a]
            circles[PARTS - a, spans, :] = cos_out[a] + sin_out[a]
        return carry

    circles = recv
    lax.fori_loop(0, wide // 16, scatter_waves, 0, unroll=6)
    narrow = lax.broadcasted_iota(jnp.int32, (24, LANES), 1)

    def pack_back(a, carry):
        rest = circles[a, pl.ds(72, 24), :]
        for at in range(3):
            spans = pl.ds(24 * at, 24)
            bsend[a, spans, :] = jnp.where(narrow < 96, circles[a, spans, :], pltpu.roll(rest, 96 - 32 * at, 1))
        return carry

    lax.fori_loop(0, PARTS, pack_back, 0, unroll=PARTS)
    send_to(backward_copy, 1)
    send_to(backward_copy, 0)
    brecv[lon] = bsend[lon]

    def unpack(pair, slot):
        chunks = []
        for quarter in range(4):
            source = slot + 2 * quarter

            @pl.when(source != lon)
            def _():
                backward_copy(source, source, source).wait_recv()

            pieces = [brecv[source, pl.ds(24 * at, 24), :] for at in range(3)]
            rest = jnp.where(narrow < 32, pltpu.roll(pieces[0], 32, 1), pltpu.roll(pieces[1], 64, 1))
            rest = jnp.where(narrow < 64, rest, pltpu.roll(pieces[2], 96, 1))
            chunks.append(jnp.concatenate(pieces + [rest], axis=0))
        parts = []
        for at in range(4):
            shift = 64 if at >= 2 else 0
            part = None
            for quarter in range(4):
                amount = (16 * (quarter - at) + shift) % LANES
                moved = pltpu.roll(chunks[quarter], amount, 1) if amount else chunks[quarter]
                part = moved if part is None else jnp.where(block == quarter, moved, part)
            parts.append(part)
        even = 2 * pair
        spans = pl.ds(0, LANES)
        result[:, even, spans] = jnp.where(first, parts[0], parts[1])[:width]
        result[:, even + 1, spans] = jnp.where(first, parts[1], parts[0])[:width]
        spans = pl.ds(LANES, LANES)
        result[:, even, spans] = jnp.where(first[:width], result[:, even, spans], parts[2][:width])
        result[:, even + 1, spans] = jnp.where(first[:width], result[:, even + 1, spans], parts[3][:width])

    for at in range(2):
        unpack(1 + at, 8 * at)
    for at in range(2):
        unpack(3 * at, 8 * at + 1)

    def finish(offset, carry):
        target = lax.rem(lon + offset, PARTS)
        forward_copy(target, lon, target).wait_send()
        backward_copy(target, lon, target).wait_send()
        return carry

    lax.fori_loop(1, PARTS, finish, 0)
    for side in range(2):
        pl.when(sides[side])(halos[side].wait_send)


def solution(mesh):
    bands = mesh.shape["lat"]

    def body(state, filter_flag, cutoff):
        rows, width, depth = state.shape
        wide = (width + 2 + 15) // 16 * 16
        tables = dft_tables(width * PARTS, width, wide)
        coefs = coef_table(rows * bands, bands)
        f32 = jnp.float32
        table = pltpu.VMEM((16, 4 * wide, 2 * wide), jnp.bfloat16)
        hbm_spec = pl.BlockSpec(memory_space=pltpu.HBM)
        dma = pltpu.SemaphoreType.DMA
        operands = (jnp.transpose(state, (1, 0, 2)), filter_flag, cutoff) + tuple(map(jnp.asarray, (coefs,) + tables))
        result = pl.pallas_call(
            functools.partial(kernel, bands),
            out_shape=jax.ShapeDtypeStruct((width, rows, depth), f32),
            in_specs=[hbm_spec] * 6,
            out_specs=pl.BlockSpec(memory_space=pltpu.VMEM),
            scratch_shapes=[
                pltpu.VMEM((width, rows, depth), f32),
                pltpu.SMEM((rows,), jnp.int32),
                pltpu.SMEM((rows,), jnp.int32),
                pltpu.VMEM((rows + 2, wide, LANES), f32),
                pltpu.VMEM((rows, wide, LANES), f32),
                pltpu.VMEM((rows, wide, LANES), f32),
                pltpu.VMEM((16, LANES), f32),
                pltpu.VMEM((16, LANES), f32),
                table,
                pltpu.VMEM((wide, LANES), f32),
                pltpu.VMEM((8, wide, LANES), f32),
                pltpu.VMEM((8, wide, LANES), f32),
                pltpu.VMEM((2, wide, LANES), f32),
                pltpu.VMEM((2, wide, LANES), f32),
                pltpu.VMEM((PARTS, wide, LANES), f32),
                pltpu.VMEM((PARTS, wide, LANES), f32),
                pltpu.VMEM((8, 2 * wide, 2 * LANES), jnp.bfloat16),
                pltpu.VMEM((8, 2 * wide, LANES), f32),
                pltpu.VMEM((PARTS, PACKED, LANES), f32),
                pltpu.VMEM((PARTS, PACKED, LANES), f32),
                dma((7,)),
                dma((2,)),
                dma((2,)),
                dma((PARTS,)),
                dma((PARTS,)),
                dma((PARTS,)),
                dma((PARTS,)),
            ],
            compiler_params=pltpu.CompilerParams(collective_id=0, has_side_effects=True, vmem_limit_bytes=32 << 20),
        )(*(pltpu.with_memory_space_constraint(value, pltpu.HBM) for value in operands))
        return jnp.transpose(result, (1, 0, 2))

    return jax.shard_map(
        body,
        mesh=mesh,
        in_specs=(P("lat", "lon", None), P("lat"), P("lat")),
        out_specs=P("lat", "lon", None),
        check_vma=False,
    )
```

```python
import functools
import math

import jax
import jax.numpy as jnp
import numpy as np
from jax import lax
from jax.experimental import pallas as pl
from jax.experimental.pallas import tpu as pltpu
from jax.sharding import PartitionSpec as P

MESH = pl.DeviceIdType.MESH
PARTS = 16
LANES = 128
OPEN_CUT = 4096.0
DEPTH = 8
PACKED = 72


def split_table(table):
    high = np.asarray(table, dtype=jnp.bfloat16)
    low = np.asarray(table - high.astype(np.float64), dtype=jnp.bfloat16)
    return high, low


def dft_tables(nlon, width, wide):
    points = np.full(wide, -10**6)
    points[:width] = np.arange(width)
    points[width] = width
    points[wide - 1] = -1
    used = points > -10**6
    forward = np.zeros((8, 2 * wide, 2 * wide))
    inverse = np.zeros((8, 2 * wide, 2 * wide))
    sines = np.zeros((8, wide))
    for group in range(8):
        for row in range(wide):
            if group:
                if row >= width:
                    continue
                wave = group + PARTS * row
                weight = 2.0 / nlon
            else:
                half = width // 2 + 1
                if row < half:
                    wave = PARTS * row
                elif row < width + 1:
                    wave = 8 + PARTS * (row - half)
                else:
                    continue
                weight = (1.0 if wave in (0, nlon // 2) else 2.0) / nlon
            phase = np.where(used, (points * wave) % nlon, 0) * (2.0 * math.pi / nlon)
            cos_vals = np.where(used, np.cos(phase), 0.0)
            sin_vals = np.where(used, np.sin(phase), 0.0)
            inner = np.arange(wide) < width
            if group:
                forward[group, row, :wide] = cos_vals
                forward[group, row, wide:] = -sin_vals
                forward[group, wide + row, :wide] = -sin_vals
                forward[group, wide + row, wide:] = -cos_vals
                inverse[group, :wide, row] = weight * cos_vals * inner
                inverse[group, :wide, wide + row] = -weight * sin_vals * inner
                inverse[group, wide:, row] = weight * sin_vals * inner
                inverse[group, wide:, wide + row] = weight * cos_vals * inner
            else:
                base = 0 if row < half else wide
                part = slice(base, base + wide)
                forward[0, row, part] = cos_vals
                forward[0, wide + row, part] = -sin_vals
                inverse[0, part, row] = weight * cos_vals * inner
                inverse[0, part, wide + row] = -weight * sin_vals * inner
            sines[group, row] = math.sin(2.0 * math.pi * wave / nlon)
    waves = np.zeros((wide, LANES), np.float32)
    waves[:, :8] = sines.T
    return np.concatenate(split_table(np.concatenate([forward, inverse])), axis=1), waves


def coef_table(nlat, bands):
    rows = nlat // bands
    index = np.arange(-1, nlat + 1).astype(np.float32)
    angle = np.float32(-0.5 * math.pi) + (index + np.float32(0.5)) * np.float32(math.pi) / np.float32(nlat)
    cosine = np.cos(angle.astype(np.float64)).astype(np.float32).astype(np.float64)
    flux = cosine.copy()
    flux[0] = 0.0
    flux[-1] = 0.0
    table = np.zeros((bands, 16, LANES))
    for band in range(bands):
        at = band * rows + 1
        for row in range(rows):
            table[band, row] = 0.015 / cosine[at + row]
        for pair in range(rows // 2):
            even = at + 2 * pair
            odd = even + 1
            lane = np.zeros(8)
            lane[0] = 0.03 / cosine[even]
            lane[1] = 0.03 / cosine[odd]
            lane[4] = -0.015 * flux[odd] / cosine[even]
            lane[5] = 0.015 * flux[even] / cosine[odd]
            lane[6] = 0.015 * flux[even - 1] / cosine[even]
            lane[7] = -0.015 * flux[odd + 1] / cosine[odd]
            table[band, 8 + pair] = np.repeat(lane, 16)
    return table.astype(np.float32)


def wave_sum(terms):
    total = None
    for factor, value in terms:
        if abs(factor) < 1e-9:
            continue
        if abs(abs(factor) - 1.0) < 1e-9:
            if total is None:
                total = value if factor > 0 else -value
            else:
                total = total + value if factor > 0 else total - value
        else:
            part = value * np.float32(factor)
            total = part if total is None else total + part
    return total


def half_dft(even_in, odd_in):
    unit = 2.0 * math.pi / PARTS
    sums = [even_in[0] + even_in[8]] + [even_in[a] + even_in[8 - a] for a in (1, 2, 3)] + [even_in[4]]
    diffs = [even_in[0] - even_in[8]] + [even_in[a] - even_in[8 - a] for a in (1, 2, 3)]
    odd_sums = [None] + [odd_in[a] + odd_in[8 - a] for a in (1, 2, 3)] + [odd_in[4]]
    odd_diffs = [None] + [odd_in[a] - odd_in[8 - a] for a in (1, 2, 3)]
    cos_out = []
    sin_out = []
    for k in range(9):
        parts = diffs if k % 2 else sums
        cos_out.append(wave_sum([(math.cos(unit * a * k), parts[a]) for a in range(len(parts))]))
        parts = odd_sums if k % 2 else odd_diffs
        sin_out.append(wave_sum([(math.sin(unit * a * k), parts[a]) for a in range(1, len(parts))]))
    return cos_out, sin_out


def split_value(value):
    high = value.astype(jnp.bfloat16)
    low = (value - high.astype(jnp.float32)).astype(jnp.bfloat16)
    return jnp.concatenate([high, low], axis=1)


def table_dot(table, pair):
    both = jnp.dot(table, pair, preferred_element_type=jnp.float32)
    half = table.shape[0] // 2
    return both[:half, :LANES] + both[:half, LANES:] + both[half:, :LANES]


def kernel(
    bands,
    state_hbm, flag_hbm, cut_hbm, coef_hbm, table_hbm, wave_hbm,
    result,
    state, flag_ref, cut_ref, winds, press, slopes, cuts, coef, table, waves, damps, turns,
    halo_out, halo_in, send, recv, spectra, fields, bsend, brecv,
    hello, load_sem, halo_send, halo_recv, send_sem, recv_sem, bsend_sem, brecv_sem,
):
    lat = lax.axis_index("lat")
    lon = lax.axis_index("lon")
    width, rows = state_hbm.shape[0], state_hbm.shape[1]
    wide = recv.shape[1]
    spare = jnp.zeros((wide - width, LANES), jnp.float32)

    def field(row, part):
        return jnp.concatenate([state[:, row, pl.ds(part * LANES, LANES)], spare], axis=0)

    above = jnp.maximum(lat - 1, 0)
    below = jnp.minimum(lat + 1, bands - 1)
    sides = (lat > 0, lat < bands - 1)
    place = lax.rem(lat, DEPTH)
    paired = (place != 0, place != DEPTH - 1)
    opening = (place == 0) & sides[0]
    closing = (place == DEPTH - 1) & sides[1]
    known = jnp.where(paired[0], 1, 0) + jnp.where(sides[1], 1, 0)
    chip = lon // 2
    core = lon % 2

    def state_copy(part):
        spans = pl.ds(part * LANES, LANES)
        return pltpu.make_async_copy(state_hbm.at[:, :, spans], state.at[:, :, spans], load_sem.at[part])

    loads = [state_copy(1), state_copy(0)]
    loads.append(pltpu.make_async_copy(coef_hbm.at[lat], coef, load_sem.at[2]))
    loads.append(pltpu.make_async_copy(flag_hbm, flag_ref, load_sem.at[3]))
    loads.append(pltpu.make_async_copy(cut_hbm, cut_ref, load_sem.at[4]))
    tables = ((wave_hbm, waves), (table_hbm, table))
    for at, (source, target) in enumerate(tables):
        loads.append(pltpu.make_async_copy(source, target, load_sem.at[5 + at]))
    for load in loads[:5]:
        load.start()

    barrier = pltpu.get_barrier_semaphore()
    for offset in range(1, PARTS):
        pl.semaphore_signal(barrier, inc=1, device_id=(lat, lax.rem(lon + offset, PARTS)), device_id_type=MESH)

    for side, device in ((0, above), (1, below)):
        @pl.when(paired[side])
        def _():
            pl.semaphore_signal(barrier, inc=1, device_id=(device, lon), device_id_type=MESH)

    lane = lax.broadcasted_iota(jnp.int32, (wide, LANES), 1)
    line = lax.broadcasted_iota(jnp.int32, (wide, LANES), 0)
    first = lane < 64
    block = (lane // 16) % 4
    loads[0].wait()
    for row in range(rows):
        right = field(row, 1)
        turned = pltpu.roll(right, 64, 1)
        step = jnp.where(lane < 63, pltpu.roll(turned, LANES - 1, 1), 0.0) - jnp.where(lane > 0, pltpu.roll(turned, 1, 1), 0.0)
        vert = right - 0.1 * step
        step = jnp.where(lane < 63, pltpu.roll(vert, LANES - 1, 1), 0.0) - jnp.where(lane > 0, pltpu.roll(vert, 1, 1), 0.0)
        press[row] = turned - 0.015 * step
        result[:, row, pl.ds(LANES, LANES)] = vert[:width]
        slopes[row] = pltpu.roll(turned, wide - 1, 0) - pltpu.roll(turned, 1, 0)
    for load in loads[1:3]:
        load.wait()

    def prepare(row):
        left = field(row, 0)
        zonal = left - coef[pl.ds(row, 1), :] * slopes[row]
        merid = left
        if row < rows - 1:
            merid = merid - 0.015 * field(row + 1, 1)
        if row > 0:
            merid = merid + 0.015 * field(row - 1, 1)
        winds[row + 1] = jnp.where(first, zonal, merid)

    def pack(pair, slot):
        even = 2 * pair + 1
        sources = (
            jnp.where(first, winds[even], winds[even + 1]),
            jnp.where(first, winds[even + 1], winds[even]),
            jnp.where(first, press[even - 1], winds[even - 1]),
            jnp.where(first, press[even], winds[even + 2]),
        )
        for quarter in range(4):
            chunk = sources[quarter]
            for at in range(4):
                if at != quarter:
                    chunk = jnp.where(block == at, pltpu.roll(sources[at], (16 * (at - quarter)) % LANES, 1), chunk)
            send[slot + 4 * quarter] = chunk

    def halo_copy(side, slot, device):
        return pltpu.make_async_remote_copy(
            src_ref=halo_out.at[side],
            dst_ref=halo_in.at[slot],
            send_sem=halo_send.at[side],
            recv_sem=halo_recv.at[slot],
            device_id=(device, lon),
            device_id_type=MESH,
        )

    halos = [halo_copy(0, 1, above), halo_copy(1, 0, below)]

    def forward_copy(source, slot, device):
        return pltpu.make_async_remote_copy(
            src_ref=send.at[source],
            dst_ref=recv.at[slot],
            send_sem=send_sem.at[source],
            recv_sem=recv_sem.at[slot],
            device_id=(lat, device),
            device_id_type=MESH,
        )

    def backward_copy(source, slot, device):
        return pltpu.make_async_remote_copy(
            src_ref=bsend.at[source],
            dst_ref=brecv.at[slot],
            send_sem=bsend_sem.at[source],
            recv_sem=brecv_sem.at[slot],
            device_id=(lat, device),
            device_id_type=MESH,
        )

    order = (4, 3, 5, 2, 6, 1, 7, 0)

    def send_to(copy, kind):
        for offset in order:
            target = 2 * lax.rem(chip + offset, 8) + kind
            if offset:
                copy(target, lon, target).start()
            else:
                @pl.when(core != kind)
                def _():
                    copy(target, lon, target).start()

    def pack_and_send(pair, at, kind):
        pack(pair, 2 * at + kind)
        for offset in (2, 1, 3, 0):
            target = 2 * at + 4 * lax.rem(chip // 2 + offset, 4) + kind

            @pl.when(target != lon)
            def _():
                forward_copy(target, lon, target).start()

    prepare(0)
    prepare(rows - 1)
    for load in loads[3:5]:
        load.wait()
    for row in range(rows):
        kept = jnp.full((1, LANES), cut_ref[row], jnp.int32).astype(jnp.float32)
        flag = jnp.full((1, LANES), flag_ref[row], jnp.int32)
        cuts[pl.ds(row + 1, 1), :] = jnp.where(flag == 1, kept, OPEN_CUT)
    for side, row in ((0, 0), (1, rows - 1)):
        turned = pltpu.roll(field(row, 1), 64, 1)
        message = jnp.where(first, turned, winds[row + 1])
        halo_out[side] = jnp.where(line == width, cuts[pl.ds(row + 1, 1), :], message)
    for row in range(1, 5):
        prepare(row)

    pl.semaphore_wait(barrier, PARTS - 1 + known)
    pl.when(paired[0])(halos[0].start)
    pl.when(sides[1])(halos[1].start)

    @pl.when(opening)
    def _():
        pl.semaphore_signal(barrier, inc=1, device_id=(above, lon), device_id_type=MESH)

    @pl.when(closing)
    def _():
        pl.semaphore_signal(hello.at[0], inc=1, device_id=(below, lon), device_id_type=MESH)

    pack_and_send(1, 0, 0)
    for load in loads[5:]:
        load.start()
    for row in range(5, 7):
        prepare(row)
    pack_and_send(2, 1, 0)

    flip = jnp.where((place == 0) | (place == DEPTH - 1), 1, 0)
    for step in range(2):
        side = flip if step == 0 else 1 - flip
        present = jnp.where(side == 0, lat, bands - 1 - lat) > 0

        @pl.when(present)
        def _():
            halo_copy(1 - side, side, above).wait_recv()

        @pl.when(jnp.logical_not(present))
        def _():
            halo_in[side] = jnp.zeros((wide, LANES), jnp.float32)

        outer = jnp.where(side == 0, 0, rows + 1)
        inner = jnp.where(side == 0, 1, rows)
        slope = jnp.where(side == 0, 0.015, -0.015)
        inside = jnp.where(present, slope, 0.0)
        arrived = halo_in[side]
        cuts[pl.ds(outer, 1), :] = arrived[width : width + 1]
        winds[outer] = jnp.where(line < width, arrived - slope * pltpu.roll(halo_out[side], 64, 1), 0.0)
        winds[inner] = winds[inner] + jnp.where(first | (line >= width), 0.0, inside * pltpu.roll(arrived, 64, 1))
        pack_and_send(3 * side, side, 1)
        if step == 0:
            @pl.when(opening)
            def _():
                pl.semaphore_wait(hello.at[0], 1)
                halos[0].start()

    recv[lon] = send[lon]

    half = chip % 2
    mine = (1 - core) * (1 + half) + core * 3 * half
    lanes = lax.broadcasted_iota(jnp.int32, (1, LANES), 1) // 16
    cut_even = cuts[pl.ds(2 * mine + 1, 1), :]
    cut_odd = cuts[pl.ds(2 * mine + 2, 1), :]
    limit = jnp.where((lanes == 0) | (lanes == 2) | (lanes == 5), cut_even, cut_odd)
    limit = jnp.where(lanes == 6, cuts[pl.ds(2 * mine, 1), :], limit)
    limit = jnp.where(lanes == 7, cuts[pl.ds(2 * mine + 3, 1), :], limit)
    factor = coef[pl.ds(8 + mine, 1), :]
    loads[5].wait()

    for group in range(8):
        wave = PARTS * line + group
        if group:
            wave = jnp.minimum(wave, PARTS * width - wave)
        else:
            wave = jnp.where(line <= width // 2, wave, PARTS * (line - width // 2 - 1) + 8)
        ratio = limit / jnp.maximum(wave, 1).astype(jnp.float32)
        damps[group] = jnp.minimum(1.0, ratio * ratio)
        turns[group] = factor * waves[:, group : group + 1]
    for load in loads[6:]:
        load.wait()

    def receive(offset, carry):
        source = lax.rem(lon + offset, PARTS)
        forward_copy(source, source, source).wait_recv()
        return carry

    lax.fori_loop(1, PARTS, receive, 0)

    def gather_waves(at, carry):
        where = pl.multiple_of(16 * at, 16)
        spans = pl.ds(where, 16)
        images = pl.ds(pl.multiple_of(wide + where, 16), 16)
        values = [recv[a, spans, :] for a in range(PARTS)]
        evens = [values[0]] + [values[a] + values[PARTS - a] for a in range(1, 8)] + [values[8]]
        odds = [None] + [values[a] - values[PARTS - a] for a in range(1, 8)]
        cos_out, sin_out = half_dft(evens, odds)
        spectra[0, spans, :] = split_value(cos_out[0])
        spectra[0, images, :] = split_value(cos_out[8])
        for k in range(1, 8):
            spectra[k, spans, :] = split_value(cos_out[k])
            spectra[k, images, :] = split_value(sin_out[k])
        return carry

    lax.fori_loop(0, wide // 16, gather_waves, 0, unroll=6)

    def transform(group, carry):
        values = table_dot(table[group], spectra[group])
        damping = damps[group]
        real = values[:wide] * damping
        imag = values[wide:] * damping
        turn = turns[group]
        zonal = lane < 32
        lift_real = jnp.where(zonal, turn * imag, factor * real)
        lift_imag = jnp.where(zonal, -turn * real, factor * imag)
        inner = (lane >= 32) & first
        outs = []
        for value, lift in ((real, lift_real), (imag, lift_imag)):
            total = pltpu.roll(lift, 32, 1) + pltpu.roll(lift, 96, 1) + pltpu.roll(lift, 64, 1)
            outs.append(jnp.where(inner, value + damping * total, value))
        both = split_value(jnp.concatenate(outs, axis=0))
        fields[group] = table_dot(table[8 + group], both)
        return carry

    lax.fori_loop(0, 8, transform, 0, unroll=8)

    def scatter_waves(at, carry):
        where = pl.multiple_of(16 * at, 16)
        spans = pl.ds(where, 16)
        images = pl.ds(pl.multiple_of(wide + where, 16), 16)
        evens = [fields[0, spans, :]] + [fields[k, spans, :] for k in range(1, 8)] + [fields[0, images, :]]
        odds = [None] + [fields[k, images, :] for k in range(1, 8)]
        cos_out, sin_out = half_dft(evens, odds)
        circles[0, spans, :] = cos_out[0]
        circles[8, spans, :] = cos_out[8]
        for a in range(1, 8):
            circles[a, spans, :] = cos_out[a] - sin_out[a]
            circles[PARTS - a, spans, :] = cos_out[a] + sin_out[a]
        return carry

    circles = recv
    lax.fori_loop(0, wide // 16, scatter_waves, 0, unroll=6)
    narrow = lax.broadcasted_iota(jnp.int32, (24, LANES), 1)

    def pack_back(a, carry):
        rest = circles[a, pl.ds(72, 24), :]
        for at in range(3):
            spans = pl.ds(24 * at, 24)
            bsend[a, spans, :] = jnp.where(narrow < 96, circles[a, spans, :], pltpu.roll(rest, 96 - 32 * at, 1))
        return carry

    lax.fori_loop(0, PARTS, pack_back, 0, unroll=PARTS)
    send_to(backward_copy, 1)
    send_to(backward_copy, 0)
    brecv[lon] = bsend[lon]

    def unpack(pair, slot):
        chunks = []
        for quarter in range(4):
            source = slot + 4 * quarter

            @pl.when(source != lon)
            def _():
                backward_copy(source, source, source).wait_recv()

            pieces = [brecv[source, pl.ds(24 * at, 24), :] for at in range(3)]
            rest = jnp.where(narrow < 32, pltpu.roll(pieces[0], 32, 1), pltpu.roll(pieces[1], 64, 1))
            rest = jnp.where(narrow < 64, rest, pltpu.roll(pieces[2], 96, 1))
            chunks.append(jnp.concatenate(pieces + [rest], axis=0))
        parts = []
        for at in range(4):
            shift = 64 if at >= 2 else 0
            part = None
            for quarter in range(4):
                amount = (16 * (quarter - at) + shift) % LANES
                moved = pltpu.roll(chunks[quarter], amount, 1) if amount else chunks[quarter]
                part = moved if part is None else jnp.where(block == quarter, moved, part)
            parts.append(part)
        even = 2 * pair
        spans = pl.ds(0, LANES)
        result[:, even, spans] = jnp.where(first, parts[0], parts[1])[:width]
        result[:, even + 1, spans] = jnp.where(first, parts[1], parts[0])[:width]
        spans = pl.ds(LANES, LANES)
        result[:, even, spans] = jnp.where(first[:width], result[:, even, spans], parts[2][:width])
        result[:, even + 1, spans] = jnp.where(first[:width], result[:, even + 1, spans], parts[3][:width])

    for at in range(2):
        unpack(1 + at, 2 * at)
    for at in range(2):
        unpack(3 * at, 2 * at + 1)

    def finish(offset, carry):
        target = lax.rem(lon + offset, PARTS)
        forward_copy(target, lon, target).wait_send()
        backward_copy(target, lon, target).wait_send()
        return carry

    lax.fori_loop(1, PARTS, finish, 0)
    for side in range(2):
        pl.when(sides[side])(halos[side].wait_send)


def solution(mesh):
    bands = mesh.shape["lat"]

    def body(state, filter_flag, cutoff):
        rows, width, depth = state.shape
        wide = (width + 2 + 15) // 16 * 16
        tables = dft_tables(width * PARTS, width, wide)
        coefs = coef_table(rows * bands, bands)
        f32 = jnp.float32
        table = pltpu.VMEM((16, 4 * wide, 2 * wide), jnp.bfloat16)
        hbm_spec = pl.BlockSpec(memory_space=pltpu.HBM)
        dma = pltpu.SemaphoreType.DMA
        operands = (jnp.transpose(state, (1, 0, 2)), filter_flag, cutoff) + tuple(map(jnp.asarray, (coefs,) + tables))
        result = pl.pallas_call(
            functools.partial(kernel, bands),
            out_shape=jax.ShapeDtypeStruct((width, rows, depth), f32),
            in_specs=[hbm_spec] * 6,
            out_specs=pl.BlockSpec(memory_space=pltpu.VMEM),
            scratch_shapes=[
                pltpu.VMEM((width, rows, depth), f32),
                pltpu.SMEM((rows,), jnp.int32),
                pltpu.SMEM((rows,), jnp.int32),
                pltpu.VMEM((rows + 2, wide, LANES), f32),
                pltpu.VMEM((rows, wide, LANES), f32),
                pltpu.VMEM((rows, wide, LANES), f32),
                pltpu.VMEM((16, LANES), f32),
                pltpu.VMEM((16, LANES), f32),
                table,
                pltpu.VMEM((wide, LANES), f32),
                pltpu.VMEM((8, wide, LANES), f32),
                pltpu.VMEM((8, wide, LANES), f32),
                pltpu.VMEM((2, wide, LANES), f32),
                pltpu.VMEM((2, wide, LANES), f32),
                pltpu.VMEM((PARTS, wide, LANES), f32),
                pltpu.VMEM((PARTS, wide, LANES), f32),
                pltpu.VMEM((8, 2 * wide, 2 * LANES), jnp.bfloat16),
                pltpu.VMEM((8, 2 * wide, LANES), f32),
                pltpu.VMEM((PARTS, PACKED, LANES), f32),
                pltpu.VMEM((PARTS, PACKED, LANES), f32),
                pltpu.SemaphoreType.REGULAR((1,)),
                dma((7,)),
                dma((2,)),
                dma((2,)),
                dma((PARTS,)),
                dma((PARTS,)),
                dma((PARTS,)),
                dma((PARTS,)),
            ],
            compiler_params=pltpu.CompilerParams(collective_id=0, has_side_effects=True, vmem_limit_bytes=32 << 20),
        )(*(pltpu.with_memory_space_constraint(value, pltpu.HBM) for value in operands))
        return jnp.transpose(result, (1, 0, 2))

    return jax.shard_map(
        body,
        mesh=mesh,
        in_specs=(P("lat", "lon", None), P("lat"), P("lat")),
        out_specs=P("lat", "lon", None),
        check_vma=False,
    )
```

```python
import functools
import math

import jax
import jax.numpy as jnp
import numpy as np
from jax import lax
from jax.experimental import pallas as pl
from jax.experimental.pallas import tpu as pltpu
from jax.sharding import PartitionSpec as P

MESH = pl.DeviceIdType.MESH
PARTS = 16
LANES = 128
OPEN_CUT = 4096.0
DEPTH = 8
PACKED = 72


def split_table(table):
    high = np.asarray(table, dtype=jnp.bfloat16)
    low = np.asarray(table - high.astype(np.float64), dtype=jnp.bfloat16)
    return high, low


def dft_tables(nlon, width, wide):
    points = np.full(wide, -10**6)
    points[:width] = np.arange(width)
    points[width] = width
    points[wide - 1] = -1
    used = points > -10**6
    forward = np.zeros((8, 2 * wide, 2 * wide))
    inverse = np.zeros((8, 2 * wide, 2 * wide))
    sines = np.zeros((8, wide))
    for group in range(8):
        for row in range(wide):
            if group:
                if row >= width:
                    continue
                wave = group + PARTS * row
                weight = 2.0 / nlon
            else:
                half = width // 2 + 1
                if row < half:
                    wave = PARTS * row
                elif row < width + 1:
                    wave = 8 + PARTS * (row - half)
                else:
                    continue
                weight = (1.0 if wave in (0, nlon // 2) else 2.0) / nlon
            phase = np.where(used, (points * wave) % nlon, 0) * (2.0 * math.pi / nlon)
            cos_vals = np.where(used, np.cos(phase), 0.0)
            sin_vals = np.where(used, np.sin(phase), 0.0)
            inner = np.arange(wide) < width
            if group:
                forward[group, row, :wide] = cos_vals
                forward[group, row, wide:] = -sin_vals
                forward[group, wide + row, :wide] = -sin_vals
                forward[group, wide + row, wide:] = -cos_vals
                inverse[group, :wide, row] = weight * cos_vals * inner
                inverse[group, :wide, wide + row] = -weight * sin_vals * inner
                inverse[group, wide:, row] = weight * sin_vals * inner
                inverse[group, wide:, wide + row] = weight * cos_vals * inner
            else:
                base = 0 if row < half else wide
                part = slice(base, base + wide)
                forward[0, row, part] = cos_vals
                forward[0, wide + row, part] = -sin_vals
                inverse[0, part, row] = weight * cos_vals * inner
                inverse[0, part, wide + row] = -weight * sin_vals * inner
            sines[group, row] = math.sin(2.0 * math.pi * wave / nlon)
    waves = np.zeros((wide, LANES), np.float32)
    waves[:, :8] = sines.T
    return np.concatenate(split_table(np.concatenate([forward, inverse])), axis=1), waves


def coef_table(nlat, bands):
    rows = nlat // bands
    index = np.arange(-1, nlat + 1).astype(np.float32)
    angle = np.float32(-0.5 * math.pi) + (index + np.float32(0.5)) * np.float32(math.pi) / np.float32(nlat)
    cosine = np.cos(angle.astype(np.float64)).astype(np.float32).astype(np.float64)
    flux = cosine.copy()
    flux[0] = 0.0
    flux[-1] = 0.0
    table = np.zeros((bands, 16, LANES))
    for band in range(bands):
        at = band * rows + 1
        for row in range(rows):
            table[band, row] = 0.015 / cosine[at + row]
        for pair in range(rows // 2):
            even = at + 2 * pair
            odd = even + 1
            lane = np.zeros(8)
            lane[0] = 0.03 / cosine[even]
            lane[1] = 0.03 / cosine[odd]
            lane[4] = -0.015 * flux[odd] / cosine[even]
            lane[5] = 0.015 * flux[even] / cosine[odd]
            lane[6] = 0.015 * flux[even - 1] / cosine[even]
            lane[7] = -0.015 * flux[odd + 1] / cosine[odd]
            table[band, 8 + pair] = np.repeat(lane, 16)
    return table.astype(np.float32)


def wave_sum(terms):
    total = None
    for factor, value in terms:
        if abs(factor) < 1e-9:
            continue
        if abs(abs(factor) - 1.0) < 1e-9:
            if total is None:
                total = value if factor > 0 else -value
            else:
                total = total + value if factor > 0 else total - value
        else:
            part = value * np.float32(factor)
            total = part if total is None else total + part
    return total


def half_dft(even_in, odd_in):
    unit = 2.0 * math.pi / PARTS
    sums = [even_in[0] + even_in[8]] + [even_in[a] + even_in[8 - a] for a in (1, 2, 3)] + [even_in[4]]
    diffs = [even_in[0] - even_in[8]] + [even_in[a] - even_in[8 - a] for a in (1, 2, 3)]
    odd_sums = [None] + [odd_in[a] + odd_in[8 - a] for a in (1, 2, 3)] + [odd_in[4]]
    odd_diffs = [None] + [odd_in[a] - odd_in[8 - a] for a in (1, 2, 3)]
    cos_out = []
    sin_out = []
    for k in range(9):
        parts = diffs if k % 2 else sums
        cos_out.append(wave_sum([(math.cos(unit * a * k), parts[a]) for a in range(len(parts))]))
        parts = odd_sums if k % 2 else odd_diffs
        sin_out.append(wave_sum([(math.sin(unit * a * k), parts[a]) for a in range(1, len(parts))]))
    return cos_out, sin_out


def split_value(value):
    high = value.astype(jnp.bfloat16)
    low = (value - high.astype(jnp.float32)).astype(jnp.bfloat16)
    return jnp.concatenate([high, low], axis=1)


def table_dot(table, pair):
    both = jnp.dot(table, pair, preferred_element_type=jnp.float32)
    half = table.shape[0] // 2
    return both[:half, :LANES] + both[:half, LANES:] + both[half:, :LANES]


def kernel(
    bands,
    state_hbm, flag_hbm, cut_hbm, coef_hbm, table_hbm, wave_hbm,
    result,
    state, flag_ref, cut_ref, winds, press, slopes, cuts, coef, table, waves, damps, turns,
    halo_out, halo_in, send, recv, spectra, fields, bsend, brecv,
    hello, load_sem, halo_send, halo_recv, send_sem, recv_sem, bsend_sem, brecv_sem,
):
    lat = lax.axis_index("lat")
    lon = lax.axis_index("lon")
    width, rows = state_hbm.shape[0], state_hbm.shape[1]
    wide = recv.shape[1]
    spare = jnp.zeros((wide - width, LANES), jnp.float32)

    def field(row, part):
        return jnp.concatenate([state[:, row, pl.ds(part * LANES, LANES)], spare], axis=0)

    above = jnp.maximum(lat - 1, 0)
    below = jnp.minimum(lat + 1, bands - 1)
    sides = (lat > 0, lat < bands - 1)
    place = lax.rem(lat, DEPTH)
    paired = (place != 0, place != DEPTH - 1)
    opening = (place == 0) & sides[0]
    closing = (place == DEPTH - 1) & sides[1]
    known = jnp.where(paired[0], 1, 0) + jnp.where(sides[1], 1, 0)
    chip = lon // 2
    core = lon % 2

    def state_copy(part):
        spans = pl.ds(part * LANES, LANES)
        return pltpu.make_async_copy(state_hbm.at[:, :, spans], state.at[:, :, spans], load_sem.at[part])

    loads = [state_copy(1), state_copy(0)]
    loads.append(pltpu.make_async_copy(coef_hbm.at[lat], coef, load_sem.at[2]))
    loads.append(pltpu.make_async_copy(flag_hbm, flag_ref, load_sem.at[3]))
    loads.append(pltpu.make_async_copy(cut_hbm, cut_ref, load_sem.at[4]))
    tables = ((wave_hbm, waves), (table_hbm, table))
    for at, (source, target) in enumerate(tables):
        loads.append(pltpu.make_async_copy(source, target, load_sem.at[5 + at]))
    for load in loads[:5]:
        load.start()

    barrier = pltpu.get_barrier_semaphore()
    for offset in range(1, PARTS):
        pl.semaphore_signal(barrier, inc=1, device_id=(lat, lax.rem(lon + offset, PARTS)), device_id_type=MESH)

    for side, device in ((0, above), (1, below)):
        @pl.when(paired[side])
        def _():
            pl.semaphore_signal(barrier, inc=1, device_id=(device, lon), device_id_type=MESH)

    lane = lax.broadcasted_iota(jnp.int32, (wide, LANES), 1)
    line = lax.broadcasted_iota(jnp.int32, (wide, LANES), 0)
    first = lane < 64
    block = (lane // 16) % 4
    loads[0].wait()
    for row in range(rows):
        right = field(row, 1)
        turned = pltpu.roll(right, 64, 1)
        step = jnp.where(lane < 63, pltpu.roll(turned, LANES - 1, 1), 0.0) - jnp.where(lane > 0, pltpu.roll(turned, 1, 1), 0.0)
        vert = right - 0.1 * step
        step = jnp.where(lane < 63, pltpu.roll(vert, LANES - 1, 1), 0.0) - jnp.where(lane > 0, pltpu.roll(vert, 1, 1), 0.0)
        press[row] = turned - 0.015 * step
        result[:, row, pl.ds(LANES, LANES)] = vert[:width]
        slopes[row] = pltpu.roll(turned, wide - 1, 0) - pltpu.roll(turned, 1, 0)
    for load in loads[1:3]:
        load.wait()

    def prepare(row):
        left = field(row, 0)
        zonal = left - coef[pl.ds(row, 1), :] * slopes[row]
        merid = left
        if row < rows - 1:
            merid = merid - 0.015 * field(row + 1, 1)
        if row > 0:
            merid = merid + 0.015 * field(row - 1, 1)
        winds[row + 1] = jnp.where(first, zonal, merid)

    def pack(pair, slot):
        even = 2 * pair + 1
        sources = (
            jnp.where(first, winds[even], winds[even + 1]),
            jnp.where(first, winds[even + 1], winds[even]),
            jnp.where(first, press[even - 1], winds[even - 1]),
            jnp.where(first, press[even], winds[even + 2]),
        )
        for quarter in range(4):
            chunk = sources[quarter]
            for at in range(4):
                if at != quarter:
                    chunk = jnp.where(block == at, pltpu.roll(sources[at], (16 * (at - quarter)) % LANES, 1), chunk)
            send[slot + 4 * quarter] = chunk

    def halo_copy(side, slot, device):
        return pltpu.make_async_remote_copy(
            src_ref=halo_out.at[side],
            dst_ref=halo_in.at[slot],
            send_sem=halo_send.at[side],
            recv_sem=halo_recv.at[slot],
            device_id=(device, lon),
            device_id_type=MESH,
        )

    halos = [halo_copy(0, 1, above), halo_copy(1, 0, below)]

    def forward_copy(source, slot, device):
        return pltpu.make_async_remote_copy(
            src_ref=send.at[source],
            dst_ref=recv.at[slot],
            send_sem=send_sem.at[source],
            recv_sem=recv_sem.at[slot],
            device_id=(lat, device),
            device_id_type=MESH,
        )

    def backward_copy(source, slot, device):
        return pltpu.make_async_remote_copy(
            src_ref=bsend.at[source],
            dst_ref=brecv.at[slot],
            send_sem=bsend_sem.at[source],
            recv_sem=brecv_sem.at[slot],
            device_id=(lat, device),
            device_id_type=MESH,
        )

    order = (4, 3, 5, 2, 6, 1, 7, 0)

    def send_to(copy, kind):
        for offset in order:
            target = 2 * lax.rem(chip + offset, 8) + kind
            if offset:
                copy(target, lon, target).start()
            else:
                @pl.when(core != kind)
                def _():
                    copy(target, lon, target).start()

    def pack_and_send(pair, at, kind):
        pack(pair, 2 * at + kind)
        for offset in (2, 1, 3, 0):
            target = 2 * at + 4 * lax.rem(chip // 2 + offset, 4) + kind

            @pl.when(target != lon)
            def _():
                forward_copy(target, lon, target).start()

    prepare(0)
    prepare(rows - 1)
    for load in loads[3:5]:
        load.wait()
    for row in range(rows):
        kept = jnp.full((1, LANES), cut_ref[row], jnp.int32).astype(jnp.float32)
        flag = jnp.full((1, LANES), flag_ref[row], jnp.int32)
        cuts[pl.ds(row + 1, 1), :] = jnp.where(flag == 1, kept, OPEN_CUT)
    for side, row in ((0, 0), (1, rows - 1)):
        turned = pltpu.roll(field(row, 1), 64, 1)
        message = jnp.where(first, turned, winds[row + 1])
        halo_out[side] = jnp.where(line == width, cuts[pl.ds(row + 1, 1), :], message)
    for row in range(1, 5):
        prepare(row)

    pl.semaphore_wait(barrier, PARTS - 1 + known)
    pl.when(paired[0])(halos[0].start)
    pl.when(sides[1])(halos[1].start)

    @pl.when(opening)
    def _():
        pl.semaphore_signal(barrier, inc=1, device_id=(above, lon), device_id_type=MESH)

    @pl.when(closing)
    def _():
        pl.semaphore_signal(hello.at[0], inc=1, device_id=(below, lon), device_id_type=MESH)

    pack_and_send(1, 0, 0)
    for load in loads[5:]:
        load.start()
    for row in range(5, 7):
        prepare(row)
    pack_and_send(2, 1, 0)

    flip = jnp.where((place == 0) | (place == DEPTH - 1), 1, 0)
    for step in range(2):
        side = flip if step == 0 else 1 - flip
        present = jnp.where(side == 0, lat, bands - 1 - lat) > 0

        @pl.when(present)
        def _():
            halo_copy(1 - side, side, above).wait_recv()

        @pl.when(jnp.logical_not(present))
        def _():
            halo_in[side] = jnp.zeros((wide, LANES), jnp.float32)

        outer = jnp.where(side == 0, 0, rows + 1)
        inner = jnp.where(side == 0, 1, rows)
        slope = jnp.where(side == 0, 0.015, -0.015)
        inside = jnp.where(present, slope, 0.0)
        arrived = halo_in[side]
        cuts[pl.ds(outer, 1), :] = arrived[width : width + 1]
        winds[outer] = jnp.where(line < width, arrived - slope * pltpu.roll(halo_out[side], 64, 1), 0.0)
        winds[inner] = winds[inner] + jnp.where(first | (line >= width), 0.0, inside * pltpu.roll(arrived, 64, 1))
        pack_and_send(3 * side, side, 1)
        if step == 0:
            @pl.when(opening)
            def _():
                pl.semaphore_wait(hello.at[0], 1)
                halos[0].start()

    recv[lon] = send[lon]

    half = chip % 2
    mine = (1 - core) * (1 + half) + core * 3 * half
    lanes = lax.broadcasted_iota(jnp.int32, (1, LANES), 1) // 16
    cut_even = cuts[pl.ds(2 * mine + 1, 1), :]
    cut_odd = cuts[pl.ds(2 * mine + 2, 1), :]
    limit = jnp.where((lanes == 0) | (lanes == 2) | (lanes == 5), cut_even, cut_odd)
    limit = jnp.where(lanes == 6, cuts[pl.ds(2 * mine, 1), :], limit)
    limit = jnp.where(lanes == 7, cuts[pl.ds(2 * mine + 3, 1), :], limit)
    factor = coef[pl.ds(8 + mine, 1), :]
    loads[5].wait()

    for group in range(8):
        wave = PARTS * line + group
        if group:
            wave = jnp.minimum(wave, PARTS * width - wave)
        else:
            wave = jnp.where(line <= width // 2, wave, PARTS * (line - width // 2 - 1) + 8)
        ratio = limit / jnp.maximum(wave, 1).astype(jnp.float32)
        damps[group] = jnp.minimum(1.0, ratio * ratio)
        turns[group] = factor * waves[:, group : group + 1]
    for load in loads[6:]:
        load.wait()

    def receive(offset, carry):
        source = lax.rem(lon + offset, PARTS)
        forward_copy(source, source, source).wait_recv()
        return carry

    lax.fori_loop(1, PARTS, receive, 0)

    def gather_waves(at, carry):
        where = pl.multiple_of(16 * at, 16)
        spans = pl.ds(where, 16)
        images = pl.ds(pl.multiple_of(wide + where, 16), 16)
        values = [recv[a, spans, :] for a in range(PARTS)]
        evens = [values[0]] + [values[a] + values[PARTS - a] for a in range(1, 8)] + [values[8]]
        odds = [None] + [values[a] - values[PARTS - a] for a in range(1, 8)]
        cos_out, sin_out = half_dft(evens, odds)
        spectra[0, spans, :] = split_value(cos_out[0])
        spectra[0, images, :] = split_value(cos_out[8])
        for k in range(1, 8):
            spectra[k, spans, :] = split_value(cos_out[k])
            spectra[k, images, :] = split_value(sin_out[k])
        return carry

    lax.fori_loop(0, wide // 16, gather_waves, 0, unroll=6)

    def transform(group, carry):
        values = table_dot(table[group], spectra[group])
        damping = damps[group]
        real = values[:wide] * damping
        imag = values[wide:] * damping
        turn = turns[group]
        zonal = lane < 32
        lift_real = jnp.where(zonal, turn * imag, factor * real)
        lift_imag = jnp.where(zonal, -turn * real, factor * imag)
        inner = (lane >= 32) & first
        outs = []
        for value, lift in ((real, lift_real), (imag, lift_imag)):
            total = pltpu.roll(lift, 32, 1) + pltpu.roll(lift, 96, 1) + pltpu.roll(lift, 64, 1)
            outs.append(jnp.where(inner, value + damping * total, value))
        both = split_value(jnp.concatenate(outs, axis=0))
        fields[group] = table_dot(table[8 + group], both)
        return carry

    lax.fori_loop(0, 8, transform, 0, unroll=8)

    def scatter_waves(at, carry):
        where = pl.multiple_of(16 * at, 16)
        spans = pl.ds(where, 16)
        images = pl.ds(pl.multiple_of(wide + where, 16), 16)
        evens = [fields[0, spans, :]] + [fields[k, spans, :] for k in range(1, 8)] + [fields[0, images, :]]
        odds = [None] + [fields[k, images, :] for k in range(1, 8)]
        cos_out, sin_out = half_dft(evens, odds)
        circles[0, spans, :] = cos_out[0]
        circles[8, spans, :] = cos_out[8]
        for a in range(1, 8):
            circles[a, spans, :] = cos_out[a] - sin_out[a]
            circles[PARTS - a, spans, :] = cos_out[a] + sin_out[a]
        return carry

    circles = recv
    lax.fori_loop(0, wide // 16, scatter_waves, 0, unroll=6)
    narrow = lax.broadcasted_iota(jnp.int32, (24, LANES), 1)

    def pack_back(a, carry):
        rest = circles[a, pl.ds(72, 24), :]
        for at in range(3):
            spans = pl.ds(24 * at, 24)
            bsend[a, spans, :] = jnp.where(narrow < 96, circles[a, spans, :], pltpu.roll(rest, 96 - 32 * at, 1))
        return carry

    lax.fori_loop(0, PARTS, pack_back, 0, unroll=PARTS)
    send_to(backward_copy, 1)
    for turn in (1, 0):
        for offset in (2, 1, 3, 0):
            target = 4 * lax.rem(chip // 2 + offset, 4) + 2 * turn

            @pl.when(target != lon)
            def _():
                backward_copy(target, lon, target).start()

    brecv[lon] = bsend[lon]

    def unpack(pair, slot):
        chunks = []
        for quarter in range(4):
            source = slot + 4 * quarter

            @pl.when(source != lon)
            def _():
                backward_copy(source, source, source).wait_recv()

            pieces = [brecv[source, pl.ds(24 * at, 24), :] for at in range(3)]
            rest = jnp.where(narrow < 32, pltpu.roll(pieces[0], 32, 1), pltpu.roll(pieces[1], 64, 1))
            rest = jnp.where(narrow < 64, rest, pltpu.roll(pieces[2], 96, 1))
            chunks.append(jnp.concatenate(pieces + [rest], axis=0))
        parts = []
        for at in range(4):
            shift = 64 if at >= 2 else 0
            part = None
            for quarter in range(4):
                amount = (16 * (quarter - at) + shift) % LANES
                moved = pltpu.roll(chunks[quarter], amount, 1) if amount else chunks[quarter]
                part = moved if part is None else jnp.where(block == quarter, moved, part)
            parts.append(part)
        even = 2 * pair
        spans = pl.ds(0, LANES)
        result[:, even, spans] = jnp.where(first, parts[0], parts[1])[:width]
        result[:, even + 1, spans] = jnp.where(first, parts[1], parts[0])[:width]
        spans = pl.ds(LANES, LANES)
        result[:, even, spans] = jnp.where(first[:width], result[:, even, spans], parts[2][:width])
        result[:, even + 1, spans] = jnp.where(first[:width], result[:, even + 1, spans], parts[3][:width])

    for at in range(2):
        unpack(1 + at, 2 * at)
    for at in range(2):
        unpack(3 * at, 2 * at + 1)

    def finish(offset, carry):
        target = lax.rem(lon + offset, PARTS)
        forward_copy(target, lon, target).wait_send()
        backward_copy(target, lon, target).wait_send()
        return carry

    lax.fori_loop(1, PARTS, finish, 0)
    for side in range(2):
        pl.when(sides[side])(halos[side].wait_send)


def solution(mesh):
    bands = mesh.shape["lat"]

    def body(state, filter_flag, cutoff):
        rows, width, depth = state.shape
        wide = (width + 2 + 15) // 16 * 16
        tables = dft_tables(width * PARTS, width, wide)
        coefs = coef_table(rows * bands, bands)
        f32 = jnp.float32
        table = pltpu.VMEM((16, 4 * wide, 2 * wide), jnp.bfloat16)
        hbm_spec = pl.BlockSpec(memory_space=pltpu.HBM)
        dma = pltpu.SemaphoreType.DMA
        operands = (jnp.transpose(state, (1, 0, 2)), filter_flag, cutoff) + tuple(map(jnp.asarray, (coefs,) + tables))
        result = pl.pallas_call(
            functools.partial(kernel, bands),
            out_shape=jax.ShapeDtypeStruct((width, rows, depth), f32),
            in_specs=[hbm_spec] * 6,
            out_specs=pl.BlockSpec(memory_space=pltpu.VMEM),
            scratch_shapes=[
                pltpu.VMEM((width, rows, depth), f32),
                pltpu.SMEM((rows,), jnp.int32),
                pltpu.SMEM((rows,), jnp.int32),
                pltpu.VMEM((rows + 2, wide, LANES), f32),
                pltpu.VMEM((rows, wide, LANES), f32),
                pltpu.VMEM((rows, wide, LANES), f32),
                pltpu.VMEM((16, LANES), f32),
                pltpu.VMEM((16, LANES), f32),
                table,
                pltpu.VMEM((wide, LANES), f32),
                pltpu.VMEM((8, wide, LANES), f32),
                pltpu.VMEM((8, wide, LANES), f32),
                pltpu.VMEM((2, wide, LANES), f32),
                pltpu.VMEM((2, wide, LANES), f32),
                pltpu.VMEM((PARTS, wide, LANES), f32),
                pltpu.VMEM((PARTS, wide, LANES), f32),
                pltpu.VMEM((8, 2 * wide, 2 * LANES), jnp.bfloat16),
                pltpu.VMEM((8, 2 * wide, LANES), f32),
                pltpu.VMEM((PARTS, PACKED, LANES), f32),
                pltpu.VMEM((PARTS, PACKED, LANES), f32),
                pltpu.SemaphoreType.REGULAR((1,)),
                dma((7,)),
                dma((2,)),
                dma((2,)),
                dma((PARTS,)),
                dma((PARTS,)),
                dma((PARTS,)),
                dma((PARTS,)),
            ],
            compiler_params=pltpu.CompilerParams(collective_id=0, has_side_effects=True, vmem_limit_bytes=32 << 20),
        )(*(pltpu.with_memory_space_constraint(value, pltpu.HBM) for value in operands))
        return jnp.transpose(result, (1, 0, 2))

    return jax.shard_map(
        body,
        mesh=mesh,
        in_specs=(P("lat", "lon", None), P("lat"), P("lat")),
        out_specs=P("lat", "lon", None),
        check_vma=False,
    )
```

```python
import functools
import math

import jax
import jax.numpy as jnp
import numpy as np
from jax import lax
from jax.experimental import pallas as pl
from jax.experimental.pallas import tpu as pltpu
from jax.sharding import PartitionSpec as P

MESH = pl.DeviceIdType.MESH
PARTS = 16
LANES = 128
OPEN_CUT = 4096.0
DEPTH = 8
PACKED = 72


def split_table(table):
    high = np.asarray(table, dtype=jnp.bfloat16)
    low = np.asarray(table - high.astype(np.float64), dtype=jnp.bfloat16)
    return high, low


def dft_tables(nlon, width, wide):
    points = np.full(wide, -10**6)
    points[:width] = np.arange(width)
    points[width] = width
    points[wide - 1] = -1
    used = points > -10**6
    forward = np.zeros((8, 2 * wide, 2 * wide))
    inverse = np.zeros((8, 2 * wide, 2 * wide))
    sines = np.zeros((8, wide))
    for group in range(8):
        for row in range(wide):
            if group:
                if row >= width:
                    continue
                wave = group + PARTS * row
                weight = 2.0 / nlon
            else:
                half = width // 2 + 1
                if row < half:
                    wave = PARTS * row
                elif row < width + 1:
                    wave = 8 + PARTS * (row - half)
                else:
                    continue
                weight = (1.0 if wave in (0, nlon // 2) else 2.0) / nlon
            phase = np.where(used, (points * wave) % nlon, 0) * (2.0 * math.pi / nlon)
            cos_vals = np.where(used, np.cos(phase), 0.0)
            sin_vals = np.where(used, np.sin(phase), 0.0)
            inner = np.arange(wide) < width
            if group:
                forward[group, row, :wide] = cos_vals
                forward[group, row, wide:] = -sin_vals
                forward[group, wide + row, :wide] = -sin_vals
                forward[group, wide + row, wide:] = -cos_vals
                inverse[group, :wide, row] = weight * cos_vals * inner
                inverse[group, :wide, wide + row] = -weight * sin_vals * inner
                inverse[group, wide:, row] = weight * sin_vals * inner
                inverse[group, wide:, wide + row] = weight * cos_vals * inner
            else:
                base = 0 if row < half else wide
                part = slice(base, base + wide)
                forward[0, row, part] = cos_vals
                forward[0, wide + row, part] = -sin_vals
                inverse[0, part, row] = weight * cos_vals * inner
                inverse[0, part, wide + row] = -weight * sin_vals * inner
            sines[group, row] = math.sin(2.0 * math.pi * wave / nlon)
    waves = np.zeros((wide, LANES), np.float32)
    waves[:, :8] = sines.T
    return np.concatenate(split_table(np.concatenate([forward, inverse])), axis=1), waves


def coef_table(nlat, bands):
    rows = nlat // bands
    index = np.arange(-1, nlat + 1).astype(np.float32)
    angle = np.float32(-0.5 * math.pi) + (index + np.float32(0.5)) * np.float32(math.pi) / np.float32(nlat)
    cosine = np.cos(angle.astype(np.float64)).astype(np.float32).astype(np.float64)
    flux = cosine.copy()
    flux[0] = 0.0
    flux[-1] = 0.0
    table = np.zeros((bands, 16, LANES))
    for band in range(bands):
        at = band * rows + 1
        for row in range(rows):
            table[band, row] = 0.015 / cosine[at + row]
        for pair in range(rows // 2):
            even = at + 2 * pair
            odd = even + 1
            lane = np.zeros(8)
            lane[0] = 0.03 / cosine[even]
            lane[1] = 0.03 / cosine[odd]
            lane[4] = -0.015 * flux[odd] / cosine[even]
            lane[5] = 0.015 * flux[even] / cosine[odd]
            lane[6] = 0.015 * flux[even - 1] / cosine[even]
            lane[7] = -0.015 * flux[odd + 1] / cosine[odd]
            table[band, 8 + pair] = np.repeat(lane, 16)
    return table.astype(np.float32)


def wave_sum(terms):
    total = None
    for factor, value in terms:
        if abs(factor) < 1e-9:
            continue
        if abs(abs(factor) - 1.0) < 1e-9:
            if total is None:
                total = value if factor > 0 else -value
            else:
                total = total + value if factor > 0 else total - value
        else:
            part = value * np.float32(factor)
            total = part if total is None else total + part
    return total


def half_dft(even_in, odd_in):
    unit = 2.0 * math.pi / PARTS
    sums = [even_in[0] + even_in[8]] + [even_in[a] + even_in[8 - a] for a in (1, 2, 3)] + [even_in[4]]
    diffs = [even_in[0] - even_in[8]] + [even_in[a] - even_in[8 - a] for a in (1, 2, 3)]
    odd_sums = [None] + [odd_in[a] + odd_in[8 - a] for a in (1, 2, 3)] + [odd_in[4]]
    odd_diffs = [None] + [odd_in[a] - odd_in[8 - a] for a in (1, 2, 3)]
    cos_out = []
    sin_out = []
    for k in range(9):
        parts = diffs if k % 2 else sums
        cos_out.append(wave_sum([(math.cos(unit * a * k), parts[a]) for a in range(len(parts))]))
        parts = odd_sums if k % 2 else odd_diffs
        sin_out.append(wave_sum([(math.sin(unit * a * k), parts[a]) for a in range(1, len(parts))]))
    return cos_out, sin_out


def split_value(value):
    high = value.astype(jnp.bfloat16)
    low = (value - high.astype(jnp.float32)).astype(jnp.bfloat16)
    return jnp.concatenate([high, low], axis=1)


def table_dot(table, pair):
    both = jnp.dot(table, pair, preferred_element_type=jnp.float32)
    half = table.shape[0] // 2
    return both[:half, :LANES] + both[:half, LANES:] + both[half:, :LANES]


def kernel(
    bands,
    state_hbm, flag_hbm, cut_hbm, coef_hbm, table_hbm, wave_hbm,
    result,
    state, flag_ref, cut_ref, winds, press, slopes, cuts, coef, table, waves, damps, turns,
    halo_out, halo_in, send, recv, spectra, fields, bsend, brecv,
    hello, load_sem, halo_send, halo_recv, send_sem, recv_sem, bsend_sem, brecv_sem,
):
    lat = lax.axis_index("lat")
    lon = lax.axis_index("lon")
    width, rows = state_hbm.shape[0], state_hbm.shape[1]
    wide = recv.shape[1]
    spare = jnp.zeros((wide - width, LANES), jnp.float32)

    def field(row, part):
        return jnp.concatenate([state[:, row, pl.ds(part * LANES, LANES)], spare], axis=0)

    above = jnp.maximum(lat - 1, 0)
    below = jnp.minimum(lat + 1, bands - 1)
    sides = (lat > 0, lat < bands - 1)
    place = lax.rem(lat, DEPTH)
    paired = (place != 0, place != DEPTH - 1)
    opening = (place == 0) & sides[0]
    closing = (place == DEPTH - 1) & sides[1]
    known = jnp.where(paired[0], 1, 0) + jnp.where(sides[1], 1, 0)
    chip = lon // 2
    core = lon % 2

    def state_copy(part):
        spans = pl.ds(part * LANES, LANES)
        return pltpu.make_async_copy(state_hbm.at[:, :, spans], state.at[:, :, spans], load_sem.at[part])

    loads = [state_copy(1), state_copy(0)]
    loads.append(pltpu.make_async_copy(coef_hbm.at[lat], coef, load_sem.at[2]))
    loads.append(pltpu.make_async_copy(flag_hbm, flag_ref, load_sem.at[3]))
    loads.append(pltpu.make_async_copy(cut_hbm, cut_ref, load_sem.at[4]))
    tables = ((wave_hbm, waves), (table_hbm, table))
    for at, (source, target) in enumerate(tables):
        loads.append(pltpu.make_async_copy(source, target, load_sem.at[5 + at]))
    for load in loads[:5]:
        load.start()

    barrier = pltpu.get_barrier_semaphore()
    for offset in range(1, PARTS):
        pl.semaphore_signal(barrier, inc=1, device_id=(lat, lax.rem(lon + offset, PARTS)), device_id_type=MESH)

    for side, device in ((0, above), (1, below)):
        @pl.when(paired[side])
        def _():
            pl.semaphore_signal(barrier, inc=1, device_id=(device, lon), device_id_type=MESH)

    lane = lax.broadcasted_iota(jnp.int32, (wide, LANES), 1)
    line = lax.broadcasted_iota(jnp.int32, (wide, LANES), 0)
    first = lane < 64
    block = (lane // 16) % 4
    loads[0].wait()
    for row in range(rows):
        right = field(row, 1)
        turned = pltpu.roll(right, 64, 1)
        step = jnp.where(lane < 63, pltpu.roll(turned, LANES - 1, 1), 0.0) - jnp.where(lane > 0, pltpu.roll(turned, 1, 1), 0.0)
        vert = right - 0.1 * step
        step = jnp.where(lane < 63, pltpu.roll(vert, LANES - 1, 1), 0.0) - jnp.where(lane > 0, pltpu.roll(vert, 1, 1), 0.0)
        press[row] = turned - 0.015 * step
        result[:, row, pl.ds(LANES, LANES)] = vert[:width]
        slopes[row] = pltpu.roll(turned, wide - 1, 0) - pltpu.roll(turned, 1, 0)
    for load in loads[1:3]:
        load.wait()

    def prepare(row):
        left = field(row, 0)
        zonal = left - coef[pl.ds(row, 1), :] * slopes[row]
        merid = left
        if row < rows - 1:
            merid = merid - 0.015 * field(row + 1, 1)
        if row > 0:
            merid = merid + 0.015 * field(row - 1, 1)
        winds[row + 1] = jnp.where(first, zonal, merid)

    def pack(pair, slot):
        even = 2 * pair + 1
        sources = (
            jnp.where(first, winds[even], winds[even + 1]),
            jnp.where(first, winds[even + 1], winds[even]),
            jnp.where(first, press[even - 1], winds[even - 1]),
            jnp.where(first, press[even], winds[even + 2]),
        )
        for quarter in range(4):
            chunk = sources[quarter]
            for at in range(4):
                if at != quarter:
                    chunk = jnp.where(block == at, pltpu.roll(sources[at], (16 * (at - quarter)) % LANES, 1), chunk)
            send[slot + 4 * quarter] = chunk

    def halo_copy(side, slot, device):
        return pltpu.make_async_remote_copy(
            src_ref=halo_out.at[side],
            dst_ref=halo_in.at[slot],
            send_sem=halo_send.at[side],
            recv_sem=halo_recv.at[slot],
            device_id=(device, lon),
            device_id_type=MESH,
        )

    halos = [halo_copy(0, 1, above), halo_copy(1, 0, below)]

    def forward_copy(source, slot, device):
        return pltpu.make_async_remote_copy(
            src_ref=send.at[source],
            dst_ref=recv.at[slot],
            send_sem=send_sem.at[source],
            recv_sem=recv_sem.at[slot],
            device_id=(lat, device),
            device_id_type=MESH,
        )

    def backward_copy(source, slot, device):
        return pltpu.make_async_remote_copy(
            src_ref=bsend.at[source],
            dst_ref=brecv.at[slot],
            send_sem=bsend_sem.at[source],
            recv_sem=brecv_sem.at[slot],
            device_id=(lat, device),
            device_id_type=MESH,
        )

    order = (4, 3, 5, 2, 6, 1, 7, 0)

    def send_to(copy, kind):
        for offset in order:
            target = 2 * lax.rem(chip + offset, 8) + kind
            if offset:
                copy(target, lon, target).start()
            else:
                @pl.when(core != kind)
                def _():
                    copy(target, lon, target).start()

    def pack_and_send(pair, at, kind):
        pack(pair, 2 * at + kind)
        for offset in (2, 1, 3, 0):
            target = 2 * at + 4 * lax.rem(chip // 2 + offset, 4) + kind

            @pl.when(target != lon)
            def _():
                forward_copy(target, lon, target).start()

    prepare(0)
    prepare(rows - 1)
    for load in loads[3:5]:
        load.wait()
    for row in range(rows):
        kept = jnp.full((1, LANES), cut_ref[row], jnp.int32).astype(jnp.float32)
        flag = jnp.full((1, LANES), flag_ref[row], jnp.int32)
        cuts[pl.ds(row + 1, 1), :] = jnp.where(flag == 1, kept, OPEN_CUT)
    for side, row in ((0, 0), (1, rows - 1)):
        turned = pltpu.roll(field(row, 1), 64, 1)
        message = jnp.where(first, turned, winds[row + 1])
        halo_out[side] = jnp.where(line == width, cuts[pl.ds(row + 1, 1), :], message)
    for row in range(1, 5):
        prepare(row)

    pl.semaphore_wait(barrier, PARTS - 1 + known)
    pl.when(paired[0])(halos[0].start)
    pl.when(sides[1])(halos[1].start)

    @pl.when(opening)
    def _():
        pl.semaphore_signal(barrier, inc=1, device_id=(above, lon), device_id_type=MESH)

    @pl.when(closing)
    def _():
        pl.semaphore_signal(hello.at[0], inc=1, device_id=(below, lon), device_id_type=MESH)

    pack_and_send(1, 0, 0)
    for load in loads[5:]:
        load.start()
    for row in range(5, 7):
        prepare(row)
    pack_and_send(2, 1, 0)

    flip = jnp.where((place == 0) | (place == DEPTH - 1), 1, 0)
    for step in range(2):
        side = flip if step == 0 else 1 - flip
        present = jnp.where(side == 0, lat, bands - 1 - lat) > 0

        @pl.when(present)
        def _():
            halo_copy(1 - side, side, above).wait_recv()

        @pl.when(jnp.logical_not(present))
        def _():
            halo_in[side] = jnp.zeros((wide, LANES), jnp.float32)

        outer = jnp.where(side == 0, 0, rows + 1)
        inner = jnp.where(side == 0, 1, rows)
        slope = jnp.where(side == 0, 0.015, -0.015)
        inside = jnp.where(present, slope, 0.0)
        arrived = halo_in[side]
        cuts[pl.ds(outer, 1), :] = arrived[width : width + 1]
        winds[outer] = jnp.where(line < width, arrived - slope * pltpu.roll(halo_out[side], 64, 1), 0.0)
        winds[inner] = winds[inner] + jnp.where(first | (line >= width), 0.0, inside * pltpu.roll(arrived, 64, 1))
        pack_and_send(3 * side, side, 1)
        if step == 0:
            @pl.when(opening)
            def _():
                pl.semaphore_wait(hello.at[0], 1)
                halos[0].start()

    recv[lon] = send[lon]

    half = chip % 2
    mine = (1 - core) * (1 + half) + core * 3 * half
    lanes = lax.broadcasted_iota(jnp.int32, (1, LANES), 1) // 16
    cut_even = cuts[pl.ds(2 * mine + 1, 1), :]
    cut_odd = cuts[pl.ds(2 * mine + 2, 1), :]
    limit = jnp.where((lanes == 0) | (lanes == 2) | (lanes == 5), cut_even, cut_odd)
    limit = jnp.where(lanes == 6, cuts[pl.ds(2 * mine, 1), :], limit)
    limit = jnp.where(lanes == 7, cuts[pl.ds(2 * mine + 3, 1), :], limit)
    factor = coef[pl.ds(8 + mine, 1), :]
    loads[5].wait()

    for group in range(8):
        wave = PARTS * line + group
        if group:
            wave = jnp.minimum(wave, PARTS * width - wave)
        else:
            wave = jnp.where(line <= width // 2, wave, PARTS * (line - width // 2 - 1) + 8)
        ratio = limit / jnp.maximum(wave, 1).astype(jnp.float32)
        damps[group] = jnp.minimum(1.0, ratio * ratio)
        turns[group] = factor * waves[:, group : group + 1]
    for load in loads[6:]:
        load.wait()

    def receive(offset, carry):
        source = lax.rem(lon + offset, PARTS)
        forward_copy(source, source, source).wait_recv()
        return carry

    lax.fori_loop(1, PARTS, receive, 0)

    def gather_waves(at, carry):
        where = pl.multiple_of(16 * at, 16)
        spans = pl.ds(where, 16)
        images = pl.ds(pl.multiple_of(wide + where, 16), 16)
        values = [recv[a, spans, :] for a in range(PARTS)]
        evens = [values[0]] + [values[a] + values[PARTS - a] for a in range(1, 8)] + [values[8]]
        odds = [None] + [values[a] - values[PARTS - a] for a in range(1, 8)]
        cos_out, sin_out = half_dft(evens, odds)
        spectra[0, spans, :] = split_value(cos_out[0])
        spectra[0, images, :] = split_value(cos_out[8])
        for k in range(1, 8):
            spectra[k, spans, :] = split_value(cos_out[k])
            spectra[k, images, :] = split_value(sin_out[k])
        return carry

    lax.fori_loop(0, wide // 16, gather_waves, 0, unroll=6)

    def transform(group, carry):
        values = table_dot(table[group], spectra[group])
        damping = damps[group]
        real = values[:wide] * damping
        imag = values[wide:] * damping
        turn = turns[group]
        zonal = lane < 32
        lift_real = jnp.where(zonal, turn * imag, factor * real)
        lift_imag = jnp.where(zonal, -turn * real, factor * imag)
        inner = (lane >= 32) & first
        outs = []
        for value, lift in ((real, lift_real), (imag, lift_imag)):
            total = pltpu.roll(lift, 32, 1) + pltpu.roll(lift, 96, 1) + pltpu.roll(lift, 64, 1)
            outs.append(jnp.where(inner, value + damping * total, value))
        both = split_value(jnp.concatenate(outs, axis=0))
        fields[group] = table_dot(table[8 + group], both)
        return carry

    lax.fori_loop(0, 8, transform, 0, unroll=8)

    def scatter_waves(at, carry):
        where = pl.multiple_of(16 * at, 16)
        spans = pl.ds(where, 16)
        images = pl.ds(pl.multiple_of(wide + where, 16), 16)
        evens = [fields[0, spans, :]] + [fields[k, spans, :] for k in range(1, 8)] + [fields[0, images, :]]
        odds = [None] + [fields[k, images, :] for k in range(1, 8)]
        cos_out, sin_out = half_dft(evens, odds)
        circles[0, spans, :] = cos_out[0]
        circles[8, spans, :] = cos_out[8]
        for a in range(1, 8):
            circles[a, spans, :] = cos_out[a] - sin_out[a]
            circles[PARTS - a, spans, :] = cos_out[a] + sin_out[a]
        return carry

    circles = recv
    lax.fori_loop(0, wide // 16, scatter_waves, 0, unroll=6)
    narrow = lax.broadcasted_iota(jnp.int32, (24, LANES), 1)

    def pack_back(a, carry):
        rest = circles[a, pl.ds(72, 24), :]
        for at in range(3):
            spans = pl.ds(24 * at, 24)
            bsend[a, spans, :] = jnp.where(narrow < 96, circles[a, spans, :], pltpu.roll(rest, 96 - 32 * at, 1))
        return carry

    lax.fori_loop(0, PARTS, pack_back, 0, unroll=PARTS)
    send_to(backward_copy, 1)
    for turn, offsets in ((1, (2, 1, 3, 0)), (2, (1, 0)), (0, (1, 0))):
        for offset in offsets:
            if turn == 1:
                target = 4 * lax.rem(chip // 2 + offset, 4) + 2
            else:
                target = 8 * lax.rem(chip // 4 + offset, 2) + 2 * turn

            @pl.when(target != lon)
            def _():
                backward_copy(target, lon, target).start()

    brecv[lon] = bsend[lon]

    def unpack(pair, slot):
        chunks = []
        for quarter in range(4):
            source = slot + 4 * quarter

            @pl.when(source != lon)
            def _():
                backward_copy(source, source, source).wait_recv()

            pieces = [brecv[source, pl.ds(24 * at, 24), :] for at in range(3)]
            rest = jnp.where(narrow < 32, pltpu.roll(pieces[0], 32, 1), pltpu.roll(pieces[1], 64, 1))
            rest = jnp.where(narrow < 64, rest, pltpu.roll(pieces[2], 96, 1))
            chunks.append(jnp.concatenate(pieces + [rest], axis=0))
        parts = []
        for at in range(4):
            shift = 64 if at >= 2 else 0
            part = None
            for quarter in range(4):
                amount = (16 * (quarter - at) + shift) % LANES
                moved = pltpu.roll(chunks[quarter], amount, 1) if amount else chunks[quarter]
                part = moved if part is None else jnp.where(block == quarter, moved, part)
            parts.append(part)
        even = 2 * pair
        spans = pl.ds(0, LANES)
        result[:, even, spans] = jnp.where(first, parts[0], parts[1])[:width]
        result[:, even + 1, spans] = jnp.where(first, parts[1], parts[0])[:width]
        spans = pl.ds(LANES, LANES)
        result[:, even, spans] = jnp.where(first[:width], result[:, even, spans], parts[2][:width])
        result[:, even + 1, spans] = jnp.where(first[:width], result[:, even + 1, spans], parts[3][:width])

    for at in range(2):
        unpack(1 + at, 2 * at)
    for at in range(2):
        unpack(3 * at, 2 * at + 1)

    def finish(offset, carry):
        target = lax.rem(lon + offset, PARTS)
        forward_copy(target, lon, target).wait_send()
        backward_copy(target, lon, target).wait_send()
        return carry

    lax.fori_loop(1, PARTS, finish, 0)
    for side in range(2):
        pl.when(sides[side])(halos[side].wait_send)


def solution(mesh):
    bands = mesh.shape["lat"]

    def body(state, filter_flag, cutoff):
        rows, width, depth = state.shape
        wide = (width + 2 + 15) // 16 * 16
        tables = dft_tables(width * PARTS, width, wide)
        coefs = coef_table(rows * bands, bands)
        f32 = jnp.float32
        table = pltpu.VMEM((16, 4 * wide, 2 * wide), jnp.bfloat16)
        hbm_spec = pl.BlockSpec(memory_space=pltpu.HBM)
        dma = pltpu.SemaphoreType.DMA
        operands = (jnp.transpose(state, (1, 0, 2)), filter_flag, cutoff) + tuple(map(jnp.asarray, (coefs,) + tables))
        result = pl.pallas_call(
            functools.partial(kernel, bands),
            out_shape=jax.ShapeDtypeStruct((width, rows, depth), f32),
            in_specs=[hbm_spec] * 6,
            out_specs=pl.BlockSpec(memory_space=pltpu.VMEM),
            scratch_shapes=[
                pltpu.VMEM((width, rows, depth), f32),
                pltpu.SMEM((rows,), jnp.int32),
                pltpu.SMEM((rows,), jnp.int32),
                pltpu.VMEM((rows + 2, wide, LANES), f32),
                pltpu.VMEM((rows, wide, LANES), f32),
                pltpu.VMEM((rows, wide, LANES), f32),
                pltpu.VMEM((16, LANES), f32),
                pltpu.VMEM((16, LANES), f32),
                table,
                pltpu.VMEM((wide, LANES), f32),
                pltpu.VMEM((8, wide, LANES), f32),
                pltpu.VMEM((8, wide, LANES), f32),
                pltpu.VMEM((2, wide, LANES), f32),
                pltpu.VMEM((2, wide, LANES), f32),
                pltpu.VMEM((PARTS, wide, LANES), f32),
                pltpu.VMEM((PARTS, wide, LANES), f32),
                pltpu.VMEM((8, 2 * wide, 2 * LANES), jnp.bfloat16),
                pltpu.VMEM((8, 2 * wide, LANES), f32),
                pltpu.VMEM((PARTS, PACKED, LANES), f32),
                pltpu.VMEM((PARTS, PACKED, LANES), f32),
                pltpu.SemaphoreType.REGULAR((1,)),
                dma((7,)),
                dma((2,)),
                dma((2,)),
                dma((PARTS,)),
                dma((PARTS,)),
                dma((PARTS,)),
                dma((PARTS,)),
            ],
            compiler_params=pltpu.CompilerParams(collective_id=0, has_side_effects=True, vmem_limit_bytes=32 << 20),
        )(*(pltpu.with_memory_space_constraint(value, pltpu.HBM) for value in operands))
        return jnp.transpose(result, (1, 0, 2))

    return jax.shard_map(
        body,
        mesh=mesh,
        in_specs=(P("lat", "lon", None), P("lat"), P("lat")),
        out_specs=P("lat", "lon", None),
        check_vma=False,
    )
```

```python
import functools
import math

import jax
import jax.numpy as jnp
import numpy as np
from jax import lax
from jax.experimental import pallas as pl
from jax.experimental.pallas import tpu as pltpu
from jax.sharding import PartitionSpec as P

MESH = pl.DeviceIdType.MESH
PARTS = 16
LANES = 128
OPEN_CUT = 4096.0
DEPTH = 8
PACKED = 72


def split_table(table):
    high = np.asarray(table, dtype=jnp.bfloat16)
    low = np.asarray(table - high.astype(np.float64), dtype=jnp.bfloat16)
    return high, low


def dft_tables(nlon, width, wide):
    points = np.full(wide, -10**6)
    points[:width] = np.arange(width)
    points[width] = width
    points[wide - 1] = -1
    used = points > -10**6
    forward = np.zeros((8, 2 * wide, 2 * wide))
    inverse = np.zeros((8, 2 * wide, 2 * wide))
    sines = np.zeros((8, wide))
    for group in range(8):
        for row in range(wide):
            if group:
                if row >= width:
                    continue
                wave = group + PARTS * row
                weight = 2.0 / nlon
            else:
                half = width // 2 + 1
                if row < half:
                    wave = PARTS * row
                elif row < width + 1:
                    wave = 8 + PARTS * (row - half)
                else:
                    continue
                weight = (1.0 if wave in (0, nlon // 2) else 2.0) / nlon
            phase = np.where(used, (points * wave) % nlon, 0) * (2.0 * math.pi / nlon)
            cos_vals = np.where(used, np.cos(phase), 0.0)
            sin_vals = np.where(used, np.sin(phase), 0.0)
            inner = np.arange(wide) < width
            if group:
                forward[group, row, :wide] = cos_vals
                forward[group, row, wide:] = -sin_vals
                forward[group, wide + row, :wide] = -sin_vals
                forward[group, wide + row, wide:] = -cos_vals
                inverse[group, :wide, row] = weight * cos_vals * inner
                inverse[group, :wide, wide + row] = -weight * sin_vals * inner
                inverse[group, wide:, row] = weight * sin_vals * inner
                inverse[group, wide:, wide + row] = weight * cos_vals * inner
            else:
                base = 0 if row < half else wide
                part = slice(base, base + wide)
                forward[0, row, part] = cos_vals
                forward[0, wide + row, part] = -sin_vals
                inverse[0, part, row] = weight * cos_vals * inner
                inverse[0, part, wide + row] = -weight * sin_vals * inner
            sines[group, row] = math.sin(2.0 * math.pi * wave / nlon)
    waves = np.zeros((wide, LANES), np.float32)
    waves[:, :8] = sines.T
    return np.concatenate(split_table(np.concatenate([forward, inverse])), axis=1), waves


def coef_table(nlat, bands):
    rows = nlat // bands
    index = np.arange(-1, nlat + 1).astype(np.float32)
    angle = np.float32(-0.5 * math.pi) + (index + np.float32(0.5)) * np.float32(math.pi) / np.float32(nlat)
    cosine = np.cos(angle.astype(np.float64)).astype(np.float32).astype(np.float64)
    flux = cosine.copy()
    flux[0] = 0.0
    flux[-1] = 0.0
    table = np.zeros((bands, 16, LANES))
    for band in range(bands):
        at = band * rows + 1
        for row in range(rows):
            table[band, row] = 0.015 / cosine[at + row]
        for pair in range(rows // 2):
            even = at + 2 * pair
            odd = even + 1
            lane = np.zeros(8)
            lane[0] = 0.03 / cosine[even]
            lane[1] = 0.03 / cosine[odd]
            lane[4] = -0.015 * flux[odd] / cosine[even]
            lane[5] = 0.015 * flux[even] / cosine[odd]
            lane[6] = 0.015 * flux[even - 1] / cosine[even]
            lane[7] = -0.015 * flux[odd + 1] / cosine[odd]
            table[band, 8 + pair] = np.repeat(lane, 16)
    return table.astype(np.float32)


def wave_sum(terms):
    total = None
    for factor, value in terms:
        if abs(factor) < 1e-9:
            continue
        if abs(abs(factor) - 1.0) < 1e-9:
            if total is None:
                total = value if factor > 0 else -value
            else:
                total = total + value if factor > 0 else total - value
        else:
            part = value * np.float32(factor)
            total = part if total is None else total + part
    return total


def half_dft(even_in, odd_in):
    unit = 2.0 * math.pi / PARTS
    sums = [even_in[0] + even_in[8]] + [even_in[a] + even_in[8 - a] for a in (1, 2, 3)] + [even_in[4]]
    diffs = [even_in[0] - even_in[8]] + [even_in[a] - even_in[8 - a] for a in (1, 2, 3)]
    odd_sums = [None] + [odd_in[a] + odd_in[8 - a] for a in (1, 2, 3)] + [odd_in[4]]
    odd_diffs = [None] + [odd_in[a] - odd_in[8 - a] for a in (1, 2, 3)]
    cos_out = []
    sin_out = []
    for k in range(9):
        parts = diffs if k % 2 else sums
        cos_out.append(wave_sum([(math.cos(unit * a * k), parts[a]) for a in range(len(parts))]))
        parts = odd_sums if k % 2 else odd_diffs
        sin_out.append(wave_sum([(math.sin(unit * a * k), parts[a]) for a in range(1, len(parts))]))
    return cos_out, sin_out


def split_value(value):
    high = value.astype(jnp.bfloat16)
    low = (value - high.astype(jnp.float32)).astype(jnp.bfloat16)
    return jnp.concatenate([high, low], axis=1)


def table_dot(table, pair):
    both = jnp.dot(table, pair, preferred_element_type=jnp.float32)
    half = table.shape[0] // 2
    return both[:half, :LANES] + both[:half, LANES:] + both[half:, :LANES]


def kernel(
    bands,
    state_hbm, flag_hbm, cut_hbm, coef_hbm, table_hbm, wave_hbm,
    result,
    state, flag_ref, cut_ref, winds, press, slopes, cuts, coef, table, waves, damps, turns,
    halo_out, halo_in, send, recv, spectra, fields, bsend, brecv,
    hello, load_sem, halo_send, halo_recv, send_sem, recv_sem, bsend_sem, brecv_sem,
):
    lat = lax.axis_index("lat")
    lon = lax.axis_index("lon")
    width, rows = state_hbm.shape[0], state_hbm.shape[1]
    wide = recv.shape[1]
    spare = jnp.zeros((wide - width, LANES), jnp.float32)

    def field(row, part):
        return jnp.concatenate([state[:, row, pl.ds(part * LANES, LANES)], spare], axis=0)

    above = jnp.maximum(lat - 1, 0)
    below = jnp.minimum(lat + 1, bands - 1)
    sides = (lat > 0, lat < bands - 1)
    place = lax.rem(lat, DEPTH)
    paired = (place != 0, place != DEPTH - 1)
    opening = (place == 0) & sides[0]
    closing = (place == DEPTH - 1) & sides[1]
    known = jnp.where(paired[0], 1, 0) + jnp.where(sides[1], 1, 0)
    chip = lon // 2
    core = lon % 2

    def state_copy(part):
        spans = pl.ds(part * LANES, LANES)
        return pltpu.make_async_copy(state_hbm.at[:, :, spans], state.at[:, :, spans], load_sem.at[part])

    loads = [state_copy(1), state_copy(0)]
    loads.append(pltpu.make_async_copy(coef_hbm.at[lat], coef, load_sem.at[2]))
    loads.append(pltpu.make_async_copy(flag_hbm, flag_ref, load_sem.at[3]))
    loads.append(pltpu.make_async_copy(cut_hbm, cut_ref, load_sem.at[4]))
    tables = ((wave_hbm, waves), (table_hbm, table))
    for at, (source, target) in enumerate(tables):
        loads.append(pltpu.make_async_copy(source, target, load_sem.at[5 + at]))
    for load in loads[:5]:
        load.start()

    barrier = pltpu.get_barrier_semaphore()
    for offset in range(1, PARTS):
        pl.semaphore_signal(barrier, inc=1, device_id=(lat, lax.rem(lon + offset, PARTS)), device_id_type=MESH)

    for side, device in ((0, above), (1, below)):
        @pl.when(paired[side])
        def _():
            pl.semaphore_signal(barrier, inc=1, device_id=(device, lon), device_id_type=MESH)

    lane = lax.broadcasted_iota(jnp.int32, (wide, LANES), 1)
    line = lax.broadcasted_iota(jnp.int32, (wide, LANES), 0)
    first = lane < 64
    block = (lane // 16) % 4
    loads[0].wait()
    for row in range(rows):
        right = field(row, 1)
        turned = pltpu.roll(right, 64, 1)
        step = jnp.where(lane < 63, pltpu.roll(turned, LANES - 1, 1), 0.0) - jnp.where(lane > 0, pltpu.roll(turned, 1, 1), 0.0)
        vert = right - 0.1 * step
        step = jnp.where(lane < 63, pltpu.roll(vert, LANES - 1, 1), 0.0) - jnp.where(lane > 0, pltpu.roll(vert, 1, 1), 0.0)
        press[row] = turned - 0.015 * step
        result[:, row, pl.ds(LANES, LANES)] = vert[:width]
        slopes[row] = pltpu.roll(turned, wide - 1, 0) - pltpu.roll(turned, 1, 0)
    for load in loads[1:3]:
        load.wait()

    def prepare(row):
        left = field(row, 0)
        zonal = left - coef[pl.ds(row, 1), :] * slopes[row]
        merid = left
        if row < rows - 1:
            merid = merid - 0.015 * field(row + 1, 1)
        if row > 0:
            merid = merid + 0.015 * field(row - 1, 1)
        winds[row + 1] = jnp.where(first, zonal, merid)

    def pack(pair, slot):
        even = 2 * pair + 1
        sources = (
            jnp.where(first, winds[even], winds[even + 1]),
            jnp.where(first, winds[even + 1], winds[even]),
            jnp.where(first, press[even - 1], winds[even - 1]),
            jnp.where(first, press[even], winds[even + 2]),
        )
        for quarter in range(4):
            chunk = sources[quarter]
            for at in range(4):
                if at != quarter:
                    chunk = jnp.where(block == at, pltpu.roll(sources[at], (16 * (at - quarter)) % LANES, 1), chunk)
            send[slot + 4 * quarter] = chunk

    def halo_copy(side, slot, device):
        return pltpu.make_async_remote_copy(
            src_ref=halo_out.at[side],
            dst_ref=halo_in.at[slot],
            send_sem=halo_send.at[side],
            recv_sem=halo_recv.at[slot],
            device_id=(device, lon),
            device_id_type=MESH,
        )

    halos = [halo_copy(0, 1, above), halo_copy(1, 0, below)]

    def forward_copy(source, slot, device):
        return pltpu.make_async_remote_copy(
            src_ref=send.at[source],
            dst_ref=recv.at[slot],
            send_sem=send_sem.at[source],
            recv_sem=recv_sem.at[slot],
            device_id=(lat, device),
            device_id_type=MESH,
        )

    def backward_copy(source, slot, device):
        return pltpu.make_async_remote_copy(
            src_ref=bsend.at[source],
            dst_ref=brecv.at[slot],
            send_sem=bsend_sem.at[source],
            recv_sem=brecv_sem.at[slot],
            device_id=(lat, device),
            device_id_type=MESH,
        )

    order = (4, 3, 5, 2, 6, 1, 7, 0)

    def send_to(copy, kind):
        for offset in order:
            target = 2 * lax.rem(chip + offset, 8) + kind
            if offset:
                copy(target, lon, target).start()
            else:
                @pl.when(core != kind)
                def _():
                    copy(target, lon, target).start()

    def pack_and_send(pair, at, kind):
        pack(pair, 2 * at + kind)
        for offset in (2, 1, 3, 0):
            target = 2 * at + 4 * lax.rem(chip // 2 + offset, 4) + kind

            @pl.when(target != lon)
            def _():
                forward_copy(target, lon, target).start()

    prepare(0)
    prepare(rows - 1)
    for load in loads[3:5]:
        load.wait()
    for row in range(rows):
        kept = jnp.full((1, LANES), cut_ref[row], jnp.int32).astype(jnp.float32)
        flag = jnp.full((1, LANES), flag_ref[row], jnp.int32)
        cuts[pl.ds(row + 1, 1), :] = jnp.where(flag == 1, kept, OPEN_CUT)
    for side, row in ((0, 0), (1, rows - 1)):
        turned = pltpu.roll(field(row, 1), 64, 1)
        message = jnp.where(first, turned, winds[row + 1])
        halo_out[side] = jnp.where(line == width, cuts[pl.ds(row + 1, 1), :], message)
    for row in range(1, 5):
        prepare(row)

    pl.semaphore_wait(barrier, PARTS - 1 + known)
    pl.when(paired[0])(halos[0].start)
    pl.when(sides[1])(halos[1].start)

    @pl.when(opening)
    def _():
        pl.semaphore_signal(barrier, inc=1, device_id=(above, lon), device_id_type=MESH)

    @pl.when(closing)
    def _():
        pl.semaphore_signal(hello.at[0], inc=1, device_id=(below, lon), device_id_type=MESH)

    pack_and_send(1, 0, 0)
    for load in loads[5:]:
        load.start()
    for row in range(5, 7):
        prepare(row)
    pack_and_send(2, 1, 0)

    flip = jnp.where((place == 0) | (place == DEPTH - 1), 1, 0)
    for step in range(2):
        side = flip if step == 0 else 1 - flip
        present = jnp.where(side == 0, lat, bands - 1 - lat) > 0

        @pl.when(present)
        def _():
            halo_copy(1 - side, side, above).wait_recv()

        @pl.when(jnp.logical_not(present))
        def _():
            halo_in[side] = jnp.zeros((wide, LANES), jnp.float32)

        outer = jnp.where(side == 0, 0, rows + 1)
        inner = jnp.where(side == 0, 1, rows)
        slope = jnp.where(side == 0, 0.015, -0.015)
        inside = jnp.where(present, slope, 0.0)
        arrived = halo_in[side]
        cuts[pl.ds(outer, 1), :] = arrived[width : width + 1]
        winds[outer] = jnp.where(line < width, arrived - slope * pltpu.roll(halo_out[side], 64, 1), 0.0)
        winds[inner] = winds[inner] + jnp.where(first | (line >= width), 0.0, inside * pltpu.roll(arrived, 64, 1))
        pack_and_send(3 * side, side, 1)
        if step == 0:
            @pl.when(opening)
            def _():
                pl.semaphore_wait(hello.at[0], 1)
                halos[0].start()

    recv[lon] = send[lon]

    half = chip % 2
    mine = (1 - core) * (1 + half) + core * 3 * half
    lanes = lax.broadcasted_iota(jnp.int32, (1, LANES), 1) // 16
    cut_even = cuts[pl.ds(2 * mine + 1, 1), :]
    cut_odd = cuts[pl.ds(2 * mine + 2, 1), :]
    limit = jnp.where((lanes == 0) | (lanes == 2) | (lanes == 5), cut_even, cut_odd)
    limit = jnp.where(lanes == 6, cuts[pl.ds(2 * mine, 1), :], limit)
    limit = jnp.where(lanes == 7, cuts[pl.ds(2 * mine + 3, 1), :], limit)
    factor = coef[pl.ds(8 + mine, 1), :]
    loads[5].wait()

    for group in range(8):
        wave = PARTS * line + group
        if group:
            wave = jnp.minimum(wave, PARTS * width - wave)
        else:
            wave = jnp.where(line <= width // 2, wave, PARTS * (line - width // 2 - 1) + 8)
        ratio = limit / jnp.maximum(wave, 1).astype(jnp.float32)
        damps[group] = jnp.minimum(1.0, ratio * ratio)
        turns[group] = factor * waves[:, group : group + 1]
    for load in loads[6:]:
        load.wait()

    def receive(offset, carry):
        source = lax.rem(lon + offset, PARTS)
        forward_copy(source, source, source).wait_recv()
        return carry

    lax.fori_loop(1, PARTS, receive, 0)

    def gather_waves(at, carry):
        where = pl.multiple_of(16 * at, 16)
        spans = pl.ds(where, 16)
        images = pl.ds(pl.multiple_of(wide + where, 16), 16)
        values = [recv[a, spans, :] for a in range(PARTS)]
        evens = [values[0]] + [values[a] + values[PARTS - a] for a in range(1, 8)] + [values[8]]
        odds = [None] + [values[a] - values[PARTS - a] for a in range(1, 8)]
        cos_out, sin_out = half_dft(evens, odds)
        spectra[0, spans, :] = split_value(cos_out[0])
        spectra[0, images, :] = split_value(cos_out[8])
        for k in range(1, 8):
            spectra[k, spans, :] = split_value(cos_out[k])
            spectra[k, images, :] = split_value(sin_out[k])
        return carry

    lax.fori_loop(0, wide // 16, gather_waves, 0, unroll=6)

    def transform(group, carry):
        values = table_dot(table[group], spectra[group])
        damping = damps[group]
        real = values[:wide] * damping
        imag = values[wide:] * damping
        turn = turns[group]
        zonal = lane < 32
        lift_real = jnp.where(zonal, turn * imag, factor * real)
        lift_imag = jnp.where(zonal, -turn * real, factor * imag)
        inner = (lane >= 32) & first
        outs = []
        for value, lift in ((real, lift_real), (imag, lift_imag)):
            total = pltpu.roll(lift, 32, 1) + pltpu.roll(lift, 96, 1) + pltpu.roll(lift, 64, 1)
            outs.append(jnp.where(inner, value + damping * total, value))
        both = split_value(jnp.concatenate(outs, axis=0))
        fields[group] = table_dot(table[8 + group], both)
        return carry

    lax.fori_loop(0, 8, transform, 0, unroll=8)

    def scatter_waves(at, carry):
        where = pl.multiple_of(16 * at, 16)
        spans = pl.ds(where, 16)
        images = pl.ds(pl.multiple_of(wide + where, 16), 16)
        evens = [fields[0, spans, :]] + [fields[k, spans, :] for k in range(1, 8)] + [fields[0, images, :]]
        odds = [None] + [fields[k, images, :] for k in range(1, 8)]
        cos_out, sin_out = half_dft(evens, odds)
        circles[0, spans, :] = cos_out[0]
        circles[8, spans, :] = cos_out[8]
        for a in range(1, 8):
            circles[a, spans, :] = cos_out[a] - sin_out[a]
            circles[PARTS - a, spans, :] = cos_out[a] + sin_out[a]
        return carry

    circles = recv
    lax.fori_loop(0, wide // 16, scatter_waves, 0, unroll=6)
    narrow = lax.broadcasted_iota(jnp.int32, (24, LANES), 1)

    def pack_back(a, carry):
        rest = circles[a, pl.ds(72, 24), :]
        for at in range(3):
            spans = pl.ds(24 * at, 24)
            bsend[a, spans, :] = jnp.where(narrow < 96, circles[a, spans, :], pltpu.roll(rest, 96 - 32 * at, 1))
        return carry

    lax.fori_loop(0, PARTS, pack_back, 0, unroll=PARTS)
    for turn, kind in ((0, 1), (1, 1), (1, 0), (0, 0)):
        for offset in (2, 1, 3, 0):
            target = 4 * lax.rem(chip // 2 + offset, 4) + 2 * turn + kind

            @pl.when(target != lon)
            def _():
                backward_copy(target, lon, target).start()

    brecv[lon] = bsend[lon]

    def unpack(pair, slot):
        chunks = []
        for quarter in range(4):
            source = slot + 4 * quarter

            @pl.when(source != lon)
            def _():
                backward_copy(source, source, source).wait_recv()

            pieces = [brecv[source, pl.ds(24 * at, 24), :] for at in range(3)]
            rest = jnp.where(narrow < 32, pltpu.roll(pieces[0], 32, 1), pltpu.roll(pieces[1], 64, 1))
            rest = jnp.where(narrow < 64, rest, pltpu.roll(pieces[2], 96, 1))
            chunks.append(jnp.concatenate(pieces + [rest], axis=0))
        parts = []
        for at in range(4):
            shift = 64 if at >= 2 else 0
            part = None
            for quarter in range(4):
                amount = (16 * (quarter - at) + shift) % LANES
                moved = pltpu.roll(chunks[quarter], amount, 1) if amount else chunks[quarter]
                part = moved if part is None else jnp.where(block == quarter, moved, part)
            parts.append(part)
        even = 2 * pair
        spans = pl.ds(0, LANES)
        result[:, even, spans] = jnp.where(first, parts[0], parts[1])[:width]
        result[:, even + 1, spans] = jnp.where(first, parts[1], parts[0])[:width]
        spans = pl.ds(LANES, LANES)
        result[:, even, spans] = jnp.where(first[:width], result[:, even, spans], parts[2][:width])
        result[:, even + 1, spans] = jnp.where(first[:width], result[:, even + 1, spans], parts[3][:width])

    for at in range(2):
        unpack(1 + at, 2 * at)
    for at in range(2):
        unpack(3 * at, 2 * at + 1)

    def finish(offset, carry):
        target = lax.rem(lon + offset, PARTS)
        forward_copy(target, lon, target).wait_send()
        backward_copy(target, lon, target).wait_send()
        return carry

    lax.fori_loop(1, PARTS, finish, 0)
    for side in range(2):
        pl.when(sides[side])(halos[side].wait_send)


def solution(mesh):
    bands = mesh.shape["lat"]

    def body(state, filter_flag, cutoff):
        rows, width, depth = state.shape
        wide = (width + 2 + 15) // 16 * 16
        tables = dft_tables(width * PARTS, width, wide)
        coefs = coef_table(rows * bands, bands)
        f32 = jnp.float32
        table = pltpu.VMEM((16, 4 * wide, 2 * wide), jnp.bfloat16)
        hbm_spec = pl.BlockSpec(memory_space=pltpu.HBM)
        dma = pltpu.SemaphoreType.DMA
        operands = (jnp.transpose(state, (1, 0, 2)), filter_flag, cutoff) + tuple(map(jnp.asarray, (coefs,) + tables))
        result = pl.pallas_call(
            functools.partial(kernel, bands),
            out_shape=jax.ShapeDtypeStruct((width, rows, depth), f32),
            in_specs=[hbm_spec] * 6,
            out_specs=pl.BlockSpec(memory_space=pltpu.VMEM),
            scratch_shapes=[
                pltpu.VMEM((width, rows, depth), f32),
                pltpu.SMEM((rows,), jnp.int32),
                pltpu.SMEM((rows,), jnp.int32),
                pltpu.VMEM((rows + 2, wide, LANES), f32),
                pltpu.VMEM((rows, wide, LANES), f32),
                pltpu.VMEM((rows, wide, LANES), f32),
                pltpu.VMEM((16, LANES), f32),
                pltpu.VMEM((16, LANES), f32),
                table,
                pltpu.VMEM((wide, LANES), f32),
                pltpu.VMEM((8, wide, LANES), f32),
                pltpu.VMEM((8, wide, LANES), f32),
                pltpu.VMEM((2, wide, LANES), f32),
                pltpu.VMEM((2, wide, LANES), f32),
                pltpu.VMEM((PARTS, wide, LANES), f32),
                pltpu.VMEM((PARTS, wide, LANES), f32),
                pltpu.VMEM((8, 2 * wide, 2 * LANES), jnp.bfloat16),
                pltpu.VMEM((8, 2 * wide, LANES), f32),
                pltpu.VMEM((PARTS, PACKED, LANES), f32),
                pltpu.VMEM((PARTS, PACKED, LANES), f32),
                pltpu.SemaphoreType.REGULAR((1,)),
                dma((7,)),
                dma((2,)),
                dma((2,)),
                dma((PARTS,)),
                dma((PARTS,)),
                dma((PARTS,)),
                dma((PARTS,)),
            ],
            compiler_params=pltpu.CompilerParams(collective_id=0, has_side_effects=True, vmem_limit_bytes=32 << 20),
        )(*(pltpu.with_memory_space_constraint(value, pltpu.HBM) for value in operands))
        return jnp.transpose(result, (1, 0, 2))

    return jax.shard_map(
        body,
        mesh=mesh,
        in_specs=(P("lat", "lon", None), P("lat"), P("lat")),
        out_specs=P("lat", "lon", None),
        check_vma=False,
    )
```
